32 devices in a mesh: shard: 4 (over y, x), rep: 8 (over z, core).
Axes of the slice: x: 2, y: 2, z: 4, core: 2. Of those that a mesh axis runs over, the one named last changes fastest.
Arguments:
- latents: bfloat16 [32, 256, 384], P(('shard', 'rep')), may hold values from -6 to 6
- condition: bfloat16 [32, 384], P(('shard', 'rep')), may hold values from -4 to 4
- cotangent: bfloat16 [32, 256, 384], P(('shard', 'rep')), may hold values from -6 to 6
- w_qkv: bfloat16 [2, 384, 1152], P(None, 'shard'), may hold values from -0.15625 to 0.15625
- b_qv: bfloat16 [2, 768], P(None, 'shard'), may hold values from -3 to 3
- w_proj: bfloat16 [2, 384, 384], P(None, 'shard'), may hold values from -1.75 to 1.75
- b_proj: bfloat16 [2, 384], P(None, 'shard'), may hold values from -3 to 3
- w_fc1: bfloat16 [2, 384, 1536], P(None, 'shard'), may hold values from -0.3125 to 0.3125
- b_fc1: bfloat16 [2, 1536], P(None, 'shard'), may hold values from -3 to 3
- w_fc2: bfloat16 [2, 1536, 384], P(None, 'shard'), may hold values from -0.15625 to 0.15625
- b_fc2: bfloat16 [2, 384], P(None, 'shard'), may hold values from -3 to 3
- w_ada: bfloat16 [2, 384, 2304], P(None, 'shard'), may hold values from -4 to 4
- b_ada: bfloat16 [2, 2304], P(None, 'shard'), may hold values from -3 to 3
Outputs:
- x_out: bfloat16 [32, 256, 384], P(('shard', 'rep'))
- x_grad: float32 [32, 256, 384], P(('shard', 'rep'))
- cond_grad: float32 [32, 384], P(('shard', 'rep'))
- grad_qkv: float32 [2, 384, 1152], P(None, 'shard')
- grad_qv_bias: float32 [2, 768], P(None, 'shard')
- grad_proj: float32 [2, 384, 384], P(None, 'shard')
- grad_proj_bias: float32 [2, 384], P(None, 'shard')
- grad_fc1: float32 [2, 384, 1536], P(None, 'shard')
- grad_fc1_bias: float32 [2, 1536], P(None, 'shard')
- grad_fc2: float32 [2, 1536, 384], P(None, 'shard')
- grad_fc2_bias: float32 [2, 384], P(None, 'shard')
- grad_ada: float32 [2, 384, 2304], P(None, 'shard')
- grad_ada_bias: float32 [2, 2304], P(None, 'shard')
The draws below stay inside these ranges and needn't reach their ends.
All inputs are finite; a program needn't handle non-finite values.
Results may differ from the reference program's by a relative error of at most 0.017.
Values may be sent and summed in bfloat16 or wider, within the bound.
No kernel may reach another device: no remote copies, remote signals or barrier semaphores. Data moves between devices by JAX's collectives and lax.ppermute only.
A program may use at most 128 MiB of HBM per device.

```python
import jax
import jax.numpy as jnp
from jax import lax

D = 384
HEADS = 6
FF = 1536
SEQ = 256
LAYERS = 2
LAT_DEV = 1
LATENTS = 32
N_SHARD = 4


def draw_condition(key, part):
    return jnp.clip(jax.random.normal(key, (LATENTS, D), jnp.float32), -4.0, 4.0).astype(jnp.bfloat16)


def draw_w_ada(key, part):
    factor = 1.0 / D ** 0.5
    values = jnp.clip(jax.random.normal(key, (LAYERS, D, 6 * D), jnp.float32), -4.0, 4.0)
    return (values * factor).astype(jnp.bfloat16)


def block_levels(key, dims, shards, smallest, top_value):
    factor_of, own = 1.0, jax.random.fold_in(key, 6)
    for axis_at, shards_of in shards:
        steps = jnp.exp(jax.random.uniform(jax.random.fold_in(own, axis_at), (shards_of,), jnp.float32, smallest / len(shards), top_value / len(shards)))
        factor_of = factor_of * jnp.repeat(steps, dims[axis_at] // shards_of).reshape([-1 if axis == axis_at else 1 for axis in range(len(dims))])
    return factor_of


def noise(own_key, dims, scale, bound, cuts=(), kind=jnp.bfloat16):
    gain = block_levels(own_key, dims, cuts, -0.22, 0.18) if cuts else 1.0
    array = jax.random.normal(own_key, dims, jnp.float32) * scale * gain
    return jnp.minimum(jnp.maximum(array, -bound), bound).astype(kind)


def setup_inputs(seed: int = 0) -> dict:
    splits = jax.random.split(jax.random.key(seed), 14)
    return {
        "latents": noise(splits[0], (LATENTS, SEQ, D), 1.0, 6.0, ((0, 32),)),
        "condition": draw_condition(jax.random.fold_in(splits[13], 71), 0),
        "cotangent": noise(splits[2], (LATENTS, SEQ, D), 1.0, 6.0, ((0, 32),)),
        "w_qkv": noise(splits[3], (LAYERS, D, 3 * D), (4 * D) ** -0.5, 0.15625, ((1, 4),)),
        "b_qv": noise(splits[4], (LAYERS, 2 * D), 0.5, 3.0, ((1, 4),)),
        "w_proj": noise(splits[5], (LAYERS, D, D), (D // 32) ** -0.5, 1.75, ((1, 4),)),
        "b_proj": noise(splits[6], (LAYERS, D), 0.5, 3.0, ((1, 4),)),
        "w_fc1": noise(splits[7], (LAYERS, D, FF), D ** -0.5, 0.3125, ((1, 4),)),
        "b_fc1": noise(splits[8], (LAYERS, FF), 0.5, 3.0, ((1, 4),)),
        "w_fc2": noise(splits[9], (LAYERS, FF, D), FF ** -0.5, 0.15625, ((1, 4),)),
        "b_fc2": noise(splits[10], (LAYERS, D), 0.5, 3.0, ((1, 4),)),
        "w_ada": draw_w_ada(jax.random.fold_in(splits[13], 71), 0),
        "b_ada": noise(splits[12], (LAYERS, 6 * D), 0.5, 3.0, ((1, 4),)),
    }


@jax.custom_vjp
def low(v):
    return lax.optimization_barrier(v.astype(jnp.bfloat16)).astype(jnp.float32)

@jax.custom_vjp
def low_back(v):
    return v

def low_keep(v):
    return (low(v), None)

def low_pass(kept, grad):
    return (grad,)

def back_keep(v):
    return (v, None)

def back_low(kept, grad):
    return (low(grad),)
low.defvjp(low_keep, low_pass)
low_back.defvjp(back_keep, back_low)
highest = lax.Precision.HIGHEST

def layer_norm(residual_state):
    center = residual_state - lax.optimization_barrier(jnp.mean(residual_state, axis=-1, keepdims=True))
    spread = lax.optimization_barrier(jnp.mean(center * center, axis=-1, keepdims=True))
    return center * lax.rsqrt(spread + 1e-06)

def project(left, right):
    return jnp.einsum('gsd,de->gse', left, right, precision=highest)

def diffusion_block(weight_set, residual_state, condition_activation):
    w_qkv, b_qv, w_proj, b_proj, w_fc1, b_fc1, w_fc2, b_fc2, w_ada, b_ada = weight_set
    groups = residual_state.shape[0]
    length = residual_state.shape[1]
    width = residual_state.shape[2]
    head_dim = width // HEADS
    modulate = low_back(jnp.dot(condition_activation, w_ada, precision=highest) + b_ada)
    pieces = [part_mod[:, None, :] for part_mod in jnp.split(modulate, 6, axis=-1)]
    shift_one, scale_one, gate_one, shift_two, scale_two, gate_two = pieces
    h_one = low(layer_norm(residual_state) * (1.0 + scale_one) + shift_one)
    mixed = project(h_one, w_qkv)
    queries = low_back(low(mixed[..., :width] + b_qv[:width])).reshape(groups, length, HEADS, head_dim)
    key_rows = low_back(low(mixed[..., width:2 * width])).reshape(groups, length, HEADS, head_dim)
    value_rows = low_back(low(mixed[..., 2 * width:] + b_qv[width:])).reshape(groups, length, HEADS, head_dim)
    scores = low_back(jnp.einsum('gqhd,gkhd->ghqk', queries, key_rows, precision=highest) * head_dim ** (-0.5))
    probs = low(jax.nn.softmax(scores, axis=-1))
    attended = jnp.einsum('ghqk,gkhd->gqhd', probs, value_rows, precision=highest).reshape(groups, length, width)
    attended = low_back(low(attended))
    branch = low_back(project(attended, w_proj) + b_proj)
    middle = residual_state + gate_one * branch
    h_two = low(layer_norm(middle) * (1.0 + scale_two) + shift_two)
    pre_act = low_back(project(h_two, w_fc1) + b_fc1)
    act_low = low(jax.nn.gelu(pre_act, approximate=True))
    mlp_out = low_back(project(act_low, w_fc2) + b_fc2)
    return middle + gate_two * mlp_out

def reference(latents, condition, cotangent, w_qkv, b_qv, w_proj, b_proj, w_fc1, b_fc1, w_fc2, b_fc2, w_ada, b_ada):
    weight_set = tuple((input_array.astype(jnp.float32) for input_array in (w_qkv, b_qv, w_proj, b_proj, w_fc1, b_fc1, w_fc2, b_fc2, w_ada, b_ada)))
    group_size = LAT_DEV * N_SHARD
    group_count = LATENTS // group_size

    def forward(residual_state, cond_in, parameter_tree):
        condition_activation = low(jax.nn.silu(cond_in))

        def run_group(pair):
            block_input, conditioned_block = pair
            for layer_number in range(LAYERS):
                block_input = diffusion_block(tuple((input_array[layer_number] for input_array in parameter_tree)), block_input, conditioned_block)
            return block_input
        grouped = (residual_state.reshape(group_count, group_size, SEQ, D), condition_activation.reshape(group_count, group_size, D))
        return lax.map(jax.checkpoint(run_group), grouped).reshape(LATENTS, SEQ, D)
    result, pullback = jax.vjp(forward, latents.astype(jnp.float32), condition.astype(jnp.float32), weight_set)
    grad_in, grad_cond, grad_params = pullback(cotangent.astype(jnp.float32))
    scaled = [grad_one / LATENTS for grad_one in grad_params]
    return (result.astype(jnp.bfloat16), grad_in, grad_cond, scaled[0], scaled[1], scaled[2], scaled[3], scaled[4], scaled[5], scaled[6], scaled[7], scaled[8], scaled[9])
```

```python
import functools

import jax
import jax.numpy as jnp
from jax import lax
from jax.experimental import pallas as pl
from jax.experimental.pallas import tpu as pltpu
from jax.sharding import PartitionSpec as P

HEADS = 6
BF = jnp.bfloat16
F32 = jnp.float32
CORES = 2
VMEM_LIMIT = 40 * 1024 * 1024


def dot(left, right):
    return jnp.dot(left, right, preferred_element_type=F32)


def dot_nt(left, right):
    return lax.dot_general(left, right, (((1,), (1,)), ((), ())), preferred_element_type=F32)


def dot_tn(left, right):
    return lax.dot_general(left, right, (((0,), (0,)), ((), ())), preferred_element_type=F32)


def layer_norm(rows):
    center = rows - jnp.mean(rows, axis=-1, keepdims=True)
    inverse = lax.rsqrt(jnp.mean(center * center, axis=-1, keepdims=True) + 1e-06)
    return center * inverse, inverse


def norm_back(grad_norm, normed, inverse):
    centered = grad_norm - jnp.mean(grad_norm, axis=-1, keepdims=True)
    return inverse * (centered - normed * jnp.mean(grad_norm * normed, axis=-1, keepdims=True))


def col_sum(rows):
    return jnp.sum(rows, axis=0, keepdims=True)


def block_at(start, size):
    return pl.ds(pl.multiple_of(start, size), size)


def start_all(copies):
    for copy in copies:
        copy.start()


def wait_all(copies):
    for copy in copies:
        copy.wait()


def make_copies(pairs, sems):
    return [
        pltpu.make_async_copy(source, target, sems.at[slot])
        for slot, (source, target) in enumerate(pairs)
    ]


def run(body, name, inputs, outputs, scratch=(), flops=0):
    places = {"v": pltpu.VMEM, "a": pl.ANY, "s": pltpu.SMEM}
    moved = sum(arr.size * arr.dtype.itemsize for arr, _ in inputs)
    return pl.pallas_call(
        body,
        out_shape=[jax.ShapeDtypeStruct(shape, dtype) for shape, dtype, _ in outputs],
        in_specs=[pl.BlockSpec(memory_space=places[kind]) for _, kind in inputs],
        out_specs=[pl.BlockSpec(memory_space=places[kind]) for _, _, kind in outputs],
        scratch_shapes=list(scratch),
        compiler_params=pltpu.CompilerParams(vmem_limit_bytes=VMEM_LIMIT),
        cost_estimate=pl.CostEstimate(flops=flops, bytes_accessed=moved, transcendentals=0),
        name=name,
    )(*[arr for arr, _ in inputs])


def qkv_pairs(idx, layer, rows, offset, w_qkv, w_proj, near, far, w_all):
    width = w_proj.shape[-1]
    own = block_at(idx[0] * rows, rows)
    pairs = [
        (w_qkv.at[layer, :, : 2 * width], w_all.at[0, own, :]),
        (w_qkv.at[layer, :, 2 * width :], w_all.at[1, own, :width]),
        (w_proj.at[layer], w_all.at[1, own, width:]),
    ]
    return pairs + piece_pairs(idx, rows, offset, 2 * width, near, far, w_all)


def mlp_pairs(idx, layer, rows, offset, w_fc1, w_fc2, near, far, w_all):
    width = w_fc2.shape[-1]
    hidden = w_fc1.shape[-1]
    own = block_at(idx[0] * rows, rows)
    pairs = [(w_fc1.at[layer], w_all.at[0, own, :])]
    for part in range(hidden // width):
        pairs.append(
            (
                w_fc2.at[layer, part * rows : (part + 1) * rows, :],
                w_all.at[1, own, part * width : (part + 1) * width],
            )
        )
    return pairs + piece_pairs(idx, rows, offset, hidden, near, far, w_all)


def piece_pairs(idx, rows, offset, wide, near, far, w_all):
    pairs = []
    for step, (near_piece, far_piece) in enumerate(zip(near, far)):
        place = block_at(jnp.bitwise_xor(idx[0], step + 1) * rows, rows)
        pairs.append((near_piece.at[:, offset : offset + wide], w_all.at[idx[2], place, :]))
        pairs.append((far_piece.at[:, offset : offset + wide], w_all.at[1 - idx[2], place, :]))
    return pairs


def grad_pairs(idx, rows, shards, grad_all, keep, send):
    pairs = []
    for step in range(shards):
        place = block_at(jnp.bitwise_xor(idx[0], step) * rows, rows)
        pairs.append((grad_all.at[idx[2], place, :], keep.at[step]))
        pairs.append((grad_all.at[1 - idx[2], place, :], send.at[step]))
    return pairs


def fc2_chunk(w_all, rows, chunk):
    width = w_all.shape[1]
    parts = w_all.shape[2] // width
    blocks = []
    for number in range(chunk * width // rows, (chunk + 1) * width // rows):
        at, part = number // parts, number % parts
        blocks.append(w_all[1, at * rows : (at + 1) * rows, part * width : (part + 1) * width])
    return jnp.concatenate(blocks, axis=0)


def attention_forward(layer, rows, offset, peers, *refs):
    idx, stream, mod, b_qv, b_proj, w_qkv, w_proj = refs[:7]
    near, far = refs[7 : 7 + peers], refs[7 + peers : 7 + 2 * peers]
    qkv_out, probs_out, attended_out, branch_out, middle_out, w_all, sems = refs[7 + 2 * peers :]
    copies = make_copies(
        qkv_pairs(idx, layer, rows, offset, w_qkv, w_proj, near, far, w_all), sems
    )
    start_all(copies)
    width = stream.shape[-1]
    head = width // HEADS
    values = stream[...].astype(F32)
    shift, scale, gate = (mod[:, part * width : (part + 1) * width] for part in range(3))
    normed, _ = layer_norm(values)
    h_one = (normed * (1.0 + scale) + shift).astype(BF)
    wait_all(copies)
    mixed = dot(h_one, w_all[0])
    qkv_out[:, :width] = (mixed[:, :width] + b_qv[:, :width]).astype(BF)
    qkv_out[:, width : 2 * width] = mixed[:, width:].astype(BF)
    qkv_out[:, 2 * width :] = (dot(h_one, w_all[1, :, :width]) + b_qv[:, width:]).astype(BF)
    lane = lax.broadcasted_iota(jnp.int32, (1, 2 * head), 1)
    masks = [(lane < head).astype(BF), (lane >= head).astype(BF)]
    for pair in range(HEADS // 2):
        at = pair * 2 * head
        queries = qkv_out[:, at : at + 2 * head]
        keys = qkv_out[:, width + at : width + at + 2 * head]
        vals = qkv_out[:, 2 * width + at : 2 * width + at + 2 * head]
        attended = 0.0
        for side in range(2):
            scores = dot_nt(queries, keys * masks[side]) * head ** (-0.5)
            raised = jnp.exp(scores - jnp.max(scores, axis=-1, keepdims=True))
            probs = raised * (1.0 / jnp.sum(raised, axis=-1, keepdims=True))
            probs_out[2 * pair + side] = probs
            attended = attended + dot(probs.astype(BF), vals * masks[side])
        attended_out[:, at : at + 2 * head] = attended.astype(BF)
    branch = dot(attended_out[...], w_all[1, :, width:]) + b_proj[...]
    branch_out[...] = branch
    middle_out[...] = values + gate * branch


def attention_backward(layer, rows, offset, peers, *refs):
    idx, stream, mod, d_middle_in, qkv, probs_in, attended, branch, w_qkv, w_proj = refs[:10]
    near, far = refs[10 : 10 + peers], refs[10 + peers : 10 + 2 * peers]
    d_stream, vec, keep, send, w_all, d_qkv, grad_all, sems, out_sems = refs[10 + 2 * peers :]
    copies = make_copies(
        qkv_pairs(idx, layer, rows, offset, w_qkv, w_proj, near, far, w_all), sems
    )
    start_all(copies)
    width = stream.shape[-1]
    head = width // HEADS
    root = head ** (-0.5)
    shift, scale, gate = (mod[:, part * width : (part + 1) * width] for part in range(3))
    normed, inverse = layer_norm(stream[...].astype(F32))
    h_one = (normed * (1.0 + scale) + shift).astype(BF)
    d_middle = d_middle_in[...]
    vec[:, 2 * width : 3 * width] = col_sum(d_middle * branch[...])
    d_branch = (d_middle * gate).astype(BF)
    grad_all[1, :, width:] = dot_tn(attended[...], d_branch).astype(BF)
    vec[:, 5 * width :] = col_sum(d_branch.astype(F32))
    wait_all(copies)
    d_attended = dot_nt(d_branch, w_all[1, :, width:]).astype(BF)
    lane = lax.broadcasted_iota(jnp.int32, (1, 2 * head), 1)
    masks = [(lane < head).astype(BF), (lane >= head).astype(BF)]
    for pair in range(HEADS // 2):
        at = pair * 2 * head
        queries = qkv[:, at : at + 2 * head]
        keys = qkv[:, width + at : width + at + 2 * head]
        vals = qkv[:, 2 * width + at : 2 * width + at + 2 * head]
        d_att = d_attended[:, at : at + 2 * head]
        d_queries, d_keys, d_values = 0.0, 0.0, 0.0
        for side in range(2):
            probs = probs_in[2 * pair + side]
            d_values = d_values + dot_tn(probs.astype(BF), d_att * masks[side])
            d_probs = dot_nt(d_att, vals * masks[side])
            inner = jnp.sum(probs * d_probs, axis=-1, keepdims=True)
            d_scores = (probs * (d_probs - inner)).astype(BF)
            d_queries = d_queries + dot(d_scores, keys * masks[side])
            d_keys = d_keys + dot_tn(d_scores, queries * masks[side])
        d_qkv[:, at : at + 2 * head] = (d_queries * root).astype(BF)
        d_qkv[:, width + at : width + at + 2 * head] = (d_keys * root).astype(BF)
        d_qkv[:, 2 * width + at : 2 * width + at + 2 * head] = d_values.astype(BF)
    d_qk, d_val = d_qkv[:, : 2 * width], d_qkv[:, 2 * width :]
    grad_all[0] = dot_tn(h_one, d_qk).astype(BF)
    grad_all[1, :, :width] = dot_tn(h_one, d_val).astype(BF)
    out_copies = make_copies(grad_pairs(idx, rows, peers + 1, grad_all, keep, send), out_sems)
    start_all(out_copies)
    vec[:, 3 * width : 4 * width] = col_sum(d_qk[:, :width].astype(F32))
    vec[:, 4 * width : 5 * width] = col_sum(d_val.astype(F32))
    d_h_one = dot_nt(d_qk, w_all[0]) + dot_nt(d_val, w_all[1, :, :width])
    vec[:, :width] = col_sum(d_h_one)
    vec[:, width : 2 * width] = col_sum(d_h_one * normed)
    d_stream[...] = d_middle + norm_back(d_h_one * (1.0 + scale), normed, inverse)
    wait_all(out_copies)


def gelu_parts(pre_act):
    root = 0.7978845608028654
    square = pre_act * pre_act
    bent = jnp.tanh(root * pre_act * (1.0 + 0.044715 * square))
    half = 0.5 * (1.0 + bent)
    slope = half + 0.5 * pre_act * (1.0 - bent * bent) * (root * (1.0 + 3 * 0.044715 * square))
    return pre_act * half, slope


def mlp_forward_part(rows, h_two, b_fc1, b_fc2, w_all, act_low, slopes):
    width = w_all.shape[1]
    mlp_out = b_fc2[...]
    for chunk in range(w_all.shape[2] // width):
        cols = slice(chunk * width, (chunk + 1) * width)
        act, slope = gelu_parts(dot(h_two, w_all[0, :, cols]) + b_fc1[:, cols])
        act_low[:, cols] = act.astype(BF)
        slopes[:, cols] = slope
        mlp_out = mlp_out + dot(act_low[:, cols], fc2_chunk(w_all, rows, chunk))
    return mlp_out


def mlp_backward_part(
    idx, rows, shards, grad_out, mlp_out, middle, normed, inverse, h_two, scale, gate,
    w_all, act_low, slopes, vec, d_middle_out, grad_all, keep, send, out_sems,
):
    width = w_all.shape[1]
    parts = w_all.shape[2] // width
    vec[:, 2 * width : 3 * width] = col_sum(grad_out * mlp_out)
    d_mlp = (grad_out * gate).astype(BF)
    vec[:, (3 + parts) * width :] = col_sum(d_mlp.astype(F32))
    d_h_two = 0.0
    for chunk in range(parts):
        cols = slice(chunk * width, (chunk + 1) * width)
        d_act = dot_nt(d_mlp, fc2_chunk(w_all, rows, chunk))
        d_pre = (d_act * slopes[:, cols]).astype(BF)
        vec[:, (3 + chunk) * width : (4 + chunk) * width] = col_sum(d_pre.astype(F32))
        grad_all[0, :, cols] = dot_tn(h_two, d_pre).astype(BF)
        grad_fc2 = dot_tn(act_low[:, cols], d_mlp).astype(BF)
        first = chunk * width // rows
        for number in range(first, (chunk + 1) * width // rows):
            at, part = number // parts, number % parts
            grad_all[1, at * rows : (at + 1) * rows, part * width : (part + 1) * width] = grad_fc2[
                (number - first) * rows : (number - first + 1) * rows
            ]
        d_h_two = d_h_two + dot_nt(d_pre, w_all[0, :, cols])
    out_copies = make_copies(grad_pairs(idx, rows, shards, grad_all, keep, send), out_sems)
    start_all(out_copies)
    vec[:, :width] = col_sum(d_h_two)
    vec[:, width : 2 * width] = col_sum(d_h_two * normed)
    d_middle_out[...] = grad_out + norm_back(d_h_two * (1.0 + scale), normed, inverse)
    wait_all(out_copies)


def mlp_forward(layer, rows, offset, peers, *refs):
    idx, middle, mod, b_fc1, b_fc2, w_fc1, w_fc2 = refs[:7]
    near, far = refs[7 : 7 + peers], refs[7 + peers : 7 + 2 * peers]
    act_low, slopes, mlp_out, stream_out, w_all, sems = refs[7 + 2 * peers :]
    copies = make_copies(mlp_pairs(idx, layer, rows, offset, w_fc1, w_fc2, near, far, w_all), sems)
    start_all(copies)
    width = middle.shape[-1]
    shift, scale, gate = (mod[:, part * width : (part + 1) * width] for part in range(3, 6))
    normed, _ = layer_norm(middle[...])
    h_two = (normed * (1.0 + scale) + shift).astype(BF)
    wait_all(copies)
    mlp_out[...] = mlp_forward_part(rows, h_two, b_fc1, b_fc2, w_all, act_low, slopes)
    stream_out[...] = middle[...] + gate * mlp_out[...]


def mlp_backward(layer, rows, offset, peers, *refs):
    idx, middle, mod, grad_out, act_low, slopes, mlp_out, w_fc1, w_fc2 = refs[:9]
    near, far = refs[9 : 9 + peers], refs[9 + peers : 9 + 2 * peers]
    d_middle, vec, keep, send, w_all, grad_all, sems, out_sems = refs[9 + 2 * peers :]
    copies = make_copies(mlp_pairs(idx, layer, rows, offset, w_fc1, w_fc2, near, far, w_all), sems)
    start_all(copies)
    width = middle.shape[-1]
    shift, scale, gate = (mod[:, part * width : (part + 1) * width] for part in range(3, 6))
    normed, inverse = layer_norm(middle[...])
    h_two = (normed * (1.0 + scale) + shift).astype(BF)
    wait_all(copies)
    mlp_backward_part(
        idx, rows, peers + 1, grad_out[...], mlp_out[...], middle, normed, inverse, h_two, scale,
        gate, w_all, act_low, slopes, vec, d_middle, grad_all, keep, send, out_sems,
    )


def mlp_both(layer, rows, offset, peers, *refs):
    idx, middle, mod, b_fc1, b_fc2, cotangent, w_fc1, w_fc2 = refs[:8]
    near, far = refs[8 : 8 + peers], refs[8 + peers : 8 + 2 * peers]
    x_out, d_middle, vec, keep, send = refs[8 + 2 * peers : 13 + 2 * peers]
    w_all, grad_all, act_low, slopes, sems, out_sems = refs[13 + 2 * peers :]
    copies = make_copies(mlp_pairs(idx, layer, rows, offset, w_fc1, w_fc2, near, far, w_all), sems)
    start_all(copies)
    width = middle.shape[-1]
    shift, scale, gate = (mod[:, part * width : (part + 1) * width] for part in range(3, 6))
    normed, inverse = layer_norm(middle[...])
    h_two = (normed * (1.0 + scale) + shift).astype(BF)
    wait_all(copies)
    mlp_out = mlp_forward_part(rows, h_two, b_fc1, b_fc2, w_all, act_low, slopes)
    x_out[...] = (middle[...] + gate * mlp_out).astype(BF)
    mlp_backward_part(
        idx, rows, peers + 1, cotangent[...].astype(F32), mlp_out, middle, normed, inverse, h_two,
        scale, gate, w_all, act_low, slopes, vec, d_middle, grad_all, keep, send, out_sems,
    )


def padded_rows(idx, w_ada, w_pad, sems):
    layers, rows, wide = w_ada.shape
    w_pad[...] = jnp.zeros(w_pad.shape, BF)
    own = block_at(idx[0] * rows, rows)
    return make_copies(
        [
            (w_ada.at[layer], w_pad.at[own, layer * wide : (layer + 1) * wide])
            for layer in range(layers)
        ],
        sems,
    )


def modulate_kernel(shards, *refs):
    idx, w_ada = refs[:2]
    conditions, outs = refs[2 : 2 + shards], refs[2 + shards : 2 + 2 * shards]
    w_pad, sems = refs[2 + 2 * shards :]
    copies = padded_rows(idx, w_ada, w_pad, sems)
    start_all(copies)
    width = w_pad.shape[0]
    acts = []
    for ref in conditions:
        cond = ref[:, :width].astype(F32)
        acts.append(cond / (1.0 + jnp.exp(-cond)))
    acts = jnp.concatenate(acts, axis=0).astype(BF)
    wait_all(copies)
    result = dot(acts, w_pad[...])
    for step in range(shards):
        outs[step][...] = result[step : step + 1]


def condition_back_kernel(shards, *refs):
    idx, w_ada = refs[:2]
    vectors, outs = refs[2 : 2 + shards], refs[2 + shards : 2 + 2 * shards]
    w_pad, sems = refs[2 + 2 * shards :]
    copies = padded_rows(idx, w_ada, w_pad, sems)
    start_all(copies)
    width, wide = w_pad.shape
    d_mod = jnp.concatenate([ref[:, width : width + wide] for ref in vectors], axis=0)
    wait_all(copies)
    result = dot_nt(d_mod, w_pad[...])
    for step in range(shards):
        outs[step][...] = result[step : step + 1]


def ada_grad_kernel(rows, wide, inverse_count, *refs):
    idx, gathered = refs[:2]
    grad_ada, sums, turned = refs[2:]
    layers = grad_ada.shape[0]
    width = turned.shape[0]
    turned[...] = gathered[:, :width].astype(F32).T
    own = turned[block_at(idx[0] * rows, rows), :].astype(BF)
    for layer in range(layers):
        at = width + layer * wide
        grad_ada[layer] = dot(own, gathered[:, at : at + wide]) * inverse_count
    sums[...] = col_sum(gathered[:, width:].astype(F32)) * inverse_count


def core_sum_kernel(shards, count, *refs):
    keeps, recvs, outs = refs[:count], refs[count : 2 * count], refs[2 * count :]
    for step in range(shards):
        at = 0
        for keep, recv in zip(keeps, recvs):
            wide = keep.shape[-1]
            total = keep[step].astype(F32) + recv[step].astype(F32)
            outs[step][:, at : at + wide] = total.astype(BF)
            at += wide


def shard_sum_kernel(shards, levels, *refs):
    idx, terms, outs = refs[0], refs[1 : 1 + shards], refs[1 + shards : 1 + shards + levels]
    units, sems = refs[1 + shards + levels :]
    total = terms[0][...].astype(F32)
    for term in terms[1:]:
        total = total + term[...].astype(F32)
    total = total.astype(BF)
    rows, wide = total.shape
    slot = 0
    for row in range(0, rows, 16):
        for col in range(0, wide, 128):
            units[slot] = total[row : row + 16, col : col + 128]
            slot += 1
    size = units.shape[0] // levels
    for extra in range(slot, units.shape[0]):
        units[extra] = jnp.zeros((16, 128), BF)
    for step in range(levels):
        outs[step][...] = units[pl.ds(jnp.bitwise_xor(idx[1], step) * size, size)]


def level_sum_kernel(*refs):
    total = refs[0][...].astype(F32)
    for term in refs[1:-1]:
        total = total + term[...].astype(F32)
    refs[-1][...] = total.astype(BF)


def unpack_units(idx, near, far, units):
    size = near[0].shape[0]
    for step, (near_piece, far_piece) in enumerate(zip(near, far)):
        place = pl.ds(jnp.bitwise_xor(idx[1], step) * size, size)
        units[idx[2], place] = near_piece[...]
        units[1 - idx[2], place] = far_piece[...]


def place_units(units, half, first, target, rows, wide, at_row, at_col, skip, total_wide, factor):
    for row in range(0, rows, 16):
        for col in range(0, wide, 128):
            slot = first + (row // 16) * (total_wide // 128) + (skip + col) // 128
            target[at_row + row : at_row + row + 16, at_col + col : at_col + col + 128] = (
                units[half, slot].astype(F32) * factor
            )


def finish_qkv(units, target_qkv, target_proj, rows, skip, total_wide, factor):
    width = target_proj.shape[-1]
    put = functools.partial(
        place_units, rows=rows, at_row=0, total_wide=total_wide, factor=factor, first=0
    )
    put(units, 0, target=target_qkv, wide=2 * width, at_col=0, skip=skip)
    put(units, 1, target=target_qkv, wide=width, at_col=2 * width, skip=skip)
    put(units, 1, target=target_proj, wide=width, at_col=0, skip=skip + width)


def finish_mlp(units, target_fc1, target_fc2, rows, skip, total_wide, factor):
    width = target_fc2.shape[-1]
    hidden = target_fc1.shape[-1]
    put = functools.partial(
        place_units, rows=rows, total_wide=total_wide, factor=factor, first=0
    )
    put(units, 0, target=target_fc1, wide=hidden, at_row=0, at_col=0, skip=skip)
    for part in range(hidden // width):
        put(
            units, 1, target=target_fc2, wide=width, at_row=part * rows, at_col=0,
            skip=skip + part * width,
        )


def finish_kernel(rows, levels, plan, factor, *refs):
    idx = refs[0]
    at = 1
    groups = []
    for _ in plan:
        groups.append((refs[at : at + levels], refs[at + levels : at + 2 * levels]))
        at += 2 * levels
    g_qkv, g_proj, g_fc1, g_fc2 = refs[at : at + 4]
    scratch = refs[at + 4 :]
    for (near, far), units, (members, total_wide) in zip(groups, scratch, plan):
        unpack_units(idx, near, far, units)
        for kind, layer, skip in members:
            if kind == "qkv":
                finish_qkv(
                    units, g_qkv.at[layer], g_proj.at[layer], rows, skip, total_wide, factor
                )
            else:
                finish_mlp(units, g_fc1.at[layer], g_fc2.at[layer], rows, skip, total_wide, factor)


def shards(
    latents, condition, cotangent, w_qkv, b_qv, w_proj, b_proj, w_fc1, b_fc1, w_fc2, b_fc2, w_ada,
    b_ada,
):
    layers, rows, _ = w_qkv.shape
    width = w_proj.shape[-1]
    hidden = w_fc1.shape[-1]
    wide = w_ada.shape[-1]
    seq = latents.shape[1]
    n_shard = lax.axis_size("shard")
    n_rep = lax.axis_size("rep")
    levels = n_rep // CORES
    peers = n_shard - 1
    shard_id = lax.axis_index("shard")
    rep_id = lax.axis_index("rep")
    core = rep_id % CORES
    idx = jnp.stack([shard_id, rep_id // CORES, core]).astype(jnp.int32)
    total_latents = latents.shape[0] * n_shard * n_rep
    factor = 1.0 / total_latents

    def exchange(array, by_shard=0, by_level=0, by_core=0):
        moves = []
        for own_shard in range(n_shard):
            for own_rep in range(n_rep):
                peer = (own_shard ^ by_shard) * n_rep + (own_rep ^ (by_level * CORES + by_core))
                moves.append((own_shard * n_rep + own_rep, peer))
        return lax.ppermute(array, ("shard", "rep"), moves)

    def half_qkv(layer):
        other = jnp.concatenate([w_qkv[layer, :, 2 * width :], w_proj[layer]], axis=1)
        return jnp.where(core == 0, w_qkv[layer, :, : 2 * width], other)

    def half_mlp(layer):
        other = jnp.concatenate(
            [w_fc2[layer, part * rows : (part + 1) * rows] for part in range(hidden // width)],
            axis=1,
        )
        return jnp.where(core == 0, w_fc1[layer], other)

    def gather(half):
        near = [exchange(half, by_shard=step) for step in range(1, n_shard)]
        far = [exchange(piece, by_core=1) for piece in near]
        return near, far

    def spread(bias):
        length = bias.shape[0]
        at = lax.broadcasted_iota(jnp.int32, (1, n_shard * length), 1) // length
        return jnp.where(at == shard_id, jnp.tile(bias[None, :], (1, n_shard)), 0).astype(BF)

    small = [condition]
    for layer in range(layers):
        small += [spread(part[layer]) for part in (b_qv, b_proj, b_fc1, b_fc2)]
    small += [spread(b_ada[layer]) for layer in range(layers)]
    small = jnp.concatenate(small, axis=1)

    pieces = [(gather(half_qkv(0)), 0)]
    small_all = [small] + [exchange(small, by_shard=step) for step in range(1, n_shard)]
    mlp_first = gather(half_mlp(0))
    later = [
        gather(jnp.concatenate([half_qkv(layer), half_mlp(layer)], axis=1))
        for layer in range(1, layers)
    ]
    qkv_pieces = pieces + [(item, 0) for item in later]
    mlp_pieces = [(mlp_first, 0)] + [(item, 2 * width) for item in later]

    pad_scratch = [pltpu.VMEM((width, layers * wide), BF), pltpu.SemaphoreType.DMA((layers,))]
    partial = run(
        functools.partial(modulate_kernel, n_shard), "modulate",
        [(idx, "s"), (w_ada, "a")] + [(array, "v") for array in small_all],
        [((1, layers * wide), F32, "v")] * n_shard, pad_scratch, flops=10**7,
    )
    bias_all = sum(array[:, width:].astype(F32) for array in small_all)
    per_layer = 4 * width + hidden
    mod_all = partial[0] + bias_all[:, layers * per_layer :]
    for step in range(1, n_shard):
        mod_all = mod_all + exchange(partial[step], by_shard=step)
    mods = [mod_all[:, layer * wide : (layer + 1) * wide] for layer in range(layers)]
    biases = []
    for layer in range(layers):
        at = layer * per_layer
        cuts = (at, at + 2 * width, at + 3 * width, at + 3 * width + hidden, at + per_layer)
        biases.append([bias_all[:, cuts[part] : cuts[part + 1]] for part in range(4)])

    big = seq * width
    row = lambda kind="v": ((seq, width), F32, kind)

    def piece_args(pair):
        return [(array, "a") for array in pair[0] + pair[1]]

    qkv_sems = pltpu.SemaphoreType.DMA((3 + 2 * peers,))
    mlp_sems = pltpu.SemaphoreType.DMA((1 + hidden // width + 2 * peers,))
    out_sems = pltpu.SemaphoreType.DMA((2 * n_shard,))
    w_qkv_all = pltpu.VMEM((2, width, 2 * width), BF)
    w_mlp_all = pltpu.VMEM((2, width, hidden), BF)

    def grads_out(half_wide):
        return [((n_shard, rows, half_wide), BF, "a")] * 2

    stream = latents[0]
    saved = []
    grad_stream = None
    vec_qkv, vec_mlp = [None] * layers, [None] * layers
    raw = {}
    for layer in range(layers):
        pair, offset = qkv_pieces[layer]
        b_qv_l, b_proj_l, b_fc1_l, b_fc2_l = biases[layer]
        qkv, probs, attended, branch, middle = run(
            functools.partial(attention_forward, layer, rows, offset, peers), "attention_forward",
            [(idx, "s"), (stream, "v"), (mods[layer], "v"), (b_qv_l, "v"), (b_proj_l, "v"),
             (w_qkv, "a"), (w_proj, "a")] + piece_args(pair),
            [((seq, 3 * width), BF, "v"), ((HEADS, seq, seq), F32, "v"), ((seq, width), BF, "v"),
             row(), row()],
            [w_qkv_all, qkv_sems], flops=10 * big * width,
        )
        pair, offset = mlp_pieces[layer]
        entry = dict(stream=stream, qkv=qkv, probs=probs, attended=attended, branch=branch,
                     middle=middle)
        if layer + 1 < layers:
            act_low, slopes, mlp_out, stream = run(
                functools.partial(mlp_forward, layer, rows, offset, peers), "mlp_forward",
                [(idx, "s"), (middle, "v"), (mods[layer], "v"), (b_fc1_l, "v"), (b_fc2_l, "v"),
                 (w_fc1, "a"), (w_fc2, "a")] + piece_args(pair),
                [((seq, hidden), BF, "v"), ((seq, hidden), F32, "v"), row(), row()],
                [w_mlp_all, mlp_sems], flops=16 * big * width,
            )
            entry.update(act_low=act_low, slopes=slopes, mlp_out=mlp_out)
        else:
            x_out, d_middle, vec_mlp[layer], keep, send = run(
                functools.partial(mlp_both, layer, rows, offset, peers), "mlp_both",
                [(idx, "s"), (middle, "v"), (mods[layer], "v"), (b_fc1_l, "v"), (b_fc2_l, "v"),
                 (cotangent[0], "v"), (w_fc1, "a"), (w_fc2, "a")] + piece_args(pair),
                [((seq, width), BF, "v"), row(), ((1, 4 * width + hidden), F32, "v")]
                + grads_out(hidden),
                [w_mlp_all, w_mlp_all, pltpu.VMEM((seq, hidden), BF),
                 pltpu.VMEM((seq, hidden), F32), mlp_sems, out_sems], flops=48 * big * width,
            )
            raw["mlp", layer] = (keep, send)
        saved.append(entry)

    def reduce_group(keys):
        pairs = [raw[key] for key in keys]
        received = [exchange(send, by_core=1) for _, send in pairs]
        total_wide = sum(keep.shape[-1] for keep, _ in pairs)
        summed = run(
            functools.partial(core_sum_kernel, n_shard, len(pairs)), "core_sum",
            [(keep, "v") for keep, _ in pairs] + [(array, "v") for array in received],
            [((rows, total_wide), BF, "v")] * n_shard,
        )
        arrived = [exchange(summed[step], by_shard=step) for step in range(1, n_shard)]
        size = -(-(rows // 16) * (total_wide // 128) // levels)
        chunks = run(
            functools.partial(shard_sum_kernel, n_shard, levels), "shard_sum",
            [(idx, "s"), (summed[0], "v")] + [(array, "v") for array in arrived],
            [((size, 16, 128), BF, "v")] * levels,
            [pltpu.VMEM((size * levels, 16, 128), BF), pltpu.SemaphoreType.DMA((1,))],
        )
        arrived = [exchange(chunks[step], by_level=step) for step in range(1, levels)]
        (total,) = run(
            level_sum_kernel, "level_sum",
            [(chunks[0], "v")] + [(array, "v") for array in arrived],
            [((size, 16, 128), BF, "v")],
        )
        near = [total] + [exchange(total, by_level=step) for step in range(1, levels)]
        far = [exchange(array, by_core=1) for array in near]
        return near, far, total_wide

    plan, finals = [], []
    for layer in reversed(range(layers)):
        entry = saved[layer]
        pair, offset = mlp_pieces[layer]
        if layer + 1 < layers:
            d_middle, vec_mlp[layer], keep, send = run(
                functools.partial(mlp_backward, layer, rows, offset, peers), "mlp_backward",
                [(idx, "s"), (entry["middle"], "v"), (mods[layer], "v"), (grad_stream, "v"),
                 (entry["act_low"], "v"), (entry["slopes"], "v"), (entry["mlp_out"], "v"),
                 (w_fc1, "a"), (w_fc2, "a")] + piece_args(pair),
                [row(), ((1, 4 * width + hidden), F32, "v")] + grads_out(hidden),
                [w_mlp_all, w_mlp_all, mlp_sems, out_sems], flops=32 * big * width,
            )
            raw["mlp", layer] = (keep, send)
            keys = [("qkv", layer + 1), ("mlp", layer)]
        else:
            keys = [("mlp", layer)]
        finals.append(reduce_group(keys))
        plan.append(keys)
        pair, offset = qkv_pieces[layer]
        grad_stream, vec_qkv[layer], keep, send = run(
            functools.partial(attention_backward, layer, rows, offset, peers),
            "attention_backward",
            [(idx, "s"), (entry["stream"], "v"), (mods[layer], "v"), (d_middle, "v"),
             (entry["qkv"], "v"), (entry["probs"], "v"), (entry["attended"], "v"),
             (entry["branch"], "v"), (w_qkv, "a"), (w_proj, "a")] + piece_args(pair),
            [row(), ((1, 6 * width), F32, "v")] + grads_out(2 * width),
            [w_qkv_all, pltpu.VMEM((seq, 3 * width), BF), w_qkv_all, qkv_sems, out_sems],
            flops=28 * big * width,
        )
        raw["qkv", layer] = (keep, send)
    finals.append(reduce_group([("qkv", 0)]))
    plan.append([("qkv", 0)])

    cond_in = condition.astype(F32)
    vector = [jax.nn.silu(cond_in).astype(BF)]
    for layer in range(layers):
        vector += [vec_qkv[layer][:, : 3 * width].astype(BF), vec_mlp[layer][:, : 3 * width].astype(BF)]
    for layer in range(layers):
        vector += [vec_qkv[layer][:, 3 * width :].astype(BF), vec_mlp[layer][:, 3 * width :].astype(BF)]
    vector = jnp.concatenate(vector, axis=1)
    same_shard = [vector] + [exchange(vector, by_level=step) for step in range(1, levels)]
    group = [vector] + [exchange(vector, by_shard=step) for step in range(1, n_shard)]
    packed = jnp.concatenate(same_shard[1:], axis=0)
    packed_all = [packed] + [exchange(packed, by_shard=step) for step in range(1, n_shard)]
    half_rows = jnp.concatenate(group + packed_all, axis=0)
    gathered = jnp.concatenate([half_rows, exchange(half_rows, by_core=1)], axis=0)
    grad_ada, sums = run(
        functools.partial(ada_grad_kernel, rows, wide, factor), "ada_grad",
        [(idx, "s"), (gathered, "v")],
        [((layers, rows, wide), F32, "v"), ((1, vector.shape[1] - width), F32, "v")],
        [pltpu.VMEM((width, total_latents), F32)], flops=10**8,
    )
    d_cond = run(
        functools.partial(condition_back_kernel, n_shard), "condition_back",
        [(idx, "s"), (w_ada, "a")] + [(array, "v") for array in group],
        [((1, width), F32, "v")] * n_shard, pad_scratch, flops=10**7,
    )
    grad_cond = d_cond[0]
    for step in range(1, n_shard):
        grad_cond = grad_cond + exchange(d_cond[step], by_shard=step)
    cond_grad = jax.vjp(jax.nn.silu, cond_in)[1](grad_cond)[0]

    def own_part(parts):
        whole = jnp.concatenate(parts, axis=0)
        length = whole.shape[1] // n_shard
        return lax.dynamic_slice_in_dim(whole, shard_id * length, length, axis=1)

    base = layers * wide
    at = [base + layer * (4 * width + hidden) for layer in range(layers)]
    grad_ada_bias = own_part([sums[:, layer * wide : (layer + 1) * wide] for layer in range(layers)])
    grad_qv_bias = own_part([sums[:, a : a + 2 * width] for a in at])
    grad_proj_bias = own_part([sums[:, a + 2 * width : a + 3 * width] for a in at])
    grad_fc1_bias = own_part([sums[:, a + 3 * width : a + 3 * width + hidden] for a in at])
    grad_fc2_bias = own_part([sums[:, a + 3 * width + hidden : a + 4 * width + hidden] for a in at])

    finish_plan, finish_inputs, finish_scratch = [], [(idx, "s")], []
    for keys, (near, far, total_wide) in zip(plan, finals):
        members, skip = [], 0
        for kind, layer in keys:
            members.append((kind, layer, skip))
            skip += 2 * width if kind == "qkv" else hidden
        finish_plan.append((members, total_wide))
        finish_inputs += [(array, "v") for array in near + far]
        finish_scratch.append(pltpu.VMEM((2, near[0].shape[0] * levels, 16, 128), BF))
    grad_qkv, grad_proj, grad_fc1, grad_fc2 = run(
        functools.partial(finish_kernel, rows, levels, finish_plan, factor), "finish",
        finish_inputs,
        [(array.shape, F32, "v") for array in (w_qkv, w_proj, w_fc1, w_fc2)],
        finish_scratch,
    )
    return (
        x_out[None], grad_stream[None], cond_grad, grad_qkv, grad_qv_bias, grad_proj,
        grad_proj_bias, grad_fc1, grad_fc1_bias, grad_fc2, grad_fc2_bias, grad_ada, grad_ada_bias,
    )


def solution(mesh):
    rows3, rows2 = P(("shard", "rep"), None, None), P(("shard", "rep"), None)
    weight, bias = P(None, "shard", None), P(None, "shard")
    return jax.shard_map(
        shards,
        mesh=mesh,
        in_specs=(rows3, rows2, rows3) + (weight, bias) * 5,
        out_specs=(rows3, rows3, rows2) + (weight, bias) * 5,
        check_vma=False,
    )
```

```python
import functools

import jax
import jax.numpy as jnp
from jax import lax
from jax.experimental import pallas as pl
from jax.experimental.pallas import tpu as pltpu
from jax.sharding import PartitionSpec as P

HEADS = 6
BF = jnp.bfloat16
F32 = jnp.float32
CORES = 2
VMEM_LIMIT = 40 * 1024 * 1024


def dot(left, right):
    return jnp.dot(left, right, preferred_element_type=F32)


def dot_nt(left, right):
    return lax.dot_general(left, right, (((1,), (1,)), ((), ())), preferred_element_type=F32)


def dot_tn(left, right):
    return lax.dot_general(left, right, (((0,), (0,)), ((), ())), preferred_element_type=F32)


def layer_norm(rows):
    center = rows - jnp.mean(rows, axis=-1, keepdims=True)
    inverse = lax.rsqrt(jnp.mean(center * center, axis=-1, keepdims=True) + 1e-06)
    return center * inverse, inverse


def norm_back(grad_norm, normed, inverse):
    centered = grad_norm - jnp.mean(grad_norm, axis=-1, keepdims=True)
    return inverse * (centered - normed * jnp.mean(grad_norm * normed, axis=-1, keepdims=True))


def col_sum(rows):
    return jnp.sum(rows, axis=0, keepdims=True)


def block_at(start, size):
    return pl.ds(pl.multiple_of(start, size), size)


def start_all(copies):
    for copy in copies:
        copy.start()


def wait_all(copies):
    for copy in copies:
        copy.wait()


def make_copies(pairs, sems):
    return [
        pltpu.make_async_copy(source, target, sems.at[slot])
        for slot, (source, target) in enumerate(pairs)
    ]


def run(body, name, inputs, outputs, scratch=(), flops=0):
    places = {"v": pltpu.VMEM, "a": pl.ANY, "s": pltpu.SMEM}
    moved = sum(arr.size * arr.dtype.itemsize for arr, _ in inputs)
    return pl.pallas_call(
        body,
        out_shape=[jax.ShapeDtypeStruct(shape, dtype) for shape, dtype, _ in outputs],
        in_specs=[pl.BlockSpec(memory_space=places[kind]) for _, kind in inputs],
        out_specs=[pl.BlockSpec(memory_space=places[kind]) for _, _, kind in outputs],
        scratch_shapes=list(scratch),
        compiler_params=pltpu.CompilerParams(vmem_limit_bytes=VMEM_LIMIT),
        cost_estimate=pl.CostEstimate(flops=1, bytes_accessed=1, transcendentals=0),
        name=name,
    )(*[arr for arr, _ in inputs])


def pack_kernel(plan, *refs):
    w_qkv, w_proj, w_fc1, w_fc2 = refs[:4]
    outs, sems = refs[4:-1], refs[-1]
    rows, width = w_proj.shape[1:]
    hidden = w_fc1.shape[-1]
    pairs = []
    for (layer, kinds), out in zip(plan, outs):
        at = 0
        pieces = {"qkv": [w_qkv.at[layer, :, : 2 * width]], "mlp": [w_fc1.at[layer]]}
        second = {
            "qkv": [w_qkv.at[layer, :, 2 * width :], w_proj.at[layer]],
            "mlp": [
                w_fc2.at[layer, part * rows : (part + 1) * rows]
                for part in range(hidden // width)
            ],
        }
        for half in (pieces, second):
            for kind in kinds:
                for piece in half[kind]:
                    pairs.append((piece, out.at[:, at : at + piece.shape[-1]]))
                    at += piece.shape[-1]
    copies = make_copies(pairs, sems)
    start_all(copies)
    wait_all(copies)


def piece_count(shards):
    return 2 if shards == 4 else shards - 1


def peer_order(shards, core):
    if shards != 4:
        return list(range(shards))
    return [0, 2 - core, 1 + core, 3]


def qkv_pairs(idx, layer, rows, offset, w_qkv, w_proj, near, far, w_all):
    width = w_proj.shape[-1]
    own = block_at(idx[0] * rows, rows)
    pairs = [
        (w_qkv.at[layer, :, : 2 * width], w_all.at[0, own, :]),
        (w_qkv.at[layer, :, 2 * width :], w_all.at[1, own, :width]),
        (w_proj.at[layer], w_all.at[1, own, width:]),
    ]
    return pairs + piece_pairs(idx, rows, offset, 2 * width, near, far, w_all)


def mlp_pairs(idx, layer, rows, offset, w_fc1, w_fc2, near, far, w_all):
    width = w_fc2.shape[-1]
    hidden = w_fc1.shape[-1]
    own = block_at(idx[0] * rows, rows)
    pairs = [(w_fc1.at[layer], w_all.at[0, own, :])]
    for part in range(hidden // width):
        pairs.append(
            (
                w_fc2.at[layer, part * rows : (part + 1) * rows, :],
                w_all.at[1, own, part * width : (part + 1) * width],
            )
        )
    return pairs + piece_pairs(idx, rows, offset, hidden, near, far, w_all)


def piece_pairs(idx, rows, offset, wide, near, far, w_all):
    pairs = []
    shards = w_all.shape[1] // rows
    for pieces, core in ((near, idx[2]), (far, 1 - idx[2])):
        for slot, piece in enumerate(pieces):
            if shards != 4:
                mask, halves = slot + 1, [(core, 0)]
            elif slot == 0:
                mask, halves = 1 + core, [(0, 0), (1, piece.shape[1] // 2)]
            else:
                mask, halves = 3, [(core, 0)]
            place = block_at(jnp.bitwise_xor(idx[0], mask) * rows, rows)
            for half, first in halves:
                at = first + offset
                pairs.append((piece.at[:, at : at + wide], w_all.at[half, place, :]))
    return pairs


def grad_pairs(idx, rows, shards, grad_all, keep, send):
    pairs = []
    for slot in range(shards):
        for target, core in ((keep, idx[2]), (send, 1 - idx[2])):
            mask = peer_order(shards, core)[slot]
            place = block_at(jnp.bitwise_xor(idx[0], mask) * rows, rows)
            pairs.append((grad_all.at[core, place, :], target.at[slot]))
    return pairs


def fc2_chunk(w_all, rows, chunk):
    width = w_all.shape[1]
    parts = w_all.shape[2] // width
    blocks = []
    for number in range(chunk * width // rows, (chunk + 1) * width // rows):
        at, part = number // parts, number % parts
        blocks.append(w_all[1, at * rows : (at + 1) * rows, part * width : (part + 1) * width])
    return jnp.concatenate(blocks, axis=0)


def attention_forward(layer, rows, offset, shards, *refs):
    peers = piece_count(shards)
    idx, stream, mod_all, w_qkv, w_proj = refs[:5]
    near, far = refs[5 : 5 + peers], refs[5 + peers : 5 + 2 * peers]
    qkv_out, probs_out, attended_out, branch_out, middle_out, w_all, sems = refs[5 + 2 * peers :]
    mod = mod_all.at[layer : layer + 1]
    copies = make_copies(
        qkv_pairs(idx, layer, rows, offset, w_qkv, w_proj, near, far, w_all), sems
    )
    start_all(copies)
    width = stream.shape[-1]
    head = width // HEADS
    b_qv, b_proj = mod[:, 6 * width : 8 * width], mod[:, 8 * width : 9 * width]
    values = stream[...].astype(F32)
    shift, scale, gate = (mod[:, part * width : (part + 1) * width] for part in range(3))
    normed, _ = layer_norm(values)
    h_one = (normed * (1.0 + scale) + shift).astype(BF)
    wait_all(copies)
    mixed = dot(h_one, w_all[0])
    qkv_out[:, :width] = (mixed[:, :width] + b_qv[:, :width]).astype(BF)
    qkv_out[:, width : 2 * width] = mixed[:, width:].astype(BF)
    qkv_out[:, 2 * width :] = (dot(h_one, w_all[1, :, :width]) + b_qv[:, width:]).astype(BF)
    lane = lax.broadcasted_iota(jnp.int32, (1, 2 * head), 1)
    masks = [(lane < head).astype(BF), (lane >= head).astype(BF)]
    for pair in range(HEADS // 2):
        at = pair * 2 * head
        queries = qkv_out[:, at : at + 2 * head]
        keys = qkv_out[:, width + at : width + at + 2 * head]
        vals = qkv_out[:, 2 * width + at : 2 * width + at + 2 * head]
        attended = 0.0
        for side in range(2):
            scores = dot_nt(queries, keys * masks[side]) * head ** (-0.5)
            raised = jnp.exp(scores - jnp.max(scores, axis=-1, keepdims=True))
            probs = raised * (1.0 / jnp.sum(raised, axis=-1, keepdims=True))
            probs_out[2 * pair + side] = probs
            attended = attended + dot(probs.astype(BF), vals * masks[side])
        attended_out[:, at : at + 2 * head] = attended.astype(BF)
    branch = dot(attended_out[...], w_all[1, :, width:]) + b_proj
    branch_out[...] = branch
    middle_out[...] = values + gate * branch


def attention_backward(layer, rows, offset, shards, *refs):
    peers = piece_count(shards)
    idx, stream, mod_all, d_middle_in, qkv, probs_in, attended, branch, w_qkv, w_proj = refs[:10]
    near, far = refs[10 : 10 + peers], refs[10 + peers : 10 + 2 * peers]
    d_stream, vec, keep, send, w_all, d_qkv, grad_all, sems, out_sems = refs[10 + 2 * peers :]
    mod = mod_all.at[layer : layer + 1]
    copies = make_copies(
        qkv_pairs(idx, layer, rows, offset, w_qkv, w_proj, near, far, w_all), sems
    )
    start_all(copies)
    width = stream.shape[-1]
    head = width // HEADS
    root = head ** (-0.5)
    shift, scale, gate = (mod[:, part * width : (part + 1) * width] for part in range(3))
    normed, inverse = layer_norm(stream[...].astype(F32))
    h_one = (normed * (1.0 + scale) + shift).astype(BF)
    d_middle = d_middle_in[...]
    vec[:, 2 * width : 3 * width] = col_sum(d_middle * branch[...])
    d_branch = (d_middle * gate).astype(BF)
    grad_all[1, :, width:] = dot_tn(attended[...], d_branch).astype(BF)
    vec[:, 5 * width :] = col_sum(d_branch.astype(F32))
    wait_all(copies)
    d_attended = dot_nt(d_branch, w_all[1, :, width:]).astype(BF)
    lane = lax.broadcasted_iota(jnp.int32, (1, 2 * head), 1)
    masks = [(lane < head).astype(BF), (lane >= head).astype(BF)]
    for pair in range(HEADS // 2):
        at = pair * 2 * head
        queries = qkv[:, at : at + 2 * head]
        keys = qkv[:, width + at : width + at + 2 * head]
        vals = qkv[:, 2 * width + at : 2 * width + at + 2 * head]
        d_att = d_attended[:, at : at + 2 * head]
        d_queries, d_keys, d_values = 0.0, 0.0, 0.0
        for side in range(2):
            probs = probs_in[2 * pair + side]
            d_values = d_values + dot_tn(probs.astype(BF), d_att * masks[side])
            d_probs = dot_nt(d_att, vals * masks[side])
            inner = jnp.sum(probs * d_probs, axis=-1, keepdims=True)
            d_scores = (probs * (d_probs - inner)).astype(BF)
            d_queries = d_queries + dot(d_scores, keys * masks[side])
            d_keys = d_keys + dot_tn(d_scores, queries * masks[side])
        d_qkv[:, at : at + 2 * head] = (d_queries * root).astype(BF)
        d_qkv[:, width + at : width + at + 2 * head] = (d_keys * root).astype(BF)
        d_qkv[:, 2 * width + at : 2 * width + at + 2 * head] = d_values.astype(BF)
    d_qk, d_val = d_qkv[:, : 2 * width], d_qkv[:, 2 * width :]
    grad_all[0] = dot_tn(h_one, d_qk).astype(BF)
    grad_all[1, :, :width] = dot_tn(h_one, d_val).astype(BF)
    out_copies = make_copies(grad_pairs(idx, rows, shards, grad_all, keep, send), out_sems)
    start_all(out_copies)
    vec[:, 3 * width : 4 * width] = col_sum(d_qk[:, :width].astype(F32))
    vec[:, 4 * width : 5 * width] = col_sum(d_val.astype(F32))
    d_h_one = dot_nt(d_qk, w_all[0]) + dot_nt(d_val, w_all[1, :, :width])
    vec[:, :width] = col_sum(d_h_one)
    vec[:, width : 2 * width] = col_sum(d_h_one * normed)
    d_stream[...] = d_middle + norm_back(d_h_one * (1.0 + scale), normed, inverse)
    wait_all(out_copies)


def gelu_parts(pre_act):
    root = 0.7978845608028654
    square = pre_act * pre_act
    bent = jnp.tanh(root * pre_act * (1.0 + 0.044715 * square))
    half = 0.5 * (1.0 + bent)
    slope = half + 0.5 * pre_act * (1.0 - bent * bent) * (root * (1.0 + 3 * 0.044715 * square))
    return pre_act * half, slope


def mlp_vectors(mod_all, layer, width):
    mod = mod_all.at[layer : layer + 1]
    last = mod_all.shape[-1] - width
    return mod, mod[:, 9 * width : last], mod[:, last:]


def mlp_forward_part(rows, h_two, b_fc1, b_fc2, w_all, act_low, slopes):
    width = w_all.shape[1]
    mlp_out = b_fc2
    for chunk in range(w_all.shape[2] // width):
        cols = slice(chunk * width, (chunk + 1) * width)
        act, slope = gelu_parts(dot(h_two, w_all[0, :, cols]) + b_fc1[:, cols])
        act_low[:, cols] = act.astype(BF)
        slopes[:, cols] = slope
        mlp_out = mlp_out + dot(act_low[:, cols], fc2_chunk(w_all, rows, chunk))
    return mlp_out


def mlp_backward_part(
    idx, rows, shards, grad_out, mlp_out, middle, normed, inverse, h_two, scale, gate,
    w_all, act_low, slopes, vec, d_middle_out, grad_all, keep, send, out_sems,
):
    width = w_all.shape[1]
    parts = w_all.shape[2] // width
    vec[:, 2 * width : 3 * width] = col_sum(grad_out * mlp_out)
    d_mlp = (grad_out * gate).astype(BF)
    vec[:, (3 + parts) * width :] = col_sum(d_mlp.astype(F32))
    d_h_two = 0.0
    for chunk in range(parts):
        cols = slice(chunk * width, (chunk + 1) * width)
        d_act = dot_nt(d_mlp, fc2_chunk(w_all, rows, chunk))
        d_pre = (d_act * slopes[:, cols]).astype(BF)
        vec[:, (3 + chunk) * width : (4 + chunk) * width] = col_sum(d_pre.astype(F32))
        grad_all[0, :, cols] = dot_tn(h_two, d_pre).astype(BF)
        grad_fc2 = dot_tn(act_low[:, cols], d_mlp).astype(BF)
        first = chunk * width // rows
        for number in range(first, (chunk + 1) * width // rows):
            at, part = number // parts, number % parts
            grad_all[1, at * rows : (at + 1) * rows, part * width : (part + 1) * width] = grad_fc2[
                (number - first) * rows : (number - first + 1) * rows
            ]
        d_h_two = d_h_two + dot_nt(d_pre, w_all[0, :, cols])
    out_copies = make_copies(grad_pairs(idx, rows, shards, grad_all, keep, send), out_sems)
    start_all(out_copies)
    vec[:, :width] = col_sum(d_h_two)
    vec[:, width : 2 * width] = col_sum(d_h_two * normed)
    d_middle_out[...] = grad_out + norm_back(d_h_two * (1.0 + scale), normed, inverse)
    wait_all(out_copies)


def mlp_forward(layer, rows, offset, shards, *refs):
    peers = piece_count(shards)
    idx, middle, mod_all, w_fc1, w_fc2 = refs[:5]
    near, far = refs[5 : 5 + peers], refs[5 + peers : 5 + 2 * peers]
    act_low, slopes, mlp_out, stream_out, w_all, sems = refs[5 + 2 * peers :]
    mod, b_fc1, b_fc2 = mlp_vectors(mod_all, layer, middle.shape[-1])
    copies = make_copies(mlp_pairs(idx, layer, rows, offset, w_fc1, w_fc2, near, far, w_all), sems)
    start_all(copies)
    width = middle.shape[-1]
    shift, scale, gate = (mod[:, part * width : (part + 1) * width] for part in range(3, 6))
    normed, _ = layer_norm(middle[...])
    h_two = (normed * (1.0 + scale) + shift).astype(BF)
    wait_all(copies)
    mlp_out[...] = mlp_forward_part(rows, h_two, b_fc1, b_fc2, w_all, act_low, slopes)
    stream_out[...] = middle[...] + gate * mlp_out[...]


def mlp_backward(layer, rows, offset, shards, *refs):
    peers = piece_count(shards)
    idx, middle, mod_all, grad_out, act_low, slopes, mlp_out, w_fc1, w_fc2 = refs[:9]
    near, far = refs[9 : 9 + peers], refs[9 + peers : 9 + 2 * peers]
    d_middle, vec, keep, send, w_all, grad_all, sems, out_sems = refs[9 + 2 * peers :]
    mod = mod_all.at[layer : layer + 1]
    copies = make_copies(mlp_pairs(idx, layer, rows, offset, w_fc1, w_fc2, near, far, w_all), sems)
    start_all(copies)
    width = middle.shape[-1]
    shift, scale, gate = (mod[:, part * width : (part + 1) * width] for part in range(3, 6))
    normed, inverse = layer_norm(middle[...])
    h_two = (normed * (1.0 + scale) + shift).astype(BF)
    wait_all(copies)
    mlp_backward_part(
        idx, rows, shards, grad_out[...], mlp_out[...], middle, normed, inverse, h_two, scale,
        gate, w_all, act_low, slopes, vec, d_middle, grad_all, keep, send, out_sems,
    )


def mlp_both(layer, rows, offset, shards, *refs):
    peers = piece_count(shards)
    idx, middle, mod_all, cotangent, w_fc1, w_fc2 = refs[:6]
    near, far = refs[6 : 6 + peers], refs[6 + peers : 6 + 2 * peers]
    x_out, d_middle, vec, keep, send = refs[6 + 2 * peers : 11 + 2 * peers]
    w_all, grad_all, act_low, slopes, sems, out_sems = refs[11 + 2 * peers :]
    mod, b_fc1, b_fc2 = mlp_vectors(mod_all, layer, middle.shape[-1])
    copies = make_copies(mlp_pairs(idx, layer, rows, offset, w_fc1, w_fc2, near, far, w_all), sems)
    start_all(copies)
    width = middle.shape[-1]
    shift, scale, gate = (mod[:, part * width : (part + 1) * width] for part in range(3, 6))
    normed, inverse = layer_norm(middle[...])
    h_two = (normed * (1.0 + scale) + shift).astype(BF)
    wait_all(copies)
    mlp_out = mlp_forward_part(rows, h_two, b_fc1, b_fc2, w_all, act_low, slopes)
    x_out[...] = (middle[...] + gate * mlp_out).astype(BF)
    mlp_backward_part(
        idx, rows, shards, cotangent[...].astype(F32), mlp_out, middle, normed, inverse, h_two,
        scale, gate, w_all, act_low, slopes, vec, d_middle, grad_all, keep, send, out_sems,
    )


def padded_rows(idx, w_ada, w_pad, sems):
    layers, rows, wide = w_ada.shape
    w_pad[...] = jnp.zeros(w_pad.shape, BF)
    own = block_at(idx[0] * rows, rows)
    return make_copies(
        [
            (w_ada.at[layer], w_pad.at[own, layer * wide : (layer + 1) * wide])
            for layer in range(layers)
        ],
        sems,
    )


def modulate_kernel(shards, *refs):
    idx, w_ada, b_ada = refs[:3]
    biases, conditions = refs[3:7], refs[7 : 7 + shards]
    outs = refs[7 + shards : 7 + 2 * shards]
    w_pad, sems = refs[7 + 2 * shards :]
    copies = padded_rows(idx, w_ada, w_pad, sems)
    start_all(copies)
    layers = w_ada.shape[0]
    wide = w_ada.shape[2]
    acts = []
    for ref in conditions:
        cond = ref[...].astype(F32)
        acts.append(cond / (1.0 + jnp.exp(-cond)))
    acts = jnp.concatenate(acts, axis=0).astype(BF)

    def spread(bias):
        length = bias.shape[1]
        row = lax.broadcasted_iota(jnp.int32, (length, shards * length), 0)
        col = lax.broadcasted_iota(jnp.int32, (length, shards * length), 1)
        place = jnp.where(col - row == idx[0] * length, 1.0, 0.0).astype(BF)
        return dot(bias[...], place)

    first = spread(b_ada)
    at = wide
    for bias in biases:
        full = spread(bias)
        for out in outs:
            out[:, at : at + full.shape[1]] = full
        at += full.shape[1]
    wait_all(copies)
    for layer in range(layers):
        result = dot(acts, w_pad[:, layer * wide : (layer + 1) * wide]) + first[layer : layer + 1]
        for step in range(shards):
            outs[step][layer : layer + 1, :wide] = result[step : step + 1]


def stack_kernel(first, second, out, rows_f32):
    size = first.shape[0]
    rows_f32[:size] = first[...].astype(F32)
    rows_f32[size:] = second[...].astype(F32)
    out[...] = rows_f32[...].astype(BF)


def group_kernel(idx, w_ada, first, second, keep, send, stacked, rows_f32, w_pad, sems):
    copies = padded_rows(idx, w_ada, w_pad, sems)
    start_all(copies)
    width, wide = w_pad.shape
    stack_kernel(first, second, stacked, rows_f32)
    wait_all(copies)
    result = dot_nt(stacked[:, width : width + wide], w_pad[...])
    half = keep.shape[0]
    keep[...] = result[:half]
    send[...] = result[half:]


def ada_grad_kernel(rows, wide, inverse_count, *refs):
    idx, stacks = refs[0], refs[1:-4]
    grad_ada, sums, turned, gathered_f32 = refs[-4:]
    layers = grad_ada.shape[0]
    width = turned.shape[0]
    size = stacks[0].shape[0]
    for number, stack in enumerate(stacks):
        gathered_f32[number * size : (number + 1) * size] = stack[...].astype(F32)
    gathered = gathered_f32[...].astype(BF)
    turned[...] = gathered_f32[:, :width].T
    own = turned[block_at(idx[0] * rows, rows), :].astype(BF)
    for layer in range(layers):
        at = width + layer * wide
        grad_ada[layer] = dot(own, gathered[:, at : at + wide]) * inverse_count
    sums[...] = col_sum(gathered_f32[:, width:]) * inverse_count


def core_sum_kernel(slots, count, *refs):
    keeps, recvs, outs = refs[:count], refs[count : 2 * count], refs[2 * count :]
    for (first, number), out in zip(slots, outs):
        for slot in range(number):
            at = 0
            for keep, recv in zip(keeps, recvs):
                wide = keep.shape[-1]
                total = keep[first + slot].astype(F32) + recv[first + slot].astype(F32)
                out[slot, :, at : at + wide] = total.astype(BF)
                at += wide


def split_sum_kernel(mine, other, keep, send):
    keep[...] = (mine[0].astype(F32) + other[0].astype(F32)).astype(BF)
    send[...] = (mine[1].astype(F32) + other[1].astype(F32)).astype(BF)


def row_split_kernel(*refs):
    idx, terms, keep, send, halves = refs[0], refs[1:-3], refs[-3], refs[-2], refs[-1]
    total = terms[0][...].astype(F32)
    for term in terms[1:]:
        total = total + term[...].astype(F32)
    half = halves.shape[1]
    for side in range(2):
        halves[side] = total[side * half : (side + 1) * half].astype(BF)
    mine = idx[1] % 2
    keep[...] = halves[mine]
    send[...] = halves[1 - mine]


def sum_kernel(*refs):
    total = refs[0][...].astype(F32)
    for term in refs[1:-1]:
        total = total + term[...].astype(F32)
    refs[-1][...] = total.astype(BF).reshape(refs[-1].shape)


def finish_kernel(rows, plan, factor, *refs):
    idx = refs[0]
    terms = list(refs[1 : 1 + sum(2 * parts for _, parts in plan)])
    at = 1 + len(terms)
    g_qkv, g_proj, g_fc1, g_fc2 = refs[at : at + 4]
    scratch = refs[at + 4 :]
    width = g_proj.shape[-1]
    hidden = g_fc1.shape[-1]
    for (members, parts), halves in zip(plan, scratch):
        for core in (idx[2], 1 - idx[2]):
            if parts == 1:
                halves[core] = terms.pop(0)[...]
            else:
                size = terms[0].shape[0]
                for side in (idx[1] % 2, 1 - idx[1] % 2):
                    halves[core, block_at(side * size, size), :] = terms.pop(0)[...]
        for kind, layer, skip in members:
            if kind == "qkv":
                first = halves[0, :, skip : skip + 2 * width]
                g_qkv[layer, :, : 2 * width] = first.astype(F32) * factor
                second = halves[1, :, skip : skip + 2 * width].astype(F32) * factor
                g_qkv[layer, :, 2 * width :] = second[:, :width]
                g_proj[layer] = second[:, width:]
            else:
                g_fc1[layer] = halves[0, :, skip : skip + hidden].astype(F32) * factor
                for part in range(hidden // width):
                    at = skip + part * width
                    g_fc2[layer, part * rows : (part + 1) * rows] = (
                        halves[1, :, at : at + width].astype(F32) * factor
                    )


def shards(
    latents, condition, cotangent, w_qkv, b_qv, w_proj, b_proj, w_fc1, b_fc1, w_fc2, b_fc2, w_ada,
    b_ada,
):
    layers, rows, _ = w_qkv.shape
    width = w_proj.shape[-1]
    hidden = w_fc1.shape[-1]
    wide = w_ada.shape[-1]
    seq = latents.shape[1]
    n_shard = lax.axis_size("shard")
    n_rep = lax.axis_size("rep")
    levels = n_rep // CORES
    shard_id = lax.axis_index("shard")
    rep_id = lax.axis_index("rep")
    core = rep_id % CORES
    idx = jnp.stack([shard_id, rep_id // CORES, core]).astype(jnp.int32)
    total_latents = latents.shape[0] * n_shard * n_rep
    factor = 1.0 / total_latents

    def exchange(array, by_shard=0, by_level=0, by_core=0, turn=None):
        moves = []
        for own_shard in range(n_shard):
            for own_rep in range(n_rep):
                mask = turn[own_rep % CORES] if turn else by_shard
                peer = (own_shard ^ mask) * n_rep + (own_rep ^ (by_level * CORES + by_core))
                moves.append((own_shard * n_rep + own_rep, peer))
        return lax.ppermute(array, ("shard", "rep"), moves)

    def after(array, *earlier):
        return lax.optimization_barrier((array,) + earlier)[0]

    relay = n_shard == 4
    first_turn, second_turn = (1, 2), (2, 1)

    half_wide = {"qkv": 2 * width, "mlp": hidden}
    copy_total = {"qkv": 3, "mlp": 1 + hidden // width}

    def pack(*plan):
        whole = run(
            functools.partial(pack_kernel, plan), "pack",
            [(array, "a") for array in (w_qkv, w_proj, w_fc1, w_fc2)],
            [((rows, 2 * sum(half_wide[kind] for kind in kinds)), BF, "a") for _, kinds in plan],
            [pltpu.SemaphoreType.DMA((sum(copy_total[kind] for _, ks in plan for kind in ks),))],
        )
        if relay:
            return whole
        return [
            lax.dynamic_slice_in_dim(array, core * (array.shape[1] // 2), array.shape[1] // 2, 1)
            for array in whole
        ]

    def near_first(packed):
        if relay:
            return [exchange(packed, turn=first_turn)]
        return [exchange(packed, by_shard=step) for step in range(1, n_shard)]

    def near_second(near, *earlier):
        if not relay:
            return near
        half = near[0].shape[1] // 2
        source = after(near[0], *earlier) if earlier else near[0]
        part = lax.dynamic_slice_in_dim(source, core * half, half, axis=1)
        return near + [exchange(part, turn=second_turn)]

    def far_of(near, *earlier):
        return [exchange(after(piece, *earlier) if earlier else piece, by_core=1) for piece in near]

    conditions = [condition] + [exchange(condition, by_shard=step) for step in range(1, n_shard)]
    packed_qkv, packed_mlp = pack((0, ("qkv",)), (0, ("mlp",)))
    qkv_near = near_first(packed_qkv)
    mlp_near = near_first(packed_mlp)
    pad_scratch = [pltpu.VMEM((width, layers * wide), BF), pltpu.SemaphoreType.DMA((layers,))]
    span = wide + 4 * width + hidden
    partial = run(
        functools.partial(modulate_kernel, n_shard), "modulate",
        [(idx, "s"), (w_ada, "a"), (b_ada, "v"), (b_qv, "v"), (b_proj, "v"), (b_fc1, "v"),
         (b_fc2, "v")] + [(array, "v") for array in conditions],
        [((layers, span), F32, "v")] * n_shard, pad_scratch, flops=10**7,
    )
    mod_all = partial[0]
    for step in range(1, n_shard):
        mod_all = mod_all + exchange(partial[step], by_shard=step)

    qkv_near = near_second(qkv_near)
    qkv_far = far_of(qkv_near)
    mod_all = after(mod_all, *mlp_near)
    later_near = []
    for layer in range(1, layers):
        (packed,) = pack((layer, ("qkv", "mlp")))
        later_near.append(near_first(after(packed, mod_all)))
    mlp_near = near_second(mlp_near)

    big = seq * width
    row = lambda kind="v": ((seq, width), F32, kind)
    vec_wide = {"qkv": 6 * width, "mlp": 4 * width + hidden}

    def piece_args(pair):
        return [(array, "a") for array in pair[0] + pair[1]]

    copy_count = 6 if relay else 2 * (n_shard - 1)
    qkv_sems = pltpu.SemaphoreType.DMA((3 + copy_count,))
    mlp_sems = pltpu.SemaphoreType.DMA((1 + hidden // width + copy_count,))
    out_sems = pltpu.SemaphoreType.DMA((2 * n_shard,))
    w_qkv_all = pltpu.VMEM((2, width, 2 * width), BF)
    w_mlp_all = pltpu.VMEM((2, width, hidden), BF)

    def grads_out(kind):
        return [((n_shard, rows, half_wide[kind]), BF, "a")] * 2

    stream = latents[0]
    saved = []
    vecs, raw = {}, {}
    qkv_pieces, mlp_pieces = {0: ((qkv_near, qkv_far), 0)}, {}
    for layer in range(layers):
        pair, offset = qkv_pieces[layer]
        qkv, probs, attended, branch, middle = run(
            functools.partial(attention_forward, layer, rows, offset, n_shard), "attention_forward",
            [(idx, "s"), (stream, "v"), (mod_all, "v"), (w_qkv, "a"), (w_proj, "a")]
            + piece_args(pair),
            [((seq, 3 * width), BF, "v"), ((HEADS, seq, seq), F32, "v"), ((seq, width), BF, "v"),
             row(), row()],
            [w_qkv_all, qkv_sems], flops=10 * big * width,
        )
        if layer == 0:
            mlp_pieces[0] = ((mlp_near, far_of(mlp_near, middle)), 0)
            later_near = [near_second(near, middle) for near in later_near]
        pair, offset = mlp_pieces[layer]
        entry = dict(stream=stream, qkv=qkv, probs=probs, attended=attended, branch=branch,
                     middle=middle)
        if layer + 1 < layers:
            act_low, slopes, mlp_out, stream = run(
                functools.partial(mlp_forward, layer, rows, offset, n_shard), "mlp_forward",
                [(idx, "s"), (middle, "v"), (mod_all, "v"), (w_fc1, "a"), (w_fc2, "a")]
                + piece_args(pair),
                [((seq, hidden), BF, "v"), ((seq, hidden), F32, "v"), row(), row()],
                [w_mlp_all, mlp_sems], flops=16 * big * width,
            )
            entry.update(act_low=act_low, slopes=slopes, mlp_out=mlp_out)
            near = later_near[layer]
            later_pair = (near, far_of(near, stream))
            qkv_pieces[layer + 1] = (later_pair, 0)
            mlp_pieces[layer + 1] = (later_pair, 2 * width)
        else:
            x_out, d_middle, vecs["mlp", layer], *raw["mlp", layer] = run(
                functools.partial(mlp_both, layer, rows, offset, n_shard), "mlp_both",
                [(idx, "s"), (middle, "v"), (mod_all, "v"), (cotangent[0], "v"), (w_fc1, "a"),
                 (w_fc2, "a")] + piece_args(pair),
                [((seq, width), BF, "v"), row(), ((1, vec_wide["mlp"]), F32, "v")]
                + grads_out("mlp"),
                [w_mlp_all, w_mlp_all, pltpu.VMEM((seq, hidden), BF),
                 pltpu.VMEM((seq, hidden), F32), mlp_sems, out_sems], flops=48 * big * width,
            )
        saved.append(entry)

    def core_sum(keys, *earlier):
        keeps = [raw[key][0] for key in keys]
        received = [exchange(raw[key][1], by_core=1) for key in keys]
        if earlier:
            keeps[0] = after(keeps[0], *earlier)
        total_wide = sum(keep.shape[-1] for keep in keeps)
        slots = [(0, 2), (2, 2)] if relay else [(slot, 1) for slot in range(n_shard)]
        return run(
            functools.partial(core_sum_kernel, slots, len(keys)), "core_sum",
            [(array, "v") for array in keeps + received],
            [((number, rows, total_wide), BF, "v") for _, number in slots],
        )

    def shard_send(summed):
        if relay:
            return [exchange(summed[1], turn=first_turn)]
        return [exchange(summed[step], by_shard=step) for step in range(1, n_shard)]

    def add(terms, shape):
        return run(sum_kernel, "add", [(array, "v") for array in terms], [(shape, BF, "v")])[0]

    def shard_second(summed, arrived, *earlier):
        shape = summed[0].shape[1:]
        mine = after(summed[0], *earlier) if earlier else summed[0]
        if not relay:
            return [mine.reshape(shape)] + [array.reshape(shape) for array in arrived]
        keep, send = run(
            split_sum_kernel, "split_sum", [(mine, "v"), (arrived[0], "v")], [(shape, BF, "v")] * 2
        )
        return [keep, exchange(send, turn=second_turn)]

    def level_first(terms, halve, *earlier):
        shape = terms[0].shape
        if earlier:
            terms = [after(terms[0], *earlier)] + terms[1:]
        if not halve or shape[0] % 32:
            total = add(terms, shape)
            return False, total, exchange(total, by_level=1)
        part = (shape[0] // 2, shape[1])
        keep, send = run(
            row_split_kernel, "row_split",
            [(idx, "s")] + [(array, "v") for array in terms],
            [(part, BF, "v")] * 2, [pltpu.VMEM((2,) + part, BF)],
        )
        return True, keep, exchange(send, by_level=1)

    def level_second(first, *earlier):
        halved, kept, arriving = first
        if earlier:
            kept = after(kept, *earlier)
        return halved, add([kept, arriving], kept.shape)

    def level_last(halved, total):
        step = 2
        while step < levels:
            total = add([total, exchange(total, by_level=step)], total.shape)
            step *= 2
        near = [total, exchange(total, by_level=1)] if halved else [total]
        return near + far_of(near)

    waiting = []
    for layer in reversed(range(layers)):
        entry = saved[layer]
        pair, offset = mlp_pieces[layer]
        if layer + 1 < layers:
            keys = [("qkv", layer + 1), ("mlp", layer + 1)]
            summed = core_sum(keys, grad_stream)
            waiting.append((keys, summed, shard_send(summed)))
            grad_stream = after(grad_stream, summed[0])
            d_middle, vecs["mlp", layer], *raw["mlp", layer] = run(
                functools.partial(mlp_backward, layer, rows, offset, n_shard), "mlp_backward",
                [(idx, "s"), (entry["middle"], "v"), (mod_all, "v"), (grad_stream, "v"),
                 (entry["act_low"], "v"), (entry["slopes"], "v"), (entry["mlp_out"], "v"),
                 (w_fc1, "a"), (w_fc2, "a")] + piece_args(pair),
                [row(), ((1, vec_wide["mlp"]), F32, "v")] + grads_out("mlp"),
                [w_mlp_all, w_mlp_all, mlp_sems, out_sems], flops=32 * big * width,
            )
        pair, offset = qkv_pieces[layer]
        grad_stream, vecs["qkv", layer], *raw["qkv", layer] = run(
            functools.partial(attention_backward, layer, rows, offset, n_shard),
            "attention_backward",
            [(idx, "s"), (entry["stream"], "v"), (mod_all, "v"), (d_middle, "v"),
             (entry["qkv"], "v"), (entry["probs"], "v"), (entry["attended"], "v"),
             (entry["branch"], "v"), (w_qkv, "a"), (w_proj, "a")] + piece_args(pair),
            [row(), ((1, vec_wide["qkv"]), F32, "v")] + grads_out("qkv"),
            [w_qkv_all, pltpu.VMEM((seq, 3 * width), BF), w_qkv_all, qkv_sems, out_sems],
            flops=28 * big * width,
        )
    (keys_first, summed, arrived), = waiting
    terms_first = shard_second(summed, arrived, grad_stream)
    core_mlp = core_sum([("mlp", 0)], terms_first[0])
    sent_mlp = shard_send(core_mlp)
    level_a = level_first(terms_first, True, core_mlp[0])
    core_qkv = core_sum([("qkv", 0)], level_a[1])
    sent_qkv = shard_send(core_qkv)
    terms_mlp = shard_second(core_mlp, sent_mlp, core_qkv[0])
    terms_qkv = shard_second(core_qkv, sent_qkv, terms_mlp[0])

    cond_in = condition.astype(F32)
    vector = [jax.nn.silu(cond_in).astype(BF)]
    for layer in range(layers):
        vector += [vecs[kind, layer][:, : 3 * width].astype(BF) for kind in ("qkv", "mlp")]
    for layer in range(layers):
        vector += [vecs[kind, layer][:, 3 * width :].astype(BF) for kind in ("qkv", "mlp")]
    vector = after(jnp.concatenate(vector, axis=1), terms_qkv[0])
    length = vector.shape[1]
    masks = [first_turn, second_turn] if relay else []
    while not relay and 2 ** len(masks) < n_shard:
        masks.append((2 ** len(masks),) * 2)

    def stack(first, second):
        shape = (2 * first.shape[0], length)
        return run(
            stack_kernel, "stack", [(first, "v"), (second, "v")], [(shape, BF, "v")],
            [pltpu.VMEM(shape, F32)],
        )[0]

    total_a = level_second(level_a, vector)
    level_b = level_first(terms_mlp, True, total_a[1])
    level_c = level_first(terms_qkv, False, level_b[1])
    plan = [keys_first, [("mlp", 0)], [("qkv", 0)]]
    finals = [level_last(*total_a), level_last(*level_second(level_b)),
              level_last(*level_second(level_c))]
    for mask in masks[:-1]:
        vector = stack(vector, exchange(vector, turn=mask))
    grad_cond, passed, stacked = run(
        group_kernel, "group",
        [(idx, "s"), (w_ada, "a"), (vector, "v"), (exchange(vector, turn=masks[-1]), "v")],
        [((n_shard // 2, width), F32, "v")] * 2 + [((n_shard, length), BF, "v")],
        [pltpu.VMEM((n_shard, length), F32)] + pad_scratch, flops=10**7,
    )
    grad_cond = grad_cond + exchange(passed, turn=masks[-1])
    for mask in masks[-2::-1]:
        half = grad_cond.shape[0] // 2
        grad_cond = grad_cond[:half] + exchange(grad_cond[half:], turn=mask)
    cond_grad = jax.vjp(jax.nn.silu, cond_in)[1](grad_cond)[0]
    step = 1
    while 2 * step < levels:
        stacked = stack(stacked, exchange(stacked, by_level=step))
        step *= 2
    stacks = [stacked, exchange(stacked, by_level=step)]
    stacks = stacks + far_of(stacks)
    grad_ada, sums = run(
        functools.partial(ada_grad_kernel, rows, wide, factor), "ada_grad",
        [(idx, "s")] + [(array, "v") for array in stacks],
        [((layers, rows, wide), F32, "v"), ((1, length - width), F32, "v")],
        [pltpu.VMEM((width, total_latents), F32), pltpu.VMEM((total_latents, length), F32)],
        flops=10**8,
    )

    def own_part(parts):
        whole = jnp.concatenate(parts, axis=0)
        length = whole.shape[1] // n_shard
        return lax.dynamic_slice_in_dim(whole, shard_id * length, length, axis=1)

    base = layers * wide
    at = [base + layer * (4 * width + hidden) for layer in range(layers)]
    grad_ada_bias = own_part([sums[:, layer * wide : (layer + 1) * wide] for layer in range(layers)])
    grad_qv_bias = own_part([sums[:, a : a + 2 * width] for a in at])
    grad_proj_bias = own_part([sums[:, a + 2 * width : a + 3 * width] for a in at])
    grad_fc1_bias = own_part([sums[:, a + 3 * width : a + 3 * width + hidden] for a in at])
    grad_fc2_bias = own_part([sums[:, a + 3 * width + hidden : a + 4 * width + hidden] for a in at])

    finish_plan, finish_inputs, finish_scratch = [], [(idx, "s")], []
    for keys, parts in zip(plan, finals):
        members, skip = [], 0
        for kind, layer in keys:
            members.append((kind, layer, skip))
            skip += half_wide[kind]
        finish_plan.append((members, len(parts) // 2))
        finish_inputs += [(array, "v") for array in parts]
        finish_scratch.append(pltpu.VMEM((2, rows, skip), BF))
    grad_qkv, grad_proj, grad_fc1, grad_fc2 = run(
        functools.partial(finish_kernel, rows, finish_plan, factor), "finish",
        finish_inputs,
        [(array.shape, F32, "v") for array in (w_qkv, w_proj, w_fc1, w_fc2)],
        finish_scratch,
    )
    return (
        x_out[None], grad_stream[None], cond_grad, grad_qkv, grad_qv_bias, grad_proj,
        grad_proj_bias, grad_fc1, grad_fc1_bias, grad_fc2, grad_fc2_bias, grad_ada, grad_ada_bias,
    )


def solution(mesh):
    rows3, rows2 = P(("shard", "rep"), None, None), P(("shard", "rep"), None)
    weight, bias = P(None, "shard", None), P(None, "shard")
    return jax.shard_map(
        shards,
        mesh=mesh,
        in_specs=(rows3, rows2, rows3) + (weight, bias) * 5,
        out_specs=(rows3, rows3, rows2) + (weight, bias) * 5,
        check_vma=False,
    )
```

```python
import functools

import jax
import jax.numpy as jnp
from jax import lax
from jax.experimental import pallas as pl
from jax.experimental.pallas import tpu as pltpu
from jax.sharding import PartitionSpec as P

HEADS = 6
BF = jnp.bfloat16
F32 = jnp.float32
CORES = 2
VMEM_LIMIT = 40 * 1024 * 1024


def dot(left, right):
    return jnp.dot(left, right, preferred_element_type=F32)


def dot_nt(left, right):
    return lax.dot_general(left, right, (((1,), (1,)), ((), ())), preferred_element_type=F32)


def dot_tn(left, right):
    return lax.dot_general(left, right, (((0,), (0,)), ((), ())), preferred_element_type=F32)


def layer_norm(rows):
    center = rows - jnp.mean(rows, axis=-1, keepdims=True)
    inverse = lax.rsqrt(jnp.mean(center * center, axis=-1, keepdims=True) + 1e-06)
    return center * inverse, inverse


def norm_back(grad_norm, normed, inverse):
    centered = grad_norm - jnp.mean(grad_norm, axis=-1, keepdims=True)
    return inverse * (centered - normed * jnp.mean(grad_norm * normed, axis=-1, keepdims=True))


def col_sum(rows):
    return jnp.sum(rows, axis=0, keepdims=True)


def block_at(start, size):
    return pl.ds(pl.multiple_of(start, size), size)


def start_all(copies):
    for copy in copies:
        copy.start()


def wait_all(copies):
    for copy in copies:
        copy.wait()


def make_copies(pairs, sems):
    return [
        pltpu.make_async_copy(source, target, sems.at[slot])
        for slot, (source, target) in enumerate(pairs)
    ]


def run(body, name, inputs, outputs, scratch=(), flops=0):
    places = {"v": pltpu.VMEM, "k": pltpu.VMEM, "a": pl.ANY, "h": pl.ANY, "s": pltpu.SMEM}
    arrays = [
        pltpu.with_memory_space_constraint(arr, pltpu.HBM) if kind in "hk" else arr
        for arr, kind in inputs
    ]
    return pl.pallas_call(
        body,
        out_shape=[
            pltpu.HBM(shape, dtype) if kind in "hk" else jax.ShapeDtypeStruct(shape, dtype)
            for shape, dtype, kind in outputs
        ],
        in_specs=[pl.BlockSpec(memory_space=places[kind]) for _, kind in inputs],
        out_specs=[pl.BlockSpec(memory_space=places[kind]) for _, _, kind in outputs],
        scratch_shapes=list(scratch),
        compiler_params=pltpu.CompilerParams(vmem_limit_bytes=VMEM_LIMIT),
        cost_estimate=pl.CostEstimate(flops=1, bytes_accessed=1, transcendentals=0),
        name=name,
    )(*arrays)


def pack_kernel(plan, *refs):
    w_qkv, w_proj, w_fc1, w_fc2 = refs[:4]
    outs, sems = refs[4:-1], refs[-1]
    rows, width = w_proj.shape[1:]
    hidden = w_fc1.shape[-1]
    pairs = []
    for (layer, kinds), out in zip(plan, outs):
        at = 0
        pieces = {"qkv": [w_qkv.at[layer, :, : 2 * width]], "mlp": [w_fc1.at[layer]]}
        second = {
            "qkv": [w_qkv.at[layer, :, 2 * width :], w_proj.at[layer]],
            "mlp": [
                w_fc2.at[layer, part * rows : (part + 1) * rows]
                for part in range(hidden // width)
            ],
        }
        for half in (pieces, second):
            for kind in kinds:
                for piece in half[kind]:
                    pairs.append((piece, out.at[:, at : at + piece.shape[-1]]))
                    at += piece.shape[-1]
    copies = make_copies(pairs, sems)
    start_all(copies)
    wait_all(copies)


def half_kernel(idx, whole, out, sems):
    half = out.shape[1]
    copies = make_copies([(whole.at[:, block_at(idx[2] * half, half)], out)], sems)
    start_all(copies)
    wait_all(copies)


def piece_count(shards):
    return 2 if shards == 4 else shards - 1


def peer_order(shards, core):
    if shards != 4:
        return list(range(shards))
    return [0, 2 - core, 1 + core, 3]


def qkv_pairs(idx, layer, rows, offset, w_qkv, w_proj, near, far, w_all):
    width = w_proj.shape[-1]
    own = block_at(idx[0] * rows, rows)
    pairs = [
        (w_qkv.at[layer, :, : 2 * width], w_all.at[0, own, :]),
        (w_qkv.at[layer, :, 2 * width :], w_all.at[1, own, :width]),
        (w_proj.at[layer], w_all.at[1, own, width:]),
    ]
    return pairs + piece_pairs(idx, rows, offset, 2 * width, near, far, w_all)


def mlp_pairs(idx, layer, rows, offset, w_fc1, w_fc2, near, far, w_all):
    width = w_fc2.shape[-1]
    hidden = w_fc1.shape[-1]
    own = block_at(idx[0] * rows, rows)
    pairs = [(w_fc1.at[layer], w_all.at[0, own, :])]
    for part in range(hidden // width):
        pairs.append(
            (
                w_fc2.at[layer, part * rows : (part + 1) * rows, :],
                w_all.at[1, own, part * width : (part + 1) * width],
            )
        )
    return pairs + piece_pairs(idx, rows, offset, hidden, near, far, w_all)


def piece_pairs(idx, rows, offset, wide, near, far, w_all):
    pairs = []
    shards = w_all.shape[1] // rows
    for pieces, core in ((near, idx[2]), (far, 1 - idx[2])):
        for slot, piece in enumerate(pieces):
            if shards != 4:
                mask, halves = slot + 1, [(core, 0)]
            elif slot == 0:
                mask, halves = 1 + core, [(0, 0), (1, piece.shape[1] // 2)]
            else:
                mask, halves = 3, [(core, 0)]
            place = block_at(jnp.bitwise_xor(idx[0], mask) * rows, rows)
            for half, first in halves:
                at = first + offset
                pairs.append((piece.at[:, at : at + wide], w_all.at[half, place, :]))
    return pairs


def grad_pairs(idx, rows, shards, grad_all, keep, send):
    pairs = []
    for slot in range(shards):
        for target, core in ((keep, idx[2]), (send, 1 - idx[2])):
            mask = peer_order(shards, core)[slot]
            place = block_at(jnp.bitwise_xor(idx[0], mask) * rows, rows)
            pairs.append((grad_all.at[core, place, :], target.at[slot]))
    return pairs


def fc2_chunk(w_all, rows, chunk):
    width = w_all.shape[1]
    parts = w_all.shape[2] // width
    blocks = []
    for number in range(chunk * width // rows, (chunk + 1) * width // rows):
        at, part = number // parts, number % parts
        blocks.append(w_all[1, at * rows : (at + 1) * rows, part * width : (part + 1) * width])
    return jnp.concatenate(blocks, axis=0)


def attention_forward(layer, rows, offset, shards, *refs):
    peers = piece_count(shards)
    idx, stream, mod_all, w_qkv, w_proj = refs[:5]
    near, far = refs[5 : 5 + peers], refs[5 + peers : 5 + 2 * peers]
    qkv_out, probs_out, attended_out, branch_out, middle_out, w_all, sems = refs[5 + 2 * peers :]
    mod = mod_all.at[layer : layer + 1]
    copies = make_copies(
        qkv_pairs(idx, layer, rows, offset, w_qkv, w_proj, near, far, w_all), sems
    )
    start_all(copies)
    width = stream.shape[-1]
    head = width // HEADS
    b_qv, b_proj = mod[:, 6 * width : 8 * width], mod[:, 8 * width : 9 * width]
    values = stream[...].astype(F32)
    shift, scale, gate = (mod[:, part * width : (part + 1) * width] for part in range(3))
    normed, _ = layer_norm(values)
    h_one = (normed * (1.0 + scale) + shift).astype(BF)
    wait_all(copies)
    mixed = dot(h_one, w_all[0])
    qkv_out[:, :width] = (mixed[:, :width] + b_qv[:, :width]).astype(BF)
    qkv_out[:, width : 2 * width] = mixed[:, width:].astype(BF)
    qkv_out[:, 2 * width :] = (dot(h_one, w_all[1, :, :width]) + b_qv[:, width:]).astype(BF)
    lane = lax.broadcasted_iota(jnp.int32, (1, 2 * head), 1)
    masks = [(lane < head).astype(BF), (lane >= head).astype(BF)]
    for pair in range(HEADS // 2):
        at = pair * 2 * head
        queries = qkv_out[:, at : at + 2 * head]
        keys = qkv_out[:, width + at : width + at + 2 * head]
        vals = qkv_out[:, 2 * width + at : 2 * width + at + 2 * head]
        attended = 0.0
        for side in range(2):
            scores = dot_nt(queries, keys * masks[side]) * head ** (-0.5)
            raised = jnp.exp(scores - jnp.max(scores, axis=-1, keepdims=True))
            probs = raised * (1.0 / jnp.sum(raised, axis=-1, keepdims=True))
            probs_out[2 * pair + side] = probs
            attended = attended + dot(probs.astype(BF), vals * masks[side])
        attended_out[:, at : at + 2 * head] = attended.astype(BF)
    branch = dot(attended_out[...], w_all[1, :, width:]) + b_proj
    branch_out[...] = branch
    middle_out[...] = values + gate * branch


def attention_backward(layer, rows, offset, shards, *refs):
    peers = piece_count(shards)
    idx, stream, mod_all, d_middle_in, qkv, probs_in, attended, branch, w_qkv, w_proj = refs[:10]
    near, far = refs[10 : 10 + peers], refs[10 + peers : 10 + 2 * peers]
    d_stream, vec, keep, send, w_all, d_qkv, grad_all, sems, out_sems = refs[10 + 2 * peers :]
    mod = mod_all.at[layer : layer + 1]
    copies = make_copies(
        qkv_pairs(idx, layer, rows, offset, w_qkv, w_proj, near, far, w_all), sems
    )
    start_all(copies)
    width = stream.shape[-1]
    head = width // HEADS
    root = head ** (-0.5)
    shift, scale, gate = (mod[:, part * width : (part + 1) * width] for part in range(3))
    normed, inverse = layer_norm(stream[...].astype(F32))
    h_one = (normed * (1.0 + scale) + shift).astype(BF)
    d_middle = d_middle_in[...]
    vec[:, 2 * width : 3 * width] = col_sum(d_middle * branch[...])
    d_branch = (d_middle * gate).astype(BF)
    grad_all[1, :, width:] = dot_tn(attended[...], d_branch).astype(BF)
    vec[:, 5 * width :] = col_sum(d_branch.astype(F32))
    wait_all(copies)
    d_attended = dot_nt(d_branch, w_all[1, :, width:]).astype(BF)
    lane = lax.broadcasted_iota(jnp.int32, (1, 2 * head), 1)
    masks = [(lane < head).astype(BF), (lane >= head).astype(BF)]
    for pair in range(HEADS // 2):
        at = pair * 2 * head
        queries = qkv[:, at : at + 2 * head]
        keys = qkv[:, width + at : width + at + 2 * head]
        vals = qkv[:, 2 * width + at : 2 * width + at + 2 * head]
        d_att = d_attended[:, at : at + 2 * head]
        d_queries, d_keys, d_values = 0.0, 0.0, 0.0
        for side in range(2):
            probs = probs_in[2 * pair + side]
            d_values = d_values + dot_tn(probs.astype(BF), d_att * masks[side])
            d_probs = dot_nt(d_att, vals * masks[side])
            inner = jnp.sum(probs * d_probs, axis=-1, keepdims=True)
            d_scores = (probs * (d_probs - inner)).astype(BF)
            d_queries = d_queries + dot(d_scores, keys * masks[side])
            d_keys = d_keys + dot_tn(d_scores, queries * masks[side])
        d_qkv[:, at : at + 2 * head] = (d_queries * root).astype(BF)
        d_qkv[:, width + at : width + at + 2 * head] = (d_keys * root).astype(BF)
        d_qkv[:, 2 * width + at : 2 * width + at + 2 * head] = d_values.astype(BF)
    d_qk, d_val = d_qkv[:, : 2 * width], d_qkv[:, 2 * width :]
    grad_all[0] = dot_tn(h_one, d_qk).astype(BF)
    grad_all[1, :, :width] = dot_tn(h_one, d_val).astype(BF)
    out_copies = make_copies(grad_pairs(idx, rows, shards, grad_all, keep, send), out_sems)
    start_all(out_copies)
    vec[:, 3 * width : 4 * width] = col_sum(d_qk[:, :width].astype(F32))
    vec[:, 4 * width : 5 * width] = col_sum(d_val.astype(F32))
    d_h_one = dot_nt(d_qk, w_all[0]) + dot_nt(d_val, w_all[1, :, :width])
    vec[:, :width] = col_sum(d_h_one)
    vec[:, width : 2 * width] = col_sum(d_h_one * normed)
    d_stream[...] = d_middle + norm_back(d_h_one * (1.0 + scale), normed, inverse)
    wait_all(out_copies)


def gelu_parts(pre_act):
    root = 0.7978845608028654
    square = pre_act * pre_act
    bent = jnp.tanh(root * pre_act * (1.0 + 0.044715 * square))
    half = 0.5 * (1.0 + bent)
    slope = half + 0.5 * pre_act * (1.0 - bent * bent) * (root * (1.0 + 3 * 0.044715 * square))
    return pre_act * half, slope


def mlp_vectors(mod_all, layer, width):
    mod = mod_all.at[layer : layer + 1]
    last = mod_all.shape[-1] - width
    return mod, mod[:, 9 * width : last], mod[:, last:]


def mlp_forward_part(rows, h_two, b_fc1, b_fc2, w_all, act_low, slopes):
    width = w_all.shape[1]
    mlp_out = b_fc2
    for chunk in range(w_all.shape[2] // width):
        cols = slice(chunk * width, (chunk + 1) * width)
        act, slope = gelu_parts(dot(h_two, w_all[0, :, cols]) + b_fc1[:, cols])
        act_low[:, cols] = act.astype(BF)
        slopes[:, cols] = slope
        mlp_out = mlp_out + dot(act_low[:, cols], fc2_chunk(w_all, rows, chunk))
    return mlp_out


def mlp_backward_part(
    idx, rows, shards, grad_out, mlp_out, middle, normed, inverse, h_two, scale, gate,
    w_all, act_low, slopes, vec, d_middle_out, grad_all, keep, send, out_sems,
):
    width = w_all.shape[1]
    parts = w_all.shape[2] // width
    vec[:, 2 * width : 3 * width] = col_sum(grad_out * mlp_out)
    d_mlp = (grad_out * gate).astype(BF)
    vec[:, (3 + parts) * width :] = col_sum(d_mlp.astype(F32))
    d_h_two = 0.0
    for chunk in range(parts):
        cols = slice(chunk * width, (chunk + 1) * width)
        d_act = dot_nt(d_mlp, fc2_chunk(w_all, rows, chunk))
        d_pre = (d_act * slopes[:, cols]).astype(BF)
        vec[:, (3 + chunk) * width : (4 + chunk) * width] = col_sum(d_pre.astype(F32))
        grad_all[0, :, cols] = dot_tn(h_two, d_pre).astype(BF)
        grad_fc2 = dot_tn(act_low[:, cols], d_mlp).astype(BF)
        first = chunk * width // rows
        for number in range(first, (chunk + 1) * width // rows):
            at, part = number // parts, number % parts
            grad_all[1, at * rows : (at + 1) * rows, part * width : (part + 1) * width] = grad_fc2[
                (number - first) * rows : (number - first + 1) * rows
            ]
        d_h_two = d_h_two + dot_nt(d_pre, w_all[0, :, cols])
    out_copies = make_copies(grad_pairs(idx, rows, shards, grad_all, keep, send), out_sems)
    start_all(out_copies)
    vec[:, :width] = col_sum(d_h_two)
    vec[:, width : 2 * width] = col_sum(d_h_two * normed)
    d_middle_out[...] = grad_out + norm_back(d_h_two * (1.0 + scale), normed, inverse)
    wait_all(out_copies)


def mlp_forward(layer, rows, offset, shards, *refs):
    peers = piece_count(shards)
    idx, middle, mod_all, w_fc1, w_fc2 = refs[:5]
    near, far = refs[5 : 5 + peers], refs[5 + peers : 5 + 2 * peers]
    act_low, slopes, mlp_out, stream_out, w_all, sems = refs[5 + 2 * peers :]
    mod, b_fc1, b_fc2 = mlp_vectors(mod_all, layer, middle.shape[-1])
    copies = make_copies(mlp_pairs(idx, layer, rows, offset, w_fc1, w_fc2, near, far, w_all), sems)
    start_all(copies)
    width = middle.shape[-1]
    shift, scale, gate = (mod[:, part * width : (part + 1) * width] for part in range(3, 6))
    normed, _ = layer_norm(middle[...])
    h_two = (normed * (1.0 + scale) + shift).astype(BF)
    wait_all(copies)
    mlp_out[...] = mlp_forward_part(rows, h_two, b_fc1, b_fc2, w_all, act_low, slopes)
    stream_out[...] = middle[...] + gate * mlp_out[...]


def mlp_backward(layer, rows, offset, shards, *refs):
    peers = piece_count(shards)
    idx, middle, mod_all, grad_out, act_low, slopes, mlp_out, w_fc1, w_fc2 = refs[:9]
    near, far = refs[9 : 9 + peers], refs[9 + peers : 9 + 2 * peers]
    d_middle, vec, keep, send, w_all, grad_all, sems, out_sems = refs[9 + 2 * peers :]
    mod = mod_all.at[layer : layer + 1]
    copies = make_copies(mlp_pairs(idx, layer, rows, offset, w_fc1, w_fc2, near, far, w_all), sems)
    start_all(copies)
    width = middle.shape[-1]
    shift, scale, gate = (mod[:, part * width : (part + 1) * width] for part in range(3, 6))
    normed, inverse = layer_norm(middle[...])
    h_two = (normed * (1.0 + scale) + shift).astype(BF)
    wait_all(copies)
    mlp_backward_part(
        idx, rows, shards, grad_out[...], mlp_out[...], middle, normed, inverse, h_two, scale,
        gate, w_all, act_low, slopes, vec, d_middle, grad_all, keep, send, out_sems,
    )


def mlp_both(layer, rows, offset, shards, *refs):
    peers = piece_count(shards)
    idx, middle, mod_all, cotangent, w_fc1, w_fc2 = refs[:6]
    near, far = refs[6 : 6 + peers], refs[6 + peers : 6 + 2 * peers]
    x_out, d_middle, vec, keep, send = refs[6 + 2 * peers : 11 + 2 * peers]
    w_all, grad_all, act_low, slopes, sems, out_sems = refs[11 + 2 * peers :]
    mod, b_fc1, b_fc2 = mlp_vectors(mod_all, layer, middle.shape[-1])
    copies = make_copies(mlp_pairs(idx, layer, rows, offset, w_fc1, w_fc2, near, far, w_all), sems)
    start_all(copies)
    width = middle.shape[-1]
    shift, scale, gate = (mod[:, part * width : (part + 1) * width] for part in range(3, 6))
    normed, inverse = layer_norm(middle[...])
    h_two = (normed * (1.0 + scale) + shift).astype(BF)
    wait_all(copies)
    mlp_out = mlp_forward_part(rows, h_two, b_fc1, b_fc2, w_all, act_low, slopes)
    x_out[...] = (middle[...] + gate * mlp_out).astype(BF)
    mlp_backward_part(
        idx, rows, shards, cotangent[...].astype(F32), mlp_out, middle, normed, inverse, h_two,
        scale, gate, w_all, act_low, slopes, vec, d_middle, grad_all, keep, send, out_sems,
    )


def padded_rows(idx, w_ada, w_pad, sems):
    layers, rows, wide = w_ada.shape
    w_pad[...] = jnp.zeros(w_pad.shape, BF)
    own = block_at(idx[0] * rows, rows)
    return make_copies(
        [
            (w_ada.at[layer], w_pad.at[own, layer * wide : (layer + 1) * wide])
            for layer in range(layers)
        ],
        sems,
    )


def modulate_kernel(shards, *refs):
    idx, w_ada, b_ada = refs[:3]
    biases, conditions = refs[3:7], refs[7 : 7 + shards]
    outs = refs[7 + shards : 7 + 2 * shards]
    w_pad, sems = refs[7 + 2 * shards :]
    copies = padded_rows(idx, w_ada, w_pad, sems)
    start_all(copies)
    layers = w_ada.shape[0]
    wide = w_ada.shape[2]
    acts = []
    for ref in conditions:
        cond = ref[...].astype(F32)
        acts.append(cond / (1.0 + jnp.exp(-cond)))
    acts = jnp.concatenate(acts, axis=0).astype(BF)

    def spread(bias):
        length = bias.shape[1]
        row = lax.broadcasted_iota(jnp.int32, (length, shards * length), 0)
        col = lax.broadcasted_iota(jnp.int32, (length, shards * length), 1)
        place = jnp.where(col - row == idx[0] * length, 1.0, 0.0).astype(BF)
        return dot(bias[...], place)

    first = spread(b_ada)
    at = wide
    for bias in biases:
        full = spread(bias)
        for out in outs:
            out[:, at : at + full.shape[1]] = full
        at += full.shape[1]
    wait_all(copies)
    for layer in range(layers):
        result = dot(acts, w_pad[:, layer * wide : (layer + 1) * wide]) + first[layer : layer + 1]
        for step in range(shards):
            outs[step][layer : layer + 1, :wide] = result[step : step + 1]


def stack_kernel(first, second, out, rows_f32):
    size = first.shape[0]
    rows_f32[:size] = first[...].astype(F32)
    rows_f32[size:] = second[...].astype(F32)
    out[...] = rows_f32[...].astype(BF)


def group_kernel(idx, w_ada, first, second, keep, send, stacked, rows_f32, w_pad, sems):
    copies = padded_rows(idx, w_ada, w_pad, sems)
    start_all(copies)
    width, wide = w_pad.shape
    stack_kernel(first, second, stacked, rows_f32)
    wait_all(copies)
    result = dot_nt(stacked[:, width : width + wide], w_pad[...])
    half = keep.shape[0]
    keep[...] = result[:half]
    send[...] = result[half:]


def ada_grad_kernel(rows, wide, inverse_count, *refs):
    idx, stacks = refs[0], refs[1:-4]
    grad_ada, sums, turned, gathered_f32 = refs[-4:]
    layers = grad_ada.shape[0]
    width = turned.shape[0]
    size = stacks[0].shape[0]
    for number, stack in enumerate(stacks):
        gathered_f32[number * size : (number + 1) * size] = stack[...].astype(F32)
    gathered = gathered_f32[...].astype(BF)
    turned[...] = gathered_f32[:, :width].T
    own = turned[block_at(idx[0] * rows, rows), :].astype(BF)
    for layer in range(layers):
        at = width + layer * wide
        grad_ada[layer] = dot(own, gathered[:, at : at + wide]) * inverse_count
    sums[...] = col_sum(gathered_f32[:, width:]) * inverse_count


def core_sum_kernel(slots, count, *refs):
    keeps, recvs, outs = refs[:count], refs[count : 2 * count], refs[2 * count :]
    for (first, number), out in zip(slots, outs):
        for slot in range(number):
            at = 0
            for keep, recv in zip(keeps, recvs):
                wide = keep.shape[-1]
                total = keep[first + slot].astype(F32) + recv[first + slot].astype(F32)
                out[slot, :, at : at + wide] = total.astype(BF)
                at += wide


def split_sum_kernel(mine, other, keep, send):
    keep[...] = (mine[0].astype(F32) + other[0].astype(F32)).astype(BF)
    send[...] = (mine[1].astype(F32) + other[1].astype(F32)).astype(BF)


def row_split_kernel(*refs):
    idx, terms, keep, send, halves = refs[0], refs[1:-3], refs[-3], refs[-2], refs[-1]
    total = terms[0][...].astype(F32)
    for term in terms[1:]:
        total = total + term[...].astype(F32)
    half = halves.shape[1]
    for side in range(2):
        halves[side] = total[side * half : (side + 1) * half].astype(BF)
    mine = idx[1] % 2
    keep[...] = halves[mine]
    send[...] = halves[1 - mine]


def sum_kernel(*refs):
    total = refs[0][...].astype(F32)
    for term in refs[1:-1]:
        total = total + term[...].astype(F32)
    refs[-1][...] = total.astype(BF).reshape(refs[-1].shape)


def finish_kernel(rows, plan, factor, *refs):
    idx = refs[0]
    terms = list(refs[1 : 1 + sum(2 * parts for _, parts in plan)])
    at = 1 + len(terms)
    g_qkv, g_proj, g_fc1, g_fc2 = refs[at : at + 4]
    scratch = refs[at + 4 :]
    width = g_proj.shape[-1]
    hidden = g_fc1.shape[-1]
    for (members, parts), halves in zip(plan, scratch):
        for core in (idx[2], 1 - idx[2]):
            if parts == 1:
                halves[core] = terms.pop(0)[...]
            else:
                size = terms[0].shape[0]
                for side in (idx[1] % 2, 1 - idx[1] % 2):
                    halves[core, block_at(side * size, size), :] = terms.pop(0)[...]
        for kind, layer, skip in members:
            if kind == "qkv":
                first = halves[0, :, skip : skip + 2 * width]
                g_qkv[layer, :, : 2 * width] = first.astype(F32) * factor
                second = halves[1, :, skip : skip + 2 * width].astype(F32) * factor
                g_qkv[layer, :, 2 * width :] = second[:, :width]
                g_proj[layer] = second[:, width:]
            else:
                g_fc1[layer] = halves[0, :, skip : skip + hidden].astype(F32) * factor
                for part in range(hidden // width):
                    at = skip + part * width
                    g_fc2[layer, part * rows : (part + 1) * rows] = (
                        halves[1, :, at : at + width].astype(F32) * factor
                    )


def shards(
    latents, condition, cotangent, w_qkv, b_qv, w_proj, b_proj, w_fc1, b_fc1, w_fc2, b_fc2, w_ada,
    b_ada,
):
    layers, rows, _ = w_qkv.shape
    width = w_proj.shape[-1]
    hidden = w_fc1.shape[-1]
    wide = w_ada.shape[-1]
    seq = latents.shape[1]
    n_shard = lax.axis_size("shard")
    n_rep = lax.axis_size("rep")
    levels = n_rep // CORES
    shard_id = lax.axis_index("shard")
    rep_id = lax.axis_index("rep")
    core = rep_id % CORES
    idx = jnp.stack([shard_id, rep_id // CORES, core]).astype(jnp.int32)
    total_latents = latents.shape[0] * n_shard * n_rep
    factor = 1.0 / total_latents

    def exchange(array, by_shard=0, by_level=0, by_core=0, turn=None):
        moves = []
        for own_shard in range(n_shard):
            for own_rep in range(n_rep):
                mask = turn[own_rep % CORES] if turn else by_shard
                peer = (own_shard ^ mask) * n_rep + (own_rep ^ (by_level * CORES + by_core))
                moves.append((own_shard * n_rep + own_rep, peer))
        return lax.ppermute(array, ("shard", "rep"), moves)

    def after(array, *earlier):
        return lax.optimization_barrier((array,) + earlier)[0]

    relay = n_shard == 4
    first_turn, second_turn = (1, 2), (2, 1)

    half_wide = {"qkv": 2 * width, "mlp": hidden}
    copy_total = {"qkv": 3, "mlp": 1 + hidden // width}

    def pack(*plan):
        whole = run(
            functools.partial(pack_kernel, plan), "pack",
            [(array, "h") for array in (w_qkv, w_proj, w_fc1, w_fc2)],
            [((rows, 2 * sum(half_wide[kind] for kind in kinds)), BF, "v") for _, kinds in plan],
            [pltpu.SemaphoreType.DMA((sum(copy_total[kind] for _, ks in plan for kind in ks),))],
        )
        if relay:
            return whole
        return [
            lax.dynamic_slice_in_dim(array, core * (array.shape[1] // 2), array.shape[1] // 2, 1)
            for array in whole
        ]

    def near_first(packed):
        if relay:
            return [exchange(packed, turn=first_turn)]
        return [exchange(packed, by_shard=step) for step in range(1, n_shard)]

    def near_half(near, *earlier):
        source = after(near[0], *earlier) if earlier else near[0]
        if not relay:
            return source
        half = source.shape[1] // 2
        return run(
            half_kernel, "half", [(idx, "s"), (source, "a")],
            [((source.shape[0], half), BF, "a")], [pltpu.SemaphoreType.DMA((1,))],
        )[0]

    def near_second(near, part):
        return near + [exchange(part, turn=second_turn)] if relay else near

    def far_of(near, *earlier):
        return [exchange(after(piece, *earlier) if earlier else piece, by_core=1) for piece in near]

    conditions = [condition] + [exchange(condition, by_shard=step) for step in range(1, n_shard)]
    packed = [pack((layer, ("qkv", "mlp")))[0] for layer in range(layers)]
    near = [near_first(own) for own in packed]
    pad_scratch = [pltpu.VMEM((width, layers * wide), BF), pltpu.SemaphoreType.DMA((layers,))]
    span = wide + 4 * width + hidden
    partial = run(
        functools.partial(modulate_kernel, n_shard), "modulate",
        [(idx, "s"), (w_ada, "a"), (b_ada, "v"), (b_qv, "v"), (b_proj, "v"), (b_fc1, "v"),
         (b_fc2, "v")] + [(array, "v") for array in conditions],
        [((layers, span), F32, "v")] * n_shard, pad_scratch, flops=10**7,
    )
    parts = [near_half(near[0], partial[0])]
    for own in near[1:]:
        parts.append(near_half(own, parts[-1]))
    near = [near_second(own, part) for own, part in zip(near, parts)]
    mod_all = partial[0]
    for step in range(1, n_shard):
        mod_all = mod_all + exchange(after(partial[step], *parts[1:]), by_shard=step)
    pieces = {0: (near[0], far_of(near[0]))}

    big = seq * width
    row = lambda kind="v": ((seq, width), F32, kind)
    vec_wide = {"qkv": 6 * width, "mlp": 4 * width + hidden}

    def piece_args(pair):
        return [(array, "a") for array in pair[0] + pair[1]]

    copy_count = 6 if relay else 2 * (n_shard - 1)
    qkv_sems = pltpu.SemaphoreType.DMA((3 + copy_count,))
    mlp_sems = pltpu.SemaphoreType.DMA((1 + hidden // width + copy_count,))
    out_sems = pltpu.SemaphoreType.DMA((2 * n_shard,))
    w_qkv_all = pltpu.VMEM((2, width, 2 * width), BF)
    w_mlp_all = pltpu.VMEM((2, width, hidden), BF)

    def grads_out(kind):
        return [((n_shard, rows, half_wide[kind]), BF, "a")] * 2

    stream = latents[0]
    saved = []
    vecs, raw = {}, {}
    for layer in range(layers):
        pair, offset = pieces[layer], 0
        keep_in = "v" if layer + 1 == layers else "k"
        qkv, probs, attended, branch, middle = run(
            functools.partial(attention_forward, layer, rows, offset, n_shard), "attention_forward",
            [(idx, "s"), (stream, "v"), (mod_all, "v"), (w_qkv, "a"), (w_proj, "a")]
            + piece_args(pair),
            [((seq, 3 * width), BF, keep_in), ((HEADS, seq, seq), F32, keep_in),
             ((seq, width), BF, keep_in), row(keep_in), row()],
            [w_qkv_all, qkv_sems], flops=10 * big * width,
        )
        pair, offset = pieces[layer], 2 * width
        entry = dict(stream=stream, qkv=qkv, probs=probs, attended=attended, branch=branch,
                     middle=middle)
        if layer + 1 < layers:
            act_low, slopes, mlp_out, stream = run(
                functools.partial(mlp_forward, layer, rows, offset, n_shard), "mlp_forward",
                [(idx, "s"), (middle, "v"), (mod_all, "v"), (w_fc1, "a"), (w_fc2, "a")]
                + piece_args(pair),
                [((seq, hidden), BF, keep_in), ((seq, hidden), F32, keep_in), row(keep_in), row()],
                [w_mlp_all, mlp_sems], flops=16 * big * width,
            )
            entry.update(act_low=act_low, slopes=slopes, mlp_out=mlp_out)
            pieces[layer + 1] = (near[layer + 1], far_of(near[layer + 1], middle))
        else:
            x_out, d_middle, vecs["mlp", layer], *raw["mlp", layer] = run(
                functools.partial(mlp_both, layer, rows, offset, n_shard), "mlp_both",
                [(idx, "s"), (middle, "v"), (mod_all, "v"), (cotangent[0], "v"), (w_fc1, "a"),
                 (w_fc2, "a")] + piece_args(pair),
                [((seq, width), BF, "v"), row(), ((1, vec_wide["mlp"]), F32, "v")]
                + grads_out("mlp"),
                [w_mlp_all, w_mlp_all, pltpu.VMEM((seq, hidden), BF),
                 pltpu.VMEM((seq, hidden), F32), mlp_sems, out_sems], flops=48 * big * width,
            )
        saved.append(entry)

    def core_sum(keys, *earlier):
        keeps = [raw[key][0] for key in keys]
        received = [exchange(raw[key][1], by_core=1) for key in keys]
        if earlier:
            keeps[0] = after(keeps[0], *earlier)
        total_wide = sum(keep.shape[-1] for keep in keeps)
        slots = [(0, 2), (2, 2)] if relay else [(slot, 1) for slot in range(n_shard)]
        return run(
            functools.partial(core_sum_kernel, slots, len(keys)), "core_sum",
            [(array, "v") for array in keeps + received],
            [((number, rows, total_wide), BF, "v") for _, number in slots],
        )

    def shard_send(summed):
        if relay:
            return [exchange(summed[1], turn=first_turn)]
        return [exchange(summed[step], by_shard=step) for step in range(1, n_shard)]

    def add(terms, shape):
        return run(sum_kernel, "add", [(array, "v") for array in terms], [(shape, BF, "v")])[0]

    def shard_second(summed, arrived, *earlier):
        shape = summed[0].shape[1:]
        mine = after(summed[0], *earlier) if earlier else summed[0]
        if not relay:
            return [mine.reshape(shape)] + [array.reshape(shape) for array in arrived]
        keep, send = run(
            split_sum_kernel, "split_sum", [(mine, "v"), (arrived[0], "v")], [(shape, BF, "v")] * 2
        )
        return [keep, exchange(send, turn=second_turn)]

    def level_first(terms, halve, *earlier):
        shape = terms[0].shape
        if earlier:
            terms = [after(terms[0], *earlier)] + terms[1:]
        if not halve or shape[0] % 32:
            total = add(terms, shape)
            return False, total, exchange(total, by_level=1)
        part = (shape[0] // 2, shape[1])
        keep, send = run(
            row_split_kernel, "row_split",
            [(idx, "s")] + [(array, "v") for array in terms],
            [(part, BF, "v")] * 2, [pltpu.VMEM((2,) + part, BF)],
        )
        return True, keep, exchange(send, by_level=1)

    def level_second(first, *earlier):
        halved, kept, arriving = first
        if earlier:
            kept = after(kept, *earlier)
        return halved, add([kept, arriving], kept.shape)

    def level_last(halved, total, step):
        while step < levels:
            total = add([total, exchange(total, by_level=step)], total.shape)
            step *= 2
        near = [total, exchange(total, by_level=1)] if halved else [total]
        return near + far_of(near)

    waiting = []
    for layer in reversed(range(layers)):
        entry = saved[layer]
        pair, offset = pieces[layer], 2 * width
        if layer + 1 < layers:
            keys = [("qkv", layer + 1), ("mlp", layer + 1)]
            summed = core_sum(keys, grad_stream)
            waiting.append((keys, summed, shard_send(summed)))
            grad_stream = after(grad_stream, summed[0])
            d_middle, vecs["mlp", layer], *raw["mlp", layer] = run(
                functools.partial(mlp_backward, layer, rows, offset, n_shard), "mlp_backward",
                [(idx, "s"), (entry["middle"], "v"), (mod_all, "v"), (grad_stream, "v"),
                 (entry["act_low"], "v"), (entry["slopes"], "v"), (entry["mlp_out"], "v"),
                 (w_fc1, "a"), (w_fc2, "a")] + piece_args(pair),
                [row(), ((1, vec_wide["mlp"]), F32, "v")] + grads_out("mlp"),
                [w_mlp_all, w_mlp_all, mlp_sems, out_sems], flops=32 * big * width,
            )
            core_mlp = core_sum([("mlp", layer)], d_middle)
            sent_mlp = shard_send(core_mlp)
            d_middle = after(d_middle, core_mlp[0])
        pair, offset = pieces[layer], 0
        grad_stream, vecs["qkv", layer], *raw["qkv", layer] = run(
            functools.partial(attention_backward, layer, rows, offset, n_shard),
            "attention_backward",
            [(idx, "s"), (entry["stream"], "v"), (mod_all, "v"), (d_middle, "v"),
             (entry["qkv"], "v"), (entry["probs"], "v"), (entry["attended"], "v"),
             (entry["branch"], "v"), (w_qkv, "a"), (w_proj, "a")] + piece_args(pair),
            [row(), ((1, vec_wide["qkv"]), F32, "v")] + grads_out("qkv"),
            [w_qkv_all, pltpu.VMEM((seq, 3 * width), BF), w_qkv_all, qkv_sems, out_sems],
            flops=28 * big * width,
        )
    cond_in = condition.astype(F32)
    vector = [jax.nn.silu(cond_in).astype(BF)]
    for layer in range(layers):
        vector += [vecs[kind, layer][:, : 3 * width].astype(BF) for kind in ("qkv", "mlp")]
    for layer in range(layers):
        vector += [vecs[kind, layer][:, 3 * width :].astype(BF) for kind in ("qkv", "mlp")]
    vector = jnp.concatenate(vector, axis=1)
    length = vector.shape[1]
    masks = [first_turn, second_turn] if relay else []
    while not relay and 2 ** len(masks) < n_shard:
        masks.append((2 ** len(masks),) * 2)

    def stack(first, second):
        shape = (2 * first.shape[0], length)
        return run(
            stack_kernel, "stack", [(first, "v"), (second, "v")], [(shape, BF, "v")],
            [pltpu.VMEM(shape, F32)],
        )[0]

    (keys_first, core_first, sent_first), = waiting
    plan = [keys_first, [("mlp", 0)], [("qkv", 0)]]
    a = shard_second(core_first, sent_first, grad_stream)
    vector = after(vector, a[0])
    for mask in masks[:-2]:
        vector = stack(vector, exchange(vector, turn=mask))
    arriving = exchange(vector, turn=masks[-2])
    core_qkv = core_sum(plan[2], vector)
    sent_qkv = shard_send(core_qkv)
    b = shard_second(core_mlp, sent_mlp, core_qkv[0])
    vector = after(vector, b[0])
    vector = stack(after(vector, core_qkv[0]), arriving)
    arriving = exchange(vector, turn=masks[-1])
    a = level_first(a, True, vector)
    grad_cond, passed, stacked = run(
        group_kernel, "group",
        [(idx, "s"), (w_ada, "a"), (after(vector, a[1]), "v"), (arriving, "v")],
        [((n_shard // 2, width), F32, "v")] * 2 + [((n_shard, length), BF, "v")],
        [pltpu.VMEM((n_shard, length), F32)] + pad_scratch, flops=10**7,
    )
    arriving = exchange(stacked, by_level=1)
    c = shard_second(core_qkv, sent_qkv, stacked)
    a = level_second(a, c[0])
    a_moving = exchange(a[1], by_level=2)
    b = level_first(b, True, a[1])
    stacked = stack(after(stacked, b[1]), arriving)
    step = 2
    while 2 * step < levels:
        stacked = stack(stacked, exchange(stacked, by_level=step))
        step *= 2
    arriving = exchange(stacked, by_level=step)
    c = level_first(c, False, stacked)
    a = (a[0], add([after(a[1], c[1]), a_moving], a[1].shape))
    a_parts = level_last(*a, 4)
    b = level_second(b, a[1])
    b_moving = exchange(b[1], by_level=2)
    c = level_second(c, b[1])
    c_moving = exchange(c[1], by_level=2)
    grad_cond = grad_cond + exchange(passed, turn=masks[-1])
    for mask in masks[-2::-1]:
        half = grad_cond.shape[0] // 2
        grad_cond = grad_cond[:half] + exchange(grad_cond[half:], turn=mask)
    cond_grad = jax.vjp(jax.nn.silu, cond_in)[1](grad_cond)[0]
    stacks = [after(stacked, c[1]), arriving]
    stacks = stacks + far_of(stacks)
    grad_ada, sums = run(
        functools.partial(ada_grad_kernel, rows, wide, factor), "ada_grad",
        [(idx, "s")] + [(array, "v") for array in stacks],
        [((layers, rows, wide), F32, "v"), ((1, length - width), F32, "v")],
        [pltpu.VMEM((width, total_latents), F32), pltpu.VMEM((total_latents, length), F32)],
        flops=10**8,
    )

    b = (b[0], add([after(b[1], sums), b_moving], b[1].shape))
    b_parts = level_last(*b, 4)
    c = (c[0], add([after(c[1], b[1]), c_moving], c[1].shape))
    finals = [a_parts, b_parts, level_last(*c, 4)]

    def own_part(parts):
        whole = jnp.concatenate(parts, axis=0)
        length = whole.shape[1] // n_shard
        return lax.dynamic_slice_in_dim(whole, shard_id * length, length, axis=1)

    base = layers * wide
    at = [base + layer * (4 * width + hidden) for layer in range(layers)]
    grad_ada_bias = own_part([sums[:, layer * wide : (layer + 1) * wide] for layer in range(layers)])
    grad_qv_bias = own_part([sums[:, a : a + 2 * width] for a in at])
    grad_proj_bias = own_part([sums[:, a + 2 * width : a + 3 * width] for a in at])
    grad_fc1_bias = own_part([sums[:, a + 3 * width : a + 3 * width + hidden] for a in at])
    grad_fc2_bias = own_part([sums[:, a + 3 * width + hidden : a + 4 * width + hidden] for a in at])

    finish_plan, finish_inputs, finish_scratch = [], [(idx, "s")], []
    for keys, parts in zip(plan, finals):
        members, skip = [], 0
        for kind, layer in keys:
            members.append((kind, layer, skip))
            skip += half_wide[kind]
        finish_plan.append((members, len(parts) // 2))
        finish_inputs += [(array, "v") for array in parts]
        finish_scratch.append(pltpu.VMEM((2, rows, skip), BF))
    grad_qkv, grad_proj, grad_fc1, grad_fc2 = run(
        functools.partial(finish_kernel, rows, finish_plan, factor), "finish",
        finish_inputs,
        [(array.shape, F32, "v") for array in (w_qkv, w_proj, w_fc1, w_fc2)],
        finish_scratch,
    )
    return (
        x_out[None], grad_stream[None], cond_grad, grad_qkv, grad_qv_bias, grad_proj,
        grad_proj_bias, grad_fc1, grad_fc1_bias, grad_fc2, grad_fc2_bias, grad_ada, grad_ada_bias,
    )


def solution(mesh):
    rows3, rows2 = P(("shard", "rep"), None, None), P(("shard", "rep"), None)
    weight, bias = P(None, "shard", None), P(None, "shard")
    return jax.shard_map(
        shards,
        mesh=mesh,
        in_specs=(rows3, rows2, rows3) + (weight, bias) * 5,
        out_specs=(rows3, rows3, rows2) + (weight, bias) * 5,
        check_vma=False,
    )
```

```python
import functools

import jax
import jax.numpy as jnp
from jax import lax
from jax.experimental import pallas as pl
from jax.experimental.pallas import tpu as pltpu
from jax.sharding import PartitionSpec as P

HEADS = 6
BF = jnp.bfloat16
F32 = jnp.float32
CORES = 2
VMEM_LIMIT = 40 * 1024 * 1024


def dot(left, right):
    return jnp.dot(left, right, preferred_element_type=F32)


def dot_nt(left, right):
    return lax.dot_general(left, right, (((1,), (1,)), ((), ())), preferred_element_type=F32)


def dot_tn(left, right):
    return lax.dot_general(left, right, (((0,), (0,)), ((), ())), preferred_element_type=F32)


def layer_norm(rows):
    center = rows - jnp.mean(rows, axis=-1, keepdims=True)
    inverse = lax.rsqrt(jnp.mean(center * center, axis=-1, keepdims=True) + 1e-06)
    return center * inverse, inverse


def norm_back(grad_norm, normed, inverse):
    centered = grad_norm - jnp.mean(grad_norm, axis=-1, keepdims=True)
    return inverse * (centered - normed * jnp.mean(grad_norm * normed, axis=-1, keepdims=True))


def col_sum(rows):
    return jnp.sum(rows, axis=0, keepdims=True)


def block_at(start, size):
    return pl.ds(pl.multiple_of(start, size), size)


def start_all(copies):
    for copy in copies:
        copy.start()


def wait_all(copies):
    for copy in copies:
        copy.wait()


def make_copies(pairs, sems):
    return [
        pltpu.make_async_copy(source, target, sems.at[slot])
        for slot, (source, target) in enumerate(pairs)
    ]


def run(body, name, inputs, outputs, scratch=(), flops=0):
    places = {"v": pltpu.VMEM, "k": pltpu.VMEM, "a": pl.ANY, "h": pl.ANY, "s": pltpu.SMEM}
    arrays = [
        pltpu.with_memory_space_constraint(arr, pltpu.HBM) if kind in "hk" else arr
        for arr, kind in inputs
    ]
    return pl.pallas_call(
        body,
        out_shape=[
            pltpu.HBM(shape, dtype) if kind in "hk" else jax.ShapeDtypeStruct(shape, dtype)
            for shape, dtype, kind in outputs
        ],
        in_specs=[pl.BlockSpec(memory_space=places[kind]) for _, kind in inputs],
        out_specs=[pl.BlockSpec(memory_space=places[kind]) for _, _, kind in outputs],
        scratch_shapes=list(scratch),
        compiler_params=pltpu.CompilerParams(vmem_limit_bytes=VMEM_LIMIT),
        cost_estimate=pl.CostEstimate(flops=1, bytes_accessed=1, transcendentals=0),
        name=name,
    )(*arrays)


def pack_kernel(plan, *refs):
    w_qkv, w_proj, w_fc1, w_fc2 = refs[:4]
    outs, sems = refs[4:-1], refs[-1]
    rows, width = w_proj.shape[1:]
    hidden = w_fc1.shape[-1]
    pairs = []
    for (layer, kinds), out in zip(plan, outs):
        at = 0
        pieces = {"qkv": [w_qkv.at[layer, :, : 2 * width]], "mlp": [w_fc1.at[layer]]}
        second = {
            "qkv": [w_qkv.at[layer, :, 2 * width :], w_proj.at[layer]],
            "mlp": [
                w_fc2.at[layer, part * rows : (part + 1) * rows]
                for part in range(hidden // width)
            ],
        }
        for half in (pieces, second):
            for kind in kinds:
                for piece in half[kind]:
                    pairs.append((piece, out.at[:, at : at + piece.shape[-1]]))
                    at += piece.shape[-1]
    copies = make_copies(pairs, sems)
    start_all(copies)
    wait_all(copies)


def half_kernel(idx, whole, out, sems):
    half = out.shape[1]
    copies = make_copies([(whole.at[:, block_at(idx[2] * half, half)], out)], sems)
    start_all(copies)
    wait_all(copies)


def piece_count(shards):
    return 2 if shards == 4 else shards - 1


def peer_order(shards, core):
    if shards != 4:
        return list(range(shards))
    return [0, 2 - core, 1 + core, 3]


def qkv_pairs(idx, layer, rows, offset, w_qkv, w_proj, near, far, w_all):
    width = w_proj.shape[-1]
    own = block_at(idx[0] * rows, rows)
    pairs = [
        (w_qkv.at[layer, :, : 2 * width], w_all.at[0, own, :]),
        (w_qkv.at[layer, :, 2 * width :], w_all.at[1, own, :width]),
        (w_proj.at[layer], w_all.at[1, own, width:]),
    ]
    return pairs + piece_pairs(idx, rows, offset, 2 * width, near, far, w_all)


def mlp_pairs(idx, layer, rows, offset, w_fc1, w_fc2, near, far, w_all):
    width = w_fc2.shape[-1]
    hidden = w_fc1.shape[-1]
    own = block_at(idx[0] * rows, rows)
    pairs = [(w_fc1.at[layer], w_all.at[0, own, :])]
    for part in range(hidden // width):
        pairs.append(
            (
                w_fc2.at[layer, part * rows : (part + 1) * rows, :],
                w_all.at[1, own, part * width : (part + 1) * width],
            )
        )
    return pairs + piece_pairs(idx, rows, offset, hidden, near, far, w_all)


def piece_pairs(idx, rows, offset, wide, near, far, w_all):
    pairs = []
    shards = w_all.shape[1] // rows
    for pieces, core in ((near, idx[2]), (far, 1 - idx[2])):
        for slot, piece in enumerate(pieces):
            if shards != 4:
                mask, halves = slot + 1, [(core, 0)]
            elif slot == 0:
                mask, halves = 1 + core, [(0, 0), (1, piece.shape[1] // 2)]
            else:
                mask, halves = 3, [(core, 0)]
            place = block_at(jnp.bitwise_xor(idx[0], mask) * rows, rows)
            for half, first in halves:
                at = first + offset
                pairs.append((piece.at[:, at : at + wide], w_all.at[half, place, :]))
    return pairs


def grad_pairs(idx, rows, shards, grad_all, keep, send):
    pairs = []
    for slot in range(shards):
        for target, core in ((keep, idx[2]), (send, 1 - idx[2])):
            mask = peer_order(shards, core)[slot]
            place = block_at(jnp.bitwise_xor(idx[0], mask) * rows, rows)
            pairs.append((grad_all.at[core, place, :], target.at[slot]))
    return pairs


def fc2_chunk(w_all, rows, chunk):
    width = w_all.shape[1]
    parts = w_all.shape[2] // width
    blocks = []
    for number in range(chunk * width // rows, (chunk + 1) * width // rows):
        at, part = number // parts, number % parts
        blocks.append(w_all[1, at * rows : (at + 1) * rows, part * width : (part + 1) * width])
    return jnp.concatenate(blocks, axis=0)


def attention_forward(layer, rows, offset, shards, *refs):
    peers = piece_count(shards)
    idx, stream, mod_all, w_qkv, w_proj = refs[:5]
    near, far = refs[5 : 5 + peers], refs[5 + peers : 5 + 2 * peers]
    qkv_out, probs_out, attended_out, branch_out, middle_out, w_all, sems = refs[5 + 2 * peers :]
    mod = mod_all.at[layer : layer + 1]
    copies = make_copies(
        qkv_pairs(idx, layer, rows, offset, w_qkv, w_proj, near, far, w_all), sems
    )
    start_all(copies)
    width = stream.shape[-1]
    head = width // HEADS
    b_qv, b_proj = mod[:, 6 * width : 8 * width], mod[:, 8 * width : 9 * width]
    values = stream[...].astype(F32)
    shift, scale, gate = (mod[:, part * width : (part + 1) * width] for part in range(3))
    normed, _ = layer_norm(values)
    h_one = (normed * (1.0 + scale) + shift).astype(BF)
    wait_all(copies)
    mixed = dot(h_one, w_all[0])
    qkv_out[:, :width] = (mixed[:, :width] + b_qv[:, :width]).astype(BF)
    qkv_out[:, width : 2 * width] = mixed[:, width:].astype(BF)
    qkv_out[:, 2 * width :] = (dot(h_one, w_all[1, :, :width]) + b_qv[:, width:]).astype(BF)
    lane = lax.broadcasted_iota(jnp.int32, (1, 2 * head), 1)
    masks = [(lane < head).astype(BF), (lane >= head).astype(BF)]
    for pair in range(HEADS // 2):
        at = pair * 2 * head
        queries = qkv_out[:, at : at + 2 * head]
        keys = qkv_out[:, width + at : width + at + 2 * head]
        vals = qkv_out[:, 2 * width + at : 2 * width + at + 2 * head]
        attended = 0.0
        for side in range(2):
            scores = dot_nt(queries, keys * masks[side]) * head ** (-0.5)
            raised = jnp.exp(scores - jnp.max(scores, axis=-1, keepdims=True))
            probs = raised * (1.0 / jnp.sum(raised, axis=-1, keepdims=True))
            probs_out[2 * pair + side] = probs
            attended = attended + dot(probs.astype(BF), vals * masks[side])
        attended_out[:, at : at + 2 * head] = attended.astype(BF)
    branch = dot(attended_out[...], w_all[1, :, width:]) + b_proj
    branch_out[...] = branch
    middle_out[...] = values + gate * branch


def attention_backward(layer, rows, offset, shards, *refs):
    peers = piece_count(shards)
    idx, stream, mod_all, d_middle_in, qkv, probs_in, attended, branch, w_qkv, w_proj = refs[:10]
    near, far = refs[10 : 10 + peers], refs[10 + peers : 10 + 2 * peers]
    d_stream, vec, keep, send, w_all, d_qkv, grad_all, sems, out_sems = refs[10 + 2 * peers :]
    mod = mod_all.at[layer : layer + 1]
    copies = make_copies(
        qkv_pairs(idx, layer, rows, offset, w_qkv, w_proj, near, far, w_all), sems
    )
    start_all(copies)
    width = stream.shape[-1]
    head = width // HEADS
    root = head ** (-0.5)
    shift, scale, gate = (mod[:, part * width : (part + 1) * width] for part in range(3))
    normed, inverse = layer_norm(stream[...].astype(F32))
    h_one = (normed * (1.0 + scale) + shift).astype(BF)
    d_middle = d_middle_in[...]
    vec[:, 2 * width : 3 * width] = col_sum(d_middle * branch[...])
    d_branch = (d_middle * gate).astype(BF)
    grad_all[1, :, width:] = dot_tn(attended[...], d_branch).astype(BF)
    vec[:, 5 * width :] = col_sum(d_branch.astype(F32))
    wait_all(copies)
    d_attended = dot_nt(d_branch, w_all[1, :, width:]).astype(BF)
    lane = lax.broadcasted_iota(jnp.int32, (1, 2 * head), 1)
    masks = [(lane < head).astype(BF), (lane >= head).astype(BF)]
    for pair in range(HEADS // 2):
        at = pair * 2 * head
        queries = qkv[:, at : at + 2 * head]
        keys = qkv[:, width + at : width + at + 2 * head]
        vals = qkv[:, 2 * width + at : 2 * width + at + 2 * head]
        d_att = d_attended[:, at : at + 2 * head]
        d_queries, d_keys, d_values = 0.0, 0.0, 0.0
        for side in range(2):
            probs = probs_in[2 * pair + side]
            d_values = d_values + dot_tn(probs.astype(BF), d_att * masks[side])
            d_probs = dot_nt(d_att, vals * masks[side])
            inner = jnp.sum(probs * d_probs, axis=-1, keepdims=True)
            d_scores = (probs * (d_probs - inner)).astype(BF)
            d_queries = d_queries + dot(d_scores, keys * masks[side])
            d_keys = d_keys + dot_tn(d_scores, queries * masks[side])
        d_qkv[:, at : at + 2 * head] = (d_queries * root).astype(BF)
        d_qkv[:, width + at : width + at + 2 * head] = (d_keys * root).astype(BF)
        d_qkv[:, 2 * width + at : 2 * width + at + 2 * head] = d_values.astype(BF)
    d_qk, d_val = d_qkv[:, : 2 * width], d_qkv[:, 2 * width :]
    grad_all[0] = dot_tn(h_one, d_qk).astype(BF)
    grad_all[1, :, :width] = dot_tn(h_one, d_val).astype(BF)
    out_copies = make_copies(grad_pairs(idx, rows, shards, grad_all, keep, send), out_sems)
    start_all(out_copies)
    vec[:, 3 * width : 4 * width] = col_sum(d_qk[:, :width].astype(F32))
    vec[:, 4 * width : 5 * width] = col_sum(d_val.astype(F32))
    d_h_one = dot_nt(d_qk, w_all[0]) + dot_nt(d_val, w_all[1, :, :width])
    vec[:, :width] = col_sum(d_h_one)
    vec[:, width : 2 * width] = col_sum(d_h_one * normed)
    d_stream[...] = d_middle + norm_back(d_h_one * (1.0 + scale), normed, inverse)
    wait_all(out_copies)


def gelu_parts(pre_act):
    root = 0.7978845608028654
    square = pre_act * pre_act
    bent = jnp.tanh(root * pre_act * (1.0 + 0.044715 * square))
    half = 0.5 * (1.0 + bent)
    slope = half + 0.5 * pre_act * (1.0 - bent * bent) * (root * (1.0 + 3 * 0.044715 * square))
    return pre_act * half, slope


def mlp_vectors(mod_all, layer, width):
    mod = mod_all.at[layer : layer + 1]
    last = mod_all.shape[-1] - width
    return mod, mod[:, 9 * width : last], mod[:, last:]


def mlp_forward_part(rows, h_two, b_fc1, b_fc2, w_all, act_low, slopes):
    width = w_all.shape[1]
    mlp_out = b_fc2
    for chunk in range(w_all.shape[2] // width):
        cols = slice(chunk * width, (chunk + 1) * width)
        act, slope = gelu_parts(dot(h_two, w_all[0, :, cols]) + b_fc1[:, cols])
        act_low[:, cols] = act.astype(BF)
        slopes[:, cols] = slope
        mlp_out = mlp_out + dot(act_low[:, cols], fc2_chunk(w_all, rows, chunk))
    return mlp_out


def mlp_backward_part(
    idx, rows, shards, grad_out, mlp_out, middle, normed, inverse, h_two, scale, gate,
    w_all, act_low, slopes, vec, d_middle_out, grad_all, keep, send, out_sems,
):
    width = w_all.shape[1]
    parts = w_all.shape[2] // width
    vec[:, 2 * width : 3 * width] = col_sum(grad_out * mlp_out)
    d_mlp = (grad_out * gate).astype(BF)
    vec[:, (3 + parts) * width :] = col_sum(d_mlp.astype(F32))
    d_h_two = 0.0
    for chunk in range(parts):
        cols = slice(chunk * width, (chunk + 1) * width)
        d_act = dot_nt(d_mlp, fc2_chunk(w_all, rows, chunk))
        d_pre = (d_act * slopes[:, cols]).astype(BF)
        vec[:, (3 + chunk) * width : (4 + chunk) * width] = col_sum(d_pre.astype(F32))
        grad_all[0, :, cols] = dot_tn(h_two, d_pre).astype(BF)
        grad_fc2 = dot_tn(act_low[:, cols], d_mlp).astype(BF)
        first = chunk * width // rows
        for number in range(first, (chunk + 1) * width // rows):
            at, part = number // parts, number % parts
            grad_all[1, at * rows : (at + 1) * rows, part * width : (part + 1) * width] = grad_fc2[
                (number - first) * rows : (number - first + 1) * rows
            ]
        d_h_two = d_h_two + dot_nt(d_pre, w_all[0, :, cols])
    out_copies = make_copies(grad_pairs(idx, rows, shards, grad_all, keep, send), out_sems)
    start_all(out_copies)
    vec[:, :width] = col_sum(d_h_two)
    vec[:, width : 2 * width] = col_sum(d_h_two * normed)
    d_middle_out[...] = grad_out + norm_back(d_h_two * (1.0 + scale), normed, inverse)
    wait_all(out_copies)


def mlp_forward(layer, rows, offset, shards, *refs):
    peers = piece_count(shards)
    idx, middle, mod_all, w_fc1, w_fc2 = refs[:5]
    near, far = refs[5 : 5 + peers], refs[5 + peers : 5 + 2 * peers]
    act_low, slopes, mlp_out, stream_out, w_all, sems = refs[5 + 2 * peers :]
    mod, b_fc1, b_fc2 = mlp_vectors(mod_all, layer, middle.shape[-1])
    copies = make_copies(mlp_pairs(idx, layer, rows, offset, w_fc1, w_fc2, near, far, w_all), sems)
    start_all(copies)
    width = middle.shape[-1]
    shift, scale, gate = (mod[:, part * width : (part + 1) * width] for part in range(3, 6))
    normed, _ = layer_norm(middle[...])
    h_two = (normed * (1.0 + scale) + shift).astype(BF)
    wait_all(copies)
    mlp_out[...] = mlp_forward_part(rows, h_two, b_fc1, b_fc2, w_all, act_low, slopes)
    stream_out[...] = middle[...] + gate * mlp_out[...]


def mlp_backward(layer, rows, offset, shards, *refs):
    peers = piece_count(shards)
    idx, middle, mod_all, grad_out, act_low, slopes, mlp_out, w_fc1, w_fc2 = refs[:9]
    near, far = refs[9 : 9 + peers], refs[9 + peers : 9 + 2 * peers]
    d_middle, vec, keep, send, w_all, grad_all, sems, out_sems = refs[9 + 2 * peers :]
    mod = mod_all.at[layer : layer + 1]
    copies = make_copies(mlp_pairs(idx, layer, rows, offset, w_fc1, w_fc2, near, far, w_all), sems)
    start_all(copies)
    width = middle.shape[-1]
    shift, scale, gate = (mod[:, part * width : (part + 1) * width] for part in range(3, 6))
    normed, inverse = layer_norm(middle[...])
    h_two = (normed * (1.0 + scale) + shift).astype(BF)
    wait_all(copies)
    mlp_backward_part(
        idx, rows, shards, grad_out[...], mlp_out[...], middle, normed, inverse, h_two, scale,
        gate, w_all, act_low, slopes, vec, d_middle, grad_all, keep, send, out_sems,
    )


def mlp_both(layer, rows, offset, shards, *refs):
    peers = piece_count(shards)
    idx, middle, mod_all, cotangent, w_fc1, w_fc2 = refs[:6]
    near, far = refs[6 : 6 + peers], refs[6 + peers : 6 + 2 * peers]
    x_out, d_middle, vec, keep, send = refs[6 + 2 * peers : 11 + 2 * peers]
    w_all, grad_all, act_low, slopes, sems, out_sems = refs[11 + 2 * peers :]
    mod, b_fc1, b_fc2 = mlp_vectors(mod_all, layer, middle.shape[-1])
    copies = make_copies(mlp_pairs(idx, layer, rows, offset, w_fc1, w_fc2, near, far, w_all), sems)
    start_all(copies)
    width = middle.shape[-1]
    shift, scale, gate = (mod[:, part * width : (part + 1) * width] for part in range(3, 6))
    normed, inverse = layer_norm(middle[...])
    h_two = (normed * (1.0 + scale) + shift).astype(BF)
    wait_all(copies)
    mlp_out = mlp_forward_part(rows, h_two, b_fc1, b_fc2, w_all, act_low, slopes)
    x_out[...] = (middle[...] + gate * mlp_out).astype(BF)
    mlp_backward_part(
        idx, rows, shards, cotangent[...].astype(F32), mlp_out, middle, normed, inverse, h_two,
        scale, gate, w_all, act_low, slopes, vec, d_middle, grad_all, keep, send, out_sems,
    )


def padded_rows(idx, w_ada, w_pad, sems):
    layers, rows, wide = w_ada.shape
    w_pad[...] = jnp.zeros(w_pad.shape, BF)
    own = block_at(idx[0] * rows, rows)
    return make_copies(
        [
            (w_ada.at[layer], w_pad.at[own, layer * wide : (layer + 1) * wide])
            for layer in range(layers)
        ],
        sems,
    )


def modulate_kernel(shards, *refs):
    idx, w_ada, b_ada = refs[:3]
    biases, conditions = refs[3:7], refs[7 : 7 + shards]
    outs = refs[7 + shards : 7 + 2 * shards]
    w_pad, sems = refs[7 + 2 * shards :]
    copies = padded_rows(idx, w_ada, w_pad, sems)
    start_all(copies)
    layers = w_ada.shape[0]
    wide = w_ada.shape[2]
    acts = []
    for ref in conditions:
        cond = ref[...].astype(F32)
        acts.append(cond / (1.0 + jnp.exp(-cond)))
    acts = jnp.concatenate(acts, axis=0).astype(BF)

    def spread(bias):
        length = bias.shape[1]
        row = lax.broadcasted_iota(jnp.int32, (length, shards * length), 0)
        col = lax.broadcasted_iota(jnp.int32, (length, shards * length), 1)
        place = jnp.where(col - row == idx[0] * length, 1.0, 0.0).astype(BF)
        return dot(bias[...], place)

    first = spread(b_ada)
    at = wide
    for bias in biases:
        full = spread(bias)
        for out in outs:
            out[:, at : at + full.shape[1]] = full
        at += full.shape[1]
    wait_all(copies)
    for layer in range(layers):
        result = dot(acts, w_pad[:, layer * wide : (layer + 1) * wide]) + first[layer : layer + 1]
        for step in range(shards):
            outs[step][layer : layer + 1, :wide] = result[step : step + 1]


def stack_kernel(extra, first, second, out, rows_f32):
    size = first.shape[0] - extra
    rows_f32[:size] = first[:size].astype(F32)
    rows_f32[size : 2 * size] = second[:size].astype(F32)
    if extra:
        rows_f32[2 * size :] = first[size:].astype(F32) + second[size:].astype(F32)
    out[...] = rows_f32[...].astype(BF)


def group_kernel(idx, w_ada, first, second, keep, send, stacked, rows_f32, out_f32, w_pad, sems):
    copies = padded_rows(idx, w_ada, w_pad, sems)
    start_all(copies)
    width = w_pad.shape[0]
    size = first.shape[0]
    rows_f32[:size] = first[...].astype(F32)
    rows_f32[size:] = second[...].astype(F32)
    cols = stacked.shape[1]
    biases = col_sum(rows_f32[:, cols:])
    out_f32[...] = jnp.zeros(out_f32.shape, F32)
    out_f32[: 2 * size] = rows_f32[:, :cols]
    for row, at in enumerate(range(0, biases.shape[1], cols)):
        part = biases[:, at : at + cols]
        out_f32[2 * size + row : 2 * size + row + 1, : part.shape[1]] = part
    stacked[...] = out_f32[...].astype(BF)
    wait_all(copies)
    result = dot_nt(rows_f32[:, width:cols].astype(BF), w_pad[...])
    half = keep.shape[0]
    keep[...] = result[:half]
    send[...] = result[half:]


def ada_grad_kernel(rows, wide, extra, inverse_count, *refs):
    idx, stacks = refs[0], refs[1:-4]
    grad_ada, sums, turned, gathered_f32 = refs[-4:]
    layers = grad_ada.shape[0]
    width = turned.shape[0]
    size = stacks[0].shape[0] - extra
    cols = stacks[0].shape[1]
    biases = 0.0
    for number, stack in enumerate(stacks):
        gathered_f32[number * size : (number + 1) * size] = stack[:size].astype(F32)
        biases = biases + stack[size:].astype(F32)
    gathered = gathered_f32[...].astype(BF)
    turned[...] = gathered_f32[:, :width].T
    own = turned[block_at(idx[0] * rows, rows), :].astype(BF)
    for layer in range(layers):
        at = width + layer * wide
        grad_ada[layer] = dot(own, gathered[:, at : at + wide]) * inverse_count
    sums[:, : cols - width] = col_sum(gathered_f32[:, width:]) * inverse_count
    for row in range(extra):
        at = cols - width + row * cols
        part = min(cols, sums.shape[1] - at)
        sums[:, at : at + part] = biases[row : row + 1, :part] * inverse_count


def core_sum_kernel(slots, count, *refs):
    keeps, recvs, outs = refs[:count], refs[count : 2 * count], refs[2 * count :]
    for (first, number), out in zip(slots, outs):
        for slot in range(number):
            at = 0
            for keep, recv in zip(keeps, recvs):
                wide = keep.shape[-1]
                total = keep[first + slot].astype(F32) + recv[first + slot].astype(F32)
                out[slot, :, at : at + wide] = total.astype(BF)
                at += wide


def split_sum_kernel(mine, other, keep, send):
    keep[...] = (mine[0].astype(F32) + other[0].astype(F32)).astype(BF)
    send[...] = (mine[1].astype(F32) + other[1].astype(F32)).astype(BF)


def row_split_kernel(*refs):
    idx, terms, keep, send, halves = refs[0], refs[1:-3], refs[-3], refs[-2], refs[-1]
    total = terms[0][...].astype(F32)
    for term in terms[1:]:
        total = total + term[...].astype(F32)
    half = halves.shape[1]
    for side in range(2):
        halves[side] = total[side * half : (side + 1) * half].astype(BF)
    mine = idx[1] % 2
    keep[...] = halves[mine]
    send[...] = halves[1 - mine]


def sum_kernel(*refs):
    total = refs[0][...].astype(F32)
    for term in refs[1:-1]:
        total = total + term[...].astype(F32)
    refs[-1][...] = total.astype(BF).reshape(refs[-1].shape)


def finish_kernel(rows, plan, factor, *refs):
    idx = refs[0]
    terms = list(refs[1 : 1 + sum(2 * parts for _, parts in plan)])
    at = 1 + len(terms)
    g_qkv, g_proj, g_fc1, g_fc2 = refs[at : at + 4]
    scratch = refs[at + 4 :]
    width = g_proj.shape[-1]
    hidden = g_fc1.shape[-1]
    for (members, parts), halves in zip(plan, scratch):
        for core in (idx[2], 1 - idx[2]):
            if parts == 1:
                halves[core] = terms.pop(0)[...]
            else:
                size = terms[0].shape[0]
                for side in (idx[1] % 2, 1 - idx[1] % 2):
                    halves[core, block_at(side * size, size), :] = terms.pop(0)[...]
        for kind, layer, skip in members:
            if kind == "qkv":
                first = halves[0, :, skip : skip + 2 * width]
                g_qkv[layer, :, : 2 * width] = first.astype(F32) * factor
                second = halves[1, :, skip : skip + 2 * width].astype(F32) * factor
                g_qkv[layer, :, 2 * width :] = second[:, :width]
                g_proj[layer] = second[:, width:]
            else:
                g_fc1[layer] = halves[0, :, skip : skip + hidden].astype(F32) * factor
                for part in range(hidden // width):
                    at = skip + part * width
                    g_fc2[layer, part * rows : (part + 1) * rows] = (
                        halves[1, :, at : at + width].astype(F32) * factor
                    )


def shards(
    latents, condition, cotangent, w_qkv, b_qv, w_proj, b_proj, w_fc1, b_fc1, w_fc2, b_fc2, w_ada,
    b_ada,
):
    layers, rows, _ = w_qkv.shape
    width = w_proj.shape[-1]
    hidden = w_fc1.shape[-1]
    wide = w_ada.shape[-1]
    seq = latents.shape[1]
    n_shard = lax.axis_size("shard")
    n_rep = lax.axis_size("rep")
    levels = n_rep // CORES
    shard_id = lax.axis_index("shard")
    rep_id = lax.axis_index("rep")
    core = rep_id % CORES
    idx = jnp.stack([shard_id, rep_id // CORES, core]).astype(jnp.int32)
    total_latents = latents.shape[0] * n_shard * n_rep
    factor = 1.0 / total_latents

    def exchange(array, by_shard=0, by_level=0, by_core=0, turn=None):
        moves = []
        for own_shard in range(n_shard):
            for own_rep in range(n_rep):
                mask = turn[own_rep % CORES] if turn else by_shard
                peer = (own_shard ^ mask) * n_rep + (own_rep ^ (by_level * CORES + by_core))
                moves.append((own_shard * n_rep + own_rep, peer))
        return lax.ppermute(array, ("shard", "rep"), moves)

    def after(array, *earlier):
        return lax.optimization_barrier((array,) + earlier)[0]

    relay = n_shard == 4
    first_turn, second_turn = (1, 2), (2, 1)

    half_wide = {"qkv": 2 * width, "mlp": hidden}
    copy_total = {"qkv": 3, "mlp": 1 + hidden // width}

    def pack(*plan):
        whole = run(
            functools.partial(pack_kernel, plan), "pack",
            [(array, "h") for array in (w_qkv, w_proj, w_fc1, w_fc2)],
            [((rows, 2 * sum(half_wide[kind] for kind in kinds)), BF, "v") for _, kinds in plan],
            [pltpu.SemaphoreType.DMA((sum(copy_total[kind] for _, ks in plan for kind in ks),))],
        )
        if relay:
            return whole
        return [
            lax.dynamic_slice_in_dim(array, core * (array.shape[1] // 2), array.shape[1] // 2, 1)
            for array in whole
        ]

    def near_first(packed):
        if relay:
            return [exchange(packed, turn=first_turn)]
        return [exchange(packed, by_shard=step) for step in range(1, n_shard)]

    def near_half(near, *earlier):
        source = after(near[0], *earlier) if earlier else near[0]
        if not relay:
            return source
        half = source.shape[1] // 2
        return run(
            half_kernel, "half", [(idx, "s"), (source, "a")],
            [((source.shape[0], half), BF, "a")], [pltpu.SemaphoreType.DMA((1,))],
        )[0]

    def near_second(near, part):
        return near + [exchange(part, turn=second_turn)] if relay else near

    def far_of(near, *earlier):
        return [exchange(after(piece, *earlier) if earlier else piece, by_core=1) for piece in near]

    conditions = [condition] + [exchange(condition, by_shard=step) for step in range(1, n_shard)]
    packed = [pack((layer, ("qkv", "mlp")))[0] for layer in range(layers)]
    near = [near_first(packed[0])]
    near += [near_first(after(own, *conditions[1:])) for own in packed[1:]]
    pad_scratch = [pltpu.VMEM((width, layers * wide), BF), pltpu.SemaphoreType.DMA((layers,))]
    span = wide + 4 * width + hidden
    partial = run(
        functools.partial(modulate_kernel, n_shard), "modulate",
        [(idx, "s"), (w_ada, "a"), (b_ada, "k"), (b_qv, "k"), (b_proj, "k"), (b_fc1, "k"),
         (b_fc2, "k"), (conditions[0], "k")] + [(array, "v") for array in conditions[1:]],
        [((layers, span), F32, "v")] * n_shard, pad_scratch, flops=10**7,
    )
    parts = [near_half(near[0], partial[0])]
    mod_all = partial[0]
    for step in range(1, n_shard):
        mod_all = mod_all + exchange(after(partial[step], parts[0]), by_shard=step)
    for own in near[1:]:
        parts.append(near_half(own, mod_all))
    near = [near_second(own, part) for own, part in zip(near, parts)]
    mod_all = after(mod_all, *parts[1:])
    pieces = {0: (near[0], far_of(near[0]))}

    big = seq * width
    row = lambda kind="v": ((seq, width), F32, kind)
    vec_wide = {"qkv": 6 * width, "mlp": 4 * width + hidden}

    def piece_args(pair):
        return [(array, "a") for array in pair[0] + pair[1]]

    copy_count = 6 if relay else 2 * (n_shard - 1)
    qkv_sems = pltpu.SemaphoreType.DMA((3 + copy_count,))
    mlp_sems = pltpu.SemaphoreType.DMA((1 + hidden // width + copy_count,))
    out_sems = pltpu.SemaphoreType.DMA((2 * n_shard,))
    w_qkv_all = pltpu.VMEM((2, width, 2 * width), BF)
    w_mlp_all = pltpu.VMEM((2, width, hidden), BF)

    def grads_out(kind):
        return [((n_shard, rows, half_wide[kind]), BF, "a")] * 2

    stream = latents[0]
    saved = []
    vecs, raw = {}, {}
    for layer in range(layers):
        pair, offset = pieces[layer], 0
        keep_in = "v" if layer + 1 == layers else "k"
        qkv, probs, attended, branch, middle = run(
            functools.partial(attention_forward, layer, rows, offset, n_shard), "attention_forward",
            [(idx, "s"), (stream, "v"), (mod_all, "v"), (w_qkv, "a"), (w_proj, "a")]
            + piece_args(pair),
            [((seq, 3 * width), BF, keep_in), ((HEADS, seq, seq), F32, keep_in),
             ((seq, width), BF, keep_in), row(keep_in), row()],
            [w_qkv_all, qkv_sems], flops=10 * big * width,
        )
        pair, offset = pieces[layer], 2 * width
        entry = dict(stream=stream, qkv=qkv, probs=probs, attended=attended, branch=branch,
                     middle=middle)
        if layer + 1 < layers:
            act_low, slopes, mlp_out, stream = run(
                functools.partial(mlp_forward, layer, rows, offset, n_shard), "mlp_forward",
                [(idx, "s"), (middle, "v"), (mod_all, "v"), (w_fc1, "a"), (w_fc2, "a")]
                + piece_args(pair),
                [((seq, hidden), BF, keep_in), ((seq, hidden), F32, keep_in), row(keep_in), row()],
                [w_mlp_all, mlp_sems], flops=16 * big * width,
            )
            entry.update(act_low=act_low, slopes=slopes, mlp_out=mlp_out)
            pieces[layer + 1] = (near[layer + 1], far_of(near[layer + 1], middle))
        else:
            x_out, d_middle, vecs["mlp", layer], *raw["mlp", layer] = run(
                functools.partial(mlp_both, layer, rows, offset, n_shard), "mlp_both",
                [(idx, "s"), (middle, "v"), (mod_all, "v"), (cotangent[0], "v"), (w_fc1, "a"),
                 (w_fc2, "a")] + piece_args(pair),
                [((seq, width), BF, "v"), row(), ((1, vec_wide["mlp"]), F32, "v")]
                + grads_out("mlp"),
                [w_mlp_all, w_mlp_all, pltpu.VMEM((seq, hidden), BF),
                 pltpu.VMEM((seq, hidden), F32), mlp_sems, out_sems], flops=48 * big * width,
            )
        saved.append(entry)

    def core_sum(keys, *earlier):
        keeps = [raw[key][0] for key in keys]
        received = [exchange(raw[key][1], by_core=1) for key in keys]
        if earlier:
            keeps[0] = after(keeps[0], *earlier)
        total_wide = sum(keep.shape[-1] for keep in keeps)
        slots = [(0, 2), (2, 2)] if relay else [(slot, 1) for slot in range(n_shard)]
        return run(
            functools.partial(core_sum_kernel, slots, len(keys)), "core_sum",
            [(array, "v") for array in keeps + received],
            [((number, rows, total_wide), BF, "v") for _, number in slots],
        )

    def shard_send(summed):
        if relay:
            return [exchange(summed[1], turn=first_turn)]
        return [exchange(summed[step], by_shard=step) for step in range(1, n_shard)]

    def add(terms, shape):
        return run(sum_kernel, "add", [(array, "v") for array in terms], [(shape, BF, "v")])[0]

    def shard_second(summed, arrived, *earlier):
        shape = summed[0].shape[1:]
        mine = after(summed[0], *earlier) if earlier else summed[0]
        if not relay:
            return [mine.reshape(shape)] + [array.reshape(shape) for array in arrived]
        keep, send = run(
            split_sum_kernel, "split_sum", [(mine, "v"), (arrived[0], "v")], [(shape, BF, "v")] * 2
        )
        return [keep, exchange(send, turn=second_turn)]

    def level_first(terms, halve, *earlier):
        shape = terms[0].shape
        if earlier:
            terms = [after(terms[0], *earlier)] + terms[1:]
        if not halve or shape[0] % 32:
            total = add(terms, shape)
            return False, total, exchange(total, by_level=1)
        part = (shape[0] // 2, shape[1])
        keep, send = run(
            row_split_kernel, "row_split",
            [(idx, "s")] + [(array, "v") for array in terms],
            [(part, BF, "v")] * 2, [pltpu.VMEM((2,) + part, BF)],
        )
        return True, keep, exchange(send, by_level=1)

    def level_second(first, *earlier):
        halved, kept, arriving = first
        if earlier:
            kept = after(kept, *earlier)
        return halved, add([kept, arriving], kept.shape)

    def level_last(halved, total, step):
        while step < levels:
            total = add([total, exchange(total, by_level=step)], total.shape)
            step *= 2
        near = [total, exchange(total, by_level=1)] if halved else [total]
        return near + far_of(near)

    waiting = []
    for layer in reversed(range(layers)):
        entry = saved[layer]
        pair, offset = pieces[layer], 2 * width
        if layer + 1 < layers:
            keys = [("qkv", layer + 1), ("mlp", layer + 1)]
            summed = core_sum(keys, grad_stream)
            waiting.append((keys, summed, shard_send(summed)))
            grad_stream = after(grad_stream, summed[0])
            d_middle, vecs["mlp", layer], *raw["mlp", layer] = run(
                functools.partial(mlp_backward, layer, rows, offset, n_shard), "mlp_backward",
                [(idx, "s"), (entry["middle"], "v"), (mod_all, "v"), (grad_stream, "v"),
                 (entry["act_low"], "v"), (entry["slopes"], "v"), (entry["mlp_out"], "v"),
                 (w_fc1, "a"), (w_fc2, "a")] + piece_args(pair),
                [row(), ((1, vec_wide["mlp"]), F32, "v")] + grads_out("mlp"),
                [w_mlp_all, w_mlp_all, mlp_sems, out_sems], flops=32 * big * width,
            )
            core_mlp = core_sum([("mlp", layer)], d_middle)
            sent_mlp = shard_send(core_mlp)
            d_middle = after(d_middle, core_mlp[0])
        pair, offset = pieces[layer], 0
        grad_stream, vecs["qkv", layer], *raw["qkv", layer] = run(
            functools.partial(attention_backward, layer, rows, offset, n_shard),
            "attention_backward",
            [(idx, "s"), (entry["stream"], "v"), (mod_all, "v"), (d_middle, "v"),
             (entry["qkv"], "v"), (entry["probs"], "v"), (entry["attended"], "v"),
             (entry["branch"], "v"), (w_qkv, "a"), (w_proj, "a")] + piece_args(pair),
            [row(), ((1, vec_wide["qkv"]), F32, "v")] + grads_out("qkv"),
            [w_qkv_all, pltpu.VMEM((seq, 3 * width), BF), w_qkv_all, qkv_sems, out_sems],
            flops=28 * big * width,
        )
    cond_in = condition.astype(F32)
    vector = [jax.nn.silu(cond_in).astype(BF)]
    for layer in range(layers):
        vector += [vecs[kind, layer][:, : 3 * width].astype(BF) for kind in ("qkv", "mlp")]
    for layer in range(layers):
        vector += [vecs[kind, layer][:, 3 * width :].astype(BF) for kind in ("qkv", "mlp")]
    vector = jnp.concatenate(vector, axis=1)
    length = vector.shape[1]
    masks = [first_turn, second_turn] if relay else []
    while not relay and 2 ** len(masks) < n_shard:
        masks.append((2 ** len(masks),) * 2)

    cols = width + layers * wide
    extra = -(-(length - cols) // cols)

    def stack(first, second, extra=0):
        shape = (2 * first.shape[0] - extra, first.shape[1])
        return run(
            functools.partial(stack_kernel, extra), "stack", [(first, "v"), (second, "v")],
            [(shape, BF, "v")], [pltpu.VMEM(shape, F32)],
        )[0]

    (keys_first, core_first, sent_first), = waiting
    plan = [keys_first, [("mlp", 0)], [("qkv", 0)]]
    a = shard_second(core_first, sent_first, grad_stream)
    core_qkv = core_sum(plan[2], a[0])
    sent_qkv = shard_send(core_qkv)
    b = shard_second(core_mlp, sent_mlp, core_qkv[0])
    a = level_first(a, True, b[0])
    c = shard_second(core_qkv, sent_qkv, a[1])
    vector = after(vector, b[0])
    for mask in masks[:-2]:
        vector = stack(vector, exchange(vector, turn=mask))
    arriving = exchange(vector, turn=masks[-2])
    vector = stack(after(vector, c[0]), arriving)
    arriving = exchange(vector, turn=masks[-1])
    b = level_first(b, True, vector)
    a = level_second(a, b[1])
    a_moving = exchange(a[1], by_level=2)
    c = level_first(c, False, a[1])
    grad_cond, passed, stacked = run(
        group_kernel, "group",
        [(idx, "s"), (w_ada, "a"), (after(vector, c[1]), "v"), (arriving, "v")],
        [((n_shard // 2, width), F32, "v")] * 2 + [((n_shard + extra, cols), BF, "v")],
        [pltpu.VMEM((n_shard, length), F32), pltpu.VMEM((n_shard + extra, cols), F32)]
        + pad_scratch, flops=10**7,
    )
    arriving = exchange(stacked, by_level=1)
    b = level_second(b, stacked)
    b_moving = exchange(b[1], by_level=2)
    c = level_second(c, b[1])
    c_moving = exchange(c[1], by_level=2)
    stacked = stack(after(stacked, c[1]), arriving, extra)
    step = 2
    while 2 * step < levels:
        stacked = stack(stacked, exchange(stacked, by_level=step), extra)
        step *= 2
    arriving = exchange(stacked, by_level=step)
    a = (a[0], add([after(a[1], stacked), a_moving], a[1].shape))
    a_parts = level_last(*a, 4)
    grad_cond = grad_cond + exchange(passed, turn=masks[-1])
    for mask in masks[-2::-1]:
        half = grad_cond.shape[0] // 2
        grad_cond = grad_cond[:half] + exchange(grad_cond[half:], turn=mask)
    cond_grad = jax.vjp(jax.nn.silu, cond_in)[1](grad_cond)[0]
    stacks = [after(stacked, a[1]), arriving]
    stacks = stacks + far_of(stacks)
    grad_ada, sums = run(
        functools.partial(ada_grad_kernel, rows, wide, extra, factor), "ada_grad",
        [(idx, "s")] + [(array, "v") for array in stacks],
        [((layers, rows, wide), F32, "v"), ((1, length - width), F32, "v")],
        [pltpu.VMEM((width, total_latents), F32), pltpu.VMEM((total_latents, cols), F32)],
        flops=10**8,
    )

    b = (b[0], add([after(b[1], sums), b_moving], b[1].shape))
    b_parts = level_last(*b, 4)
    c = (c[0], add([after(c[1], b[1]), c_moving], c[1].shape))
    finals = [a_parts, b_parts, level_last(*c, 4)]

    def own_part(parts):
        whole = jnp.concatenate(parts, axis=0)
        length = whole.shape[1] // n_shard
        return lax.dynamic_slice_in_dim(whole, shard_id * length, length, axis=1)

    base = layers * wide
    at = [base + layer * (4 * width + hidden) for layer in range(layers)]
    grad_ada_bias = own_part([sums[:, layer * wide : (layer + 1) * wide] for layer in range(layers)])
    grad_qv_bias = own_part([sums[:, a : a + 2 * width] for a in at])
    grad_proj_bias = own_part([sums[:, a + 2 * width : a + 3 * width] for a in at])
    grad_fc1_bias = own_part([sums[:, a + 3 * width : a + 3 * width + hidden] for a in at])
    grad_fc2_bias = own_part([sums[:, a + 3 * width + hidden : a + 4 * width + hidden] for a in at])

    finish_plan, finish_inputs, finish_scratch = [], [(idx, "s")], []
    for keys, parts in zip(plan, finals):
        members, skip = [], 0
        for kind, layer in keys:
            members.append((kind, layer, skip))
            skip += half_wide[kind]
        finish_plan.append((members, len(parts) // 2))
        finish_inputs += [(array, "v") for array in parts]
        finish_scratch.append(pltpu.VMEM((2, rows, skip), BF))
    grad_qkv, grad_proj, grad_fc1, grad_fc2 = run(
        functools.partial(finish_kernel, rows, finish_plan, factor), "finish",
        finish_inputs,
        [(array.shape, F32, "v") for array in (w_qkv, w_proj, w_fc1, w_fc2)],
        finish_scratch,
    )
    return (
        x_out[None], grad_stream[None], cond_grad, grad_qkv, grad_qv_bias, grad_proj,
        grad_proj_bias, grad_fc1, grad_fc1_bias, grad_fc2, grad_fc2_bias, grad_ada, grad_ada_bias,
    )


def solution(mesh):
    rows3, rows2 = P(("shard", "rep"), None, None), P(("shard", "rep"), None)
    weight, bias = P(None, "shard", None), P(None, "shard")
    return jax.shard_map(
        shards,
        mesh=mesh,
        in_specs=(rows3, rows2, rows3) + (weight, bias) * 5,
        out_specs=(rows3, rows3, rows2) + (weight, bias) * 5,
        check_vma=False,
    )
```

```python
import functools

import jax
import jax.numpy as jnp
from jax import lax
from jax.experimental import pallas as pl
from jax.experimental.pallas import tpu as pltpu
from jax.sharding import PartitionSpec as P

HEADS = 6
BF = jnp.bfloat16
F32 = jnp.float32
CORES = 2
VMEM_LIMIT = 40 * 1024 * 1024


def dot(left, right):
    return jnp.dot(left, right, preferred_element_type=F32)


def dot_nt(left, right):
    return lax.dot_general(left, right, (((1,), (1,)), ((), ())), preferred_element_type=F32)


def dot_tn(left, right):
    return lax.dot_general(left, right, (((0,), (0,)), ((), ())), preferred_element_type=F32)


def layer_norm(rows):
    center = rows - jnp.mean(rows, axis=-1, keepdims=True)
    inverse = lax.rsqrt(jnp.mean(center * center, axis=-1, keepdims=True) + 1e-06)
    return center * inverse, inverse


def norm_back(grad_norm, normed, inverse):
    centered = grad_norm - jnp.mean(grad_norm, axis=-1, keepdims=True)
    return inverse * (centered - normed * jnp.mean(grad_norm * normed, axis=-1, keepdims=True))


def col_sum(rows):
    return jnp.sum(rows, axis=0, keepdims=True)


def block_at(start, size):
    return pl.ds(pl.multiple_of(start, size), size)


def start_all(copies):
    for copy in copies:
        copy.start()


def wait_all(copies):
    for copy in copies:
        copy.wait()


def make_copies(pairs, sems):
    return [
        pltpu.make_async_copy(source, target, sems.at[slot])
        for slot, (source, target) in enumerate(pairs)
    ]


def run(body, name, inputs, outputs, scratch=(), flops=0):
    places = {"v": pltpu.VMEM, "k": pltpu.VMEM, "a": pl.ANY, "h": pl.ANY, "s": pltpu.SMEM}
    arrays = [
        pltpu.with_memory_space_constraint(arr, pltpu.HBM) if kind in "hk" else arr
        for arr, kind in inputs
    ]
    return pl.pallas_call(
        body,
        out_shape=[
            pltpu.HBM(shape, dtype) if kind in "hk" else jax.ShapeDtypeStruct(shape, dtype)
            for shape, dtype, kind in outputs
        ],
        in_specs=[pl.BlockSpec(memory_space=places[kind]) for _, kind in inputs],
        out_specs=[pl.BlockSpec(memory_space=places[kind]) for _, _, kind in outputs],
        scratch_shapes=list(scratch),
        compiler_params=pltpu.CompilerParams(vmem_limit_bytes=VMEM_LIMIT),
        cost_estimate=pl.CostEstimate(flops=1, bytes_accessed=1, transcendentals=0),
        name=name,
    )(*arrays)


def pack_kernel(plan, *refs):
    w_qkv, w_proj, w_fc1, w_fc2 = refs[:4]
    outs, sems = refs[4:-1], refs[-1]
    rows, width = w_proj.shape[1:]
    hidden = w_fc1.shape[-1]
    pairs = []
    for (layer, kinds), out in zip(plan, outs):
        at = 0
        pieces = {"qkv": [w_qkv.at[layer, :, : 2 * width]], "mlp": [w_fc1.at[layer]]}
        second = {
            "qkv": [w_qkv.at[layer, :, 2 * width :], w_proj.at[layer]],
            "mlp": [
                w_fc2.at[layer, part * rows : (part + 1) * rows]
                for part in range(hidden // width)
            ],
        }
        for half in (pieces, second):
            for kind in kinds:
                for piece in half[kind]:
                    pairs.append((piece, out.at[:, at : at + piece.shape[-1]]))
                    at += piece.shape[-1]
    copies = make_copies(pairs, sems)
    start_all(copies)
    wait_all(copies)


def half_kernel(idx, whole, out, sems):
    half = out.shape[1]
    copies = make_copies([(whole.at[:, block_at(idx[2] * half, half)], out)], sems)
    start_all(copies)
    wait_all(copies)


def piece_count(shards):
    return 2 if shards == 4 else shards - 1


def peer_order(shards, core):
    if shards != 4:
        return list(range(shards))
    return [0, 2 - core, 1 + core, 3]


def qkv_pairs(idx, layer, rows, offset, w_qkv, w_proj, near, far, w_all):
    width = w_proj.shape[-1]
    own = block_at(idx[0] * rows, rows)
    pairs = [
        (w_qkv.at[layer, :, : 2 * width], w_all.at[0, own, :]),
        (w_qkv.at[layer, :, 2 * width :], w_all.at[1, own, :width]),
        (w_proj.at[layer], w_all.at[1, own, width:]),
    ]
    return pairs + piece_pairs(idx, rows, offset, 2 * width, near, far, w_all)


def mlp_pairs(idx, layer, rows, offset, w_fc1, w_fc2, near, far, w_all):
    width = w_fc2.shape[-1]
    hidden = w_fc1.shape[-1]
    own = block_at(idx[0] * rows, rows)
    pairs = [(w_fc1.at[layer], w_all.at[0, own, :])]
    for part in range(hidden // width):
        pairs.append(
            (
                w_fc2.at[layer, part * rows : (part + 1) * rows, :],
                w_all.at[1, own, part * width : (part + 1) * width],
            )
        )
    return pairs + piece_pairs(idx, rows, offset, hidden, near, far, w_all)


def piece_pairs(idx, rows, offset, wide, near, far, w_all):
    pairs = []
    shards = w_all.shape[1] // rows
    for pieces, core in ((near, idx[2]), (far, 1 - idx[2])):
        for slot, piece in enumerate(pieces):
            if shards != 4:
                mask, halves = slot + 1, [(core, 0)]
            elif slot == 0:
                mask, halves = 1 + core, [(0, 0), (1, piece.shape[1] // 2)]
            else:
                mask, halves = 3, [(core, 0)]
            place = block_at(jnp.bitwise_xor(idx[0], mask) * rows, rows)
            for half, first in halves:
                at = first + offset
                pairs.append((piece.at[:, at : at + wide], w_all.at[half, place, :]))
    return pairs


def grad_pairs(idx, rows, shards, grad_all, keep, send):
    pairs = []
    for slot in range(shards):
        for target, core in ((keep, idx[2]), (send, 1 - idx[2])):
            mask = peer_order(shards, core)[slot]
            place = block_at(jnp.bitwise_xor(idx[0], mask) * rows, rows)
            pairs.append((grad_all.at[core, place, :], target.at[slot]))
    return pairs


def fc2_chunk(w_all, rows, chunk):
    width = w_all.shape[1]
    parts = w_all.shape[2] // width
    blocks = []
    for number in range(chunk * width // rows, (chunk + 1) * width // rows):
        at, part = number // parts, number % parts
        blocks.append(w_all[1, at * rows : (at + 1) * rows, part * width : (part + 1) * width])
    return jnp.concatenate(blocks, axis=0)


def attention_forward(layer, rows, offset, shards, *refs):
    peers = piece_count(shards)
    idx, stream, mod_all, w_qkv, w_proj = refs[:5]
    near, far = refs[5 : 5 + peers], refs[5 + peers : 5 + 2 * peers]
    qkv_out, probs_out, attended_out, branch_out, middle_out, w_all, sems = refs[5 + 2 * peers :]
    mod = mod_all.at[layer : layer + 1]
    copies = make_copies(
        qkv_pairs(idx, layer, rows, offset, w_qkv, w_proj, near, far, w_all), sems
    )
    start_all(copies)
    width = stream.shape[-1]
    head = width // HEADS
    b_qv, b_proj = mod[:, 6 * width : 8 * width], mod[:, 8 * width : 9 * width]
    values = stream[...].astype(F32)
    shift, scale, gate = (mod[:, part * width : (part + 1) * width] for part in range(3))
    normed, _ = layer_norm(values)
    h_one = (normed * (1.0 + scale) + shift).astype(BF)
    wait_all(copies)
    mixed = dot(h_one, w_all[0])
    qkv_out[:, :width] = (mixed[:, :width] + b_qv[:, :width]).astype(BF)
    qkv_out[:, width : 2 * width] = mixed[:, width:].astype(BF)
    qkv_out[:, 2 * width :] = (dot(h_one, w_all[1, :, :width]) + b_qv[:, width:]).astype(BF)
    lane = lax.broadcasted_iota(jnp.int32, (1, 2 * head), 1)
    masks = [(lane < head).astype(BF), (lane >= head).astype(BF)]
    for pair in range(HEADS // 2):
        at = pair * 2 * head
        queries = qkv_out[:, at : at + 2 * head]
        keys = qkv_out[:, width + at : width + at + 2 * head]
        vals = qkv_out[:, 2 * width + at : 2 * width + at + 2 * head]
        attended = 0.0
        for side in range(2):
            scores = dot_nt(queries, keys * masks[side]) * head ** (-0.5)
            raised = jnp.exp(scores - jnp.max(scores, axis=-1, keepdims=True))
            probs = raised * (1.0 / jnp.sum(raised, axis=-1, keepdims=True))
            probs_out[2 * pair + side] = probs
            attended = attended + dot(probs.astype(BF), vals * masks[side])
        attended_out[:, at : at + 2 * head] = attended.astype(BF)
    branch = dot(attended_out[...], w_all[1, :, width:]) + b_proj
    branch_out[...] = branch
    middle_out[...] = values + gate * branch


def attention_backward(layer, rows, offset, shards, *refs):
    peers = piece_count(shards)
    idx, stream, mod_all, d_middle_in, qkv, probs_in, attended, branch, w_qkv, w_proj = refs[:10]
    near, far = refs[10 : 10 + peers], refs[10 + peers : 10 + 2 * peers]
    d_stream, vec, keep, send, w_all, d_qkv, grad_all, sems, out_sems = refs[10 + 2 * peers :]
    mod = mod_all.at[layer : layer + 1]
    copies = make_copies(
        qkv_pairs(idx, layer, rows, offset, w_qkv, w_proj, near, far, w_all), sems
    )
    start_all(copies)
    width = stream.shape[-1]
    head = width // HEADS
    root = head ** (-0.5)
    shift, scale, gate = (mod[:, part * width : (part + 1) * width] for part in range(3))
    normed, inverse = layer_norm(stream[...].astype(F32))
    h_one = (normed * (1.0 + scale) + shift).astype(BF)
    d_middle = d_middle_in[...]
    vec[:, 2 * width : 3 * width] = col_sum(d_middle * branch[...])
    d_branch = (d_middle * gate).astype(BF)
    grad_all[1, :, width:] = dot_tn(attended[...], d_branch).astype(BF)
    vec[:, 5 * width :] = col_sum(d_branch.astype(F32))
    wait_all(copies)
    d_attended = dot_nt(d_branch, w_all[1, :, width:]).astype(BF)
    lane = lax.broadcasted_iota(jnp.int32, (1, 2 * head), 1)
    masks = [(lane < head).astype(BF), (lane >= head).astype(BF)]
    for pair in range(HEADS // 2):
        at = pair * 2 * head
        queries = qkv[:, at : at + 2 * head]
        keys = qkv[:, width + at : width + at + 2 * head]
        vals = qkv[:, 2 * width + at : 2 * width + at + 2 * head]
        d_att = d_attended[:, at : at + 2 * head]
        d_queries, d_keys, d_values = 0.0, 0.0, 0.0
        for side in range(2):
            probs = probs_in[2 * pair + side]
            d_values = d_values + dot_tn(probs.astype(BF), d_att * masks[side])
            d_probs = dot_nt(d_att, vals * masks[side])
            inner = jnp.sum(probs * d_probs, axis=-1, keepdims=True)
            d_scores = (probs * (d_probs - inner)).astype(BF)
            d_queries = d_queries + dot(d_scores, keys * masks[side])
            d_keys = d_keys + dot_tn(d_scores, queries * masks[side])
        d_qkv[:, at : at + 2 * head] = (d_queries * root).astype(BF)
        d_qkv[:, width + at : width + at + 2 * head] = (d_keys * root).astype(BF)
        d_qkv[:, 2 * width + at : 2 * width + at + 2 * head] = d_values.astype(BF)
    d_qk, d_val = d_qkv[:, : 2 * width], d_qkv[:, 2 * width :]
    grad_all[0] = dot_tn(h_one, d_qk).astype(BF)
    grad_all[1, :, :width] = dot_tn(h_one, d_val).astype(BF)
    out_copies = make_copies(grad_pairs(idx, rows, shards, grad_all, keep, send), out_sems)
    start_all(out_copies)
    vec[:, 3 * width : 4 * width] = col_sum(d_qk[:, :width].astype(F32))
    vec[:, 4 * width : 5 * width] = col_sum(d_val.astype(F32))
    d_h_one = dot_nt(d_qk, w_all[0]) + dot_nt(d_val, w_all[1, :, :width])
    vec[:, :width] = col_sum(d_h_one)
    vec[:, width : 2 * width] = col_sum(d_h_one * normed)
    d_stream[...] = d_middle + norm_back(d_h_one * (1.0 + scale), normed, inverse)
    wait_all(out_copies)


def gelu_parts(pre_act):
    root = 0.7978845608028654
    square = pre_act * pre_act
    bent = jnp.tanh(root * pre_act * (1.0 + 0.044715 * square))
    half = 0.5 * (1.0 + bent)
    slope = half + 0.5 * pre_act * (1.0 - bent * bent) * (root * (1.0 + 3 * 0.044715 * square))
    return pre_act * half, slope


def mlp_vectors(mod_all, layer, width):
    mod = mod_all.at[layer : layer + 1]
    last = mod_all.shape[-1] - width
    return mod, mod[:, 9 * width : last], mod[:, last:]


def mlp_forward_part(rows, h_two, b_fc1, b_fc2, w_all, act_low, slopes):
    width = w_all.shape[1]
    mlp_out = b_fc2
    for chunk in range(w_all.shape[2] // width):
        cols = slice(chunk * width, (chunk + 1) * width)
        act, slope = gelu_parts(dot(h_two, w_all[0, :, cols]) + b_fc1[:, cols])
        act_low[:, cols] = act.astype(BF)
        slopes[:, cols] = slope
        mlp_out = mlp_out + dot(act_low[:, cols], fc2_chunk(w_all, rows, chunk))
    return mlp_out


def mlp_backward_part(
    idx, rows, shards, grad_out, mlp_out, middle, normed, inverse, h_two, scale, gate,
    w_all, act_low, slopes, vec, d_middle_out, grad_all, keep, send, out_sems,
):
    width = w_all.shape[1]
    parts = w_all.shape[2] // width
    vec[:, 2 * width : 3 * width] = col_sum(grad_out * mlp_out)
    d_mlp = (grad_out * gate).astype(BF)
    vec[:, (3 + parts) * width :] = col_sum(d_mlp.astype(F32))
    d_h_two = 0.0
    for chunk in range(parts):
        cols = slice(chunk * width, (chunk + 1) * width)
        d_act = dot_nt(d_mlp, fc2_chunk(w_all, rows, chunk))
        d_pre = (d_act * slopes[:, cols]).astype(BF)
        vec[:, (3 + chunk) * width : (4 + chunk) * width] = col_sum(d_pre.astype(F32))
        grad_all[0, :, cols] = dot_tn(h_two, d_pre).astype(BF)
        grad_fc2 = dot_tn(act_low[:, cols], d_mlp).astype(BF)
        first = chunk * width // rows
        for number in range(first, (chunk + 1) * width // rows):
            at, part = number // parts, number % parts
            grad_all[1, at * rows : (at + 1) * rows, part * width : (part + 1) * width] = grad_fc2[
                (number - first) * rows : (number - first + 1) * rows
            ]
        d_h_two = d_h_two + dot_nt(d_pre, w_all[0, :, cols])
    out_copies = make_copies(grad_pairs(idx, rows, shards, grad_all, keep, send), out_sems)
    start_all(out_copies)
    vec[:, :width] = col_sum(d_h_two)
    vec[:, width : 2 * width] = col_sum(d_h_two * normed)
    d_middle_out[...] = grad_out + norm_back(d_h_two * (1.0 + scale), normed, inverse)
    wait_all(out_copies)


def mlp_forward(layer, rows, offset, shards, *refs):
    peers = piece_count(shards)
    idx, middle, mod_all, w_fc1, w_fc2 = refs[:5]
    near, far = refs[5 : 5 + peers], refs[5 + peers : 5 + 2 * peers]
    act_low, slopes, mlp_out, stream_out, w_all, sems = refs[5 + 2 * peers :]
    mod, b_fc1, b_fc2 = mlp_vectors(mod_all, layer, middle.shape[-1])
    copies = make_copies(mlp_pairs(idx, layer, rows, offset, w_fc1, w_fc2, near, far, w_all), sems)
    start_all(copies)
    width = middle.shape[-1]
    shift, scale, gate = (mod[:, part * width : (part + 1) * width] for part in range(3, 6))
    normed, _ = layer_norm(middle[...])
    h_two = (normed * (1.0 + scale) + shift).astype(BF)
    wait_all(copies)
    mlp_out[...] = mlp_forward_part(rows, h_two, b_fc1, b_fc2, w_all, act_low, slopes)
    stream_out[...] = middle[...] + gate * mlp_out[...]


def mlp_backward(layer, rows, offset, shards, *refs):
    peers = piece_count(shards)
    idx, middle, mod_all, grad_out, act_low, slopes, mlp_out, w_fc1, w_fc2 = refs[:9]
    near, far = refs[9 : 9 + peers], refs[9 + peers : 9 + 2 * peers]
    d_middle, vec, keep, send, w_all, grad_all, sems, out_sems = refs[9 + 2 * peers :]
    mod = mod_all.at[layer : layer + 1]
    copies = make_copies(mlp_pairs(idx, layer, rows, offset, w_fc1, w_fc2, near, far, w_all), sems)
    start_all(copies)
    width = middle.shape[-1]
    shift, scale, gate = (mod[:, part * width : (part + 1) * width] for part in range(3, 6))
    normed, inverse = layer_norm(middle[...])
    h_two = (normed * (1.0 + scale) + shift).astype(BF)
    wait_all(copies)
    mlp_backward_part(
        idx, rows, shards, grad_out[...], mlp_out[...], middle, normed, inverse, h_two, scale,
        gate, w_all, act_low, slopes, vec, d_middle, grad_all, keep, send, out_sems,
    )


def mlp_both(layer, rows, offset, shards, *refs):
    peers = piece_count(shards)
    idx, middle, mod_all, cotangent, w_fc1, w_fc2 = refs[:6]
    near, far = refs[6 : 6 + peers], refs[6 + peers : 6 + 2 * peers]
    x_out, d_middle, vec, keep, send = refs[6 + 2 * peers : 11 + 2 * peers]
    w_all, grad_all, act_low, slopes, sems, out_sems = refs[11 + 2 * peers :]
    mod, b_fc1, b_fc2 = mlp_vectors(mod_all, layer, middle.shape[-1])
    copies = make_copies(mlp_pairs(idx, layer, rows, offset, w_fc1, w_fc2, near, far, w_all), sems)
    start_all(copies)
    width = middle.shape[-1]
    shift, scale, gate = (mod[:, part * width : (part + 1) * width] for part in range(3, 6))
    normed, inverse = layer_norm(middle[...])
    h_two = (normed * (1.0 + scale) + shift).astype(BF)
    wait_all(copies)
    mlp_out = mlp_forward_part(rows, h_two, b_fc1, b_fc2, w_all, act_low, slopes)
    x_out[...] = (middle[...] + gate * mlp_out).astype(BF)
    mlp_backward_part(
        idx, rows, shards, cotangent[...].astype(F32), mlp_out, middle, normed, inverse, h_two,
        scale, gate, w_all, act_low, slopes, vec, d_middle, grad_all, keep, send, out_sems,
    )


def padded_rows(idx, w_ada, w_pad, sems):
    layers, rows, wide = w_ada.shape
    w_pad[...] = jnp.zeros(w_pad.shape, BF)
    own = block_at(idx[0] * rows, rows)
    return make_copies(
        [
            (w_ada.at[layer], w_pad.at[own, layer * wide : (layer + 1) * wide])
            for layer in range(layers)
        ],
        sems,
    )


def modulate_kernel(shards, *refs):
    idx, w_ada, b_ada = refs[:3]
    biases, conditions = refs[3:7], refs[7 : 7 + shards]
    outs = refs[7 + shards : 7 + 2 * shards]
    w_pad, sems = refs[7 + 2 * shards :]
    copies = padded_rows(idx, w_ada, w_pad, sems)
    start_all(copies)
    layers = w_ada.shape[0]
    wide = w_ada.shape[2]
    acts = []
    for ref in conditions:
        cond = ref[...].astype(F32)
        acts.append(cond / (1.0 + jnp.exp(-cond)))
    acts = jnp.concatenate(acts, axis=0).astype(BF)

    def spread(bias):
        length = bias.shape[1]
        row = lax.broadcasted_iota(jnp.int32, (length, shards * length), 0)
        col = lax.broadcasted_iota(jnp.int32, (length, shards * length), 1)
        place = jnp.where(col - row == idx[0] * length, 1.0, 0.0).astype(BF)
        return dot(bias[...], place)

    first = spread(b_ada)
    at = wide
    for bias in biases:
        full = spread(bias)
        for out in outs:
            out[:, at : at + full.shape[1]] = full
        at += full.shape[1]
    wait_all(copies)
    for layer in range(layers):
        result = dot(acts, w_pad[:, layer * wide : (layer + 1) * wide]) + first[layer : layer + 1]
        for step in range(shards):
            outs[step][layer : layer + 1, :wide] = result[step : step + 1]


def stack_kernel(extra, first, second, out, rows_f32):
    size = first.shape[0] - extra
    rows_f32[:size] = first[:size].astype(F32)
    rows_f32[size : 2 * size] = second[:size].astype(F32)
    if extra:
        rows_f32[2 * size :] = first[size:].astype(F32) + second[size:].astype(F32)
    out[...] = rows_f32[...].astype(BF)


def group_kernel(idx, w_ada, first, second, keep, send, stacked, rows_f32, out_f32, w_pad, sems):
    copies = padded_rows(idx, w_ada, w_pad, sems)
    start_all(copies)
    width = w_pad.shape[0]
    size = first.shape[0]
    rows_f32[:size] = first[...].astype(F32)
    rows_f32[size:] = second[...].astype(F32)
    cols = stacked.shape[1]
    biases = col_sum(rows_f32[:, cols:])
    out_f32[...] = jnp.zeros(out_f32.shape, F32)
    out_f32[: 2 * size] = rows_f32[:, :cols]
    for row, at in enumerate(range(0, biases.shape[1], cols)):
        part = biases[:, at : at + cols]
        out_f32[2 * size + row : 2 * size + row + 1, : part.shape[1]] = part
    stacked[...] = out_f32[...].astype(BF)
    wait_all(copies)
    result = dot_nt(rows_f32[:, width:cols].astype(BF), w_pad[...])
    half = keep.shape[0]
    keep[...] = result[:half]
    send[...] = result[half:]


def ada_grad_kernel(rows, wide, extra, inverse_count, *refs):
    idx, stacks = refs[0], refs[1:-4]
    grad_ada, sums, turned, gathered_f32 = refs[-4:]
    layers = grad_ada.shape[0]
    width = turned.shape[0]
    size = stacks[0].shape[0] - extra
    cols = stacks[0].shape[1]
    biases = 0.0
    for number, stack in enumerate(stacks):
        gathered_f32[number * size : (number + 1) * size] = stack[:size].astype(F32)
        biases = biases + stack[size:].astype(F32)
    gathered = gathered_f32[...].astype(BF)
    turned[...] = gathered_f32[:, :width].T
    own = turned[block_at(idx[0] * rows, rows), :].astype(BF)
    for layer in range(layers):
        at = width + layer * wide
        grad_ada[layer] = dot(own, gathered[:, at : at + wide]) * inverse_count
    sums[:, : cols - width] = col_sum(gathered_f32[:, width:]) * inverse_count
    for row in range(extra):
        at = cols - width + row * cols
        part = min(cols, sums.shape[1] - at)
        sums[:, at : at + part] = biases[row : row + 1, :part] * inverse_count


def core_sum_kernel(slots, count, *refs):
    keeps, recvs, outs = refs[:count], refs[count : 2 * count], refs[2 * count :]
    for (first, number), out in zip(slots, outs):
        for slot in range(number):
            at = 0
            for keep, recv in zip(keeps, recvs):
                wide = keep.shape[-1]
                total = keep[first + slot].astype(F32) + recv[first + slot].astype(F32)
                out[slot, :, at : at + wide] = total.astype(BF)
                at += wide


def split_sum_kernel(mine, other, keep, send):
    keep[...] = (mine[0].astype(F32) + other[0].astype(F32)).astype(BF)
    send[...] = (mine[1].astype(F32) + other[1].astype(F32)).astype(BF)


def row_split_kernel(*refs):
    idx, terms, keep, send, halves = refs[0], refs[1:-3], refs[-3], refs[-2], refs[-1]
    total = terms[0][...].astype(F32)
    for term in terms[1:]:
        total = total + term[...].astype(F32)
    half = halves.shape[1]
    for side in range(2):
        halves[side] = total[side * half : (side + 1) * half].astype(BF)
    mine = idx[1] % 2
    keep[...] = halves[mine]
    send[...] = halves[1 - mine]


def sum_kernel(*refs):
    total = refs[0][...].astype(F32)
    for term in refs[1:-1]:
        total = total + term[...].astype(F32)
    refs[-1][...] = total.astype(BF).reshape(refs[-1].shape)


def finish_kernel(rows, plan, factor, *refs):
    idx = refs[0]
    terms = list(refs[1 : 1 + sum(2 * parts for _, parts in plan)])
    at = 1 + len(terms)
    g_qkv, g_proj, g_fc1, g_fc2 = refs[at : at + 4]
    scratch = refs[at + 4 :]
    width = g_proj.shape[-1]
    hidden = g_fc1.shape[-1]
    for (members, parts), halves in zip(plan, scratch):
        for core in (idx[2], 1 - idx[2]):
            if parts == 1:
                halves[core] = terms.pop(0)[...]
            else:
                size = terms[0].shape[0]
                for side in (idx[1] % 2, 1 - idx[1] % 2):
                    halves[core, block_at(side * size, size), :] = terms.pop(0)[...]
        for kind, layer, skip in members:
            if kind == "qkv":
                first = halves[0, :, skip : skip + 2 * width]
                g_qkv[layer, :, : 2 * width] = first.astype(F32) * factor
                second = halves[1, :, skip : skip + 2 * width].astype(F32) * factor
                g_qkv[layer, :, 2 * width :] = second[:, :width]
                g_proj[layer] = second[:, width:]
            else:
                g_fc1[layer] = halves[0, :, skip : skip + hidden].astype(F32) * factor
                for part in range(hidden // width):
                    at = skip + part * width
                    g_fc2[layer, part * rows : (part + 1) * rows] = (
                        halves[1, :, at : at + width].astype(F32) * factor
                    )


def shards(
    latents, condition, cotangent, w_qkv, b_qv, w_proj, b_proj, w_fc1, b_fc1, w_fc2, b_fc2, w_ada,
    b_ada,
):
    layers, rows, _ = w_qkv.shape
    width = w_proj.shape[-1]
    hidden = w_fc1.shape[-1]
    wide = w_ada.shape[-1]
    seq = latents.shape[1]
    n_shard = lax.axis_size("shard")
    n_rep = lax.axis_size("rep")
    levels = n_rep // CORES
    shard_id = lax.axis_index("shard")
    rep_id = lax.axis_index("rep")
    core = rep_id % CORES
    idx = jnp.stack([shard_id, rep_id // CORES, core]).astype(jnp.int32)
    total_latents = latents.shape[0] * n_shard * n_rep
    factor = 1.0 / total_latents

    def exchange(array, by_shard=0, by_level=0, by_core=0, turn=None):
        moves = []
        for own_shard in range(n_shard):
            for own_rep in range(n_rep):
                mask = turn[own_rep % CORES] if turn else by_shard
                peer = (own_shard ^ mask) * n_rep + (own_rep ^ (by_level * CORES + by_core))
                moves.append((own_shard * n_rep + own_rep, peer))
        return lax.ppermute(array, ("shard", "rep"), moves)

    def after(array, *earlier):
        return lax.optimization_barrier((array,) + earlier)[0]

    relay = n_shard == 4
    first_turn, second_turn = (1, 2), (2, 1)

    half_wide = {"qkv": 2 * width, "mlp": hidden}
    copy_total = {"qkv": 3, "mlp": 1 + hidden // width}

    def pack(*plan):
        whole = run(
            functools.partial(pack_kernel, plan), "pack",
            [(array, "h") for array in (w_qkv, w_proj, w_fc1, w_fc2)],
            [((rows, 2 * sum(half_wide[kind] for kind in kinds)), BF, "v") for _, kinds in plan],
            [pltpu.SemaphoreType.DMA((sum(copy_total[kind] for _, ks in plan for kind in ks),))],
        )
        if relay:
            return whole
        return [
            lax.dynamic_slice_in_dim(array, core * (array.shape[1] // 2), array.shape[1] // 2, 1)
            for array in whole
        ]

    def near_first(packed):
        if relay:
            return [exchange(packed, turn=first_turn)]
        return [exchange(packed, by_shard=step) for step in range(1, n_shard)]

    def near_half(near, *earlier):
        source = after(near[0], *earlier) if earlier else near[0]
        if not relay:
            return source
        half = source.shape[1] // 2
        return run(
            half_kernel, "half", [(idx, "s"), (source, "a")],
            [((source.shape[0], half), BF, "a")], [pltpu.SemaphoreType.DMA((1,))],
        )[0]

    def near_second(near, part):
        return near + [exchange(part, turn=second_turn)] if relay else near

    def far_of(near, *earlier):
        return [exchange(after(piece, *earlier) if earlier else piece, by_core=1) for piece in near]

    conditions = [condition] + [exchange(condition, by_shard=step) for step in range(1, n_shard)]
    packed = [pack((layer, ("qkv", "mlp")))[0] for layer in range(layers)]
    near = [near_first(packed[0])]
    near += [near_first(after(own, *conditions[1:])) for own in packed[1:]]
    pad_scratch = [pltpu.VMEM((width, layers * wide), BF), pltpu.SemaphoreType.DMA((layers,))]
    span = wide + 4 * width + hidden
    partial = run(
        functools.partial(modulate_kernel, n_shard), "modulate",
        [(idx, "s"), (w_ada, "a"), (b_ada, "k"), (b_qv, "k"), (b_proj, "k"), (b_fc1, "k"),
         (b_fc2, "k"), (conditions[0], "k")] + [(array, "v") for array in conditions[1:]],
        [((layers, span), F32, "v")] * n_shard, pad_scratch, flops=10**7,
    )
    parts = [near_half(near[0], partial[0])]
    mod_all = partial[0]
    for step in range(1, n_shard):
        mod_all = mod_all + exchange(after(partial[step], parts[0]), by_shard=step)
    for own in near[1:]:
        parts.append(near_half(own, mod_all))
    near = [near_second(own, part) for own, part in zip(near, parts)]
    mod_all = after(mod_all, *parts[1:])
    pieces = {0: (near[0], far_of(near[0]))}

    big = seq * width
    row = lambda kind="v": ((seq, width), F32, kind)
    vec_wide = {"qkv": 6 * width, "mlp": 4 * width + hidden}

    def piece_args(pair):
        return [(array, "a") for array in pair[0] + pair[1]]

    copy_count = 6 if relay else 2 * (n_shard - 1)
    qkv_sems = pltpu.SemaphoreType.DMA((3 + copy_count,))
    mlp_sems = pltpu.SemaphoreType.DMA((1 + hidden // width + copy_count,))
    out_sems = pltpu.SemaphoreType.DMA((2 * n_shard,))
    w_qkv_all = pltpu.VMEM((2, width, 2 * width), BF)
    w_mlp_all = pltpu.VMEM((2, width, hidden), BF)

    def grads_out(kind):
        return [((n_shard, rows, half_wide[kind]), BF, "a")] * 2

    stream = latents[0]
    saved = []
    vecs, raw = {}, {}
    for layer in range(layers):
        pair, offset = pieces[layer], 0
        keep_in = "v" if layer + 1 == layers else "k"
        qkv, probs, attended, branch, middle = run(
            functools.partial(attention_forward, layer, rows, offset, n_shard), "attention_forward",
            [(idx, "s"), (stream, "v"), (mod_all, "v"), (w_qkv, "a"), (w_proj, "a")]
            + piece_args(pair),
            [((seq, 3 * width), BF, keep_in), ((HEADS, seq, seq), F32, keep_in),
             ((seq, width), BF, keep_in), row(keep_in), row()],
            [w_qkv_all, qkv_sems], flops=10 * big * width,
        )
        pair, offset = pieces[layer], 2 * width
        entry = dict(stream=stream, qkv=qkv, probs=probs, attended=attended, branch=branch,
                     middle=middle)
        if layer + 1 < layers:
            act_low, slopes, mlp_out, stream = run(
                functools.partial(mlp_forward, layer, rows, offset, n_shard), "mlp_forward",
                [(idx, "s"), (middle, "v"), (mod_all, "v"), (w_fc1, "a"), (w_fc2, "a")]
                + piece_args(pair),
                [((seq, hidden), BF, keep_in), ((seq, hidden), F32, keep_in), row(keep_in), row()],
                [w_mlp_all, mlp_sems], flops=16 * big * width,
            )
            entry.update(act_low=act_low, slopes=slopes, mlp_out=mlp_out)
            pieces[layer + 1] = (near[layer + 1], far_of(near[layer + 1], middle))
        else:
            x_out, d_middle, vecs["mlp", layer], *raw["mlp", layer] = run(
                functools.partial(mlp_both, layer, rows, offset, n_shard), "mlp_both",
                [(idx, "s"), (middle, "v"), (mod_all, "v"), (cotangent[0], "v"), (w_fc1, "a"),
                 (w_fc2, "a")] + piece_args(pair),
                [((seq, width), BF, "v"), row(), ((1, vec_wide["mlp"]), F32, "v")]
                + grads_out("mlp"),
                [w_mlp_all, w_mlp_all, pltpu.VMEM((seq, hidden), BF),
                 pltpu.VMEM((seq, hidden), F32), mlp_sems, out_sems], flops=48 * big * width,
            )
        saved.append(entry)

    def core_sum(keys, *earlier):
        keeps = [raw[key][0] for key in keys]
        received = [exchange(raw[key][1], by_core=1) for key in keys]
        if earlier:
            keeps[0] = after(keeps[0], *earlier)
        total_wide = sum(keep.shape[-1] for keep in keeps)
        slots = [(0, 2), (2, 2)] if relay else [(slot, 1) for slot in range(n_shard)]
        return run(
            functools.partial(core_sum_kernel, slots, len(keys)), "core_sum",
            [(array, "v") for array in keeps + received],
            [((number, rows, total_wide), BF, "v") for _, number in slots],
        )

    def shard_send(summed):
        if relay:
            return [exchange(summed[1], turn=first_turn)]
        return [exchange(summed[step], by_shard=step) for step in range(1, n_shard)]

    def add(terms, shape):
        return run(sum_kernel, "add", [(array, "v") for array in terms], [(shape, BF, "v")])[0]

    def shard_second(summed, arrived, *earlier):
        shape = summed[0].shape[1:]
        mine = after(summed[0], *earlier) if earlier else summed[0]
        if not relay:
            return [mine.reshape(shape)] + [array.reshape(shape) for array in arrived]
        keep, send = run(
            split_sum_kernel, "split_sum", [(mine, "v"), (arrived[0], "v")], [(shape, BF, "v")] * 2
        )
        return [keep, exchange(send, turn=second_turn)]

    def level_first(terms, halve, *earlier):
        shape = terms[0].shape
        if earlier:
            terms = [after(terms[0], *earlier)] + terms[1:]
        if not halve or shape[0] % 32:
            total = add(terms, shape)
            return False, total, exchange(total, by_level=1)
        part = (shape[0] // 2, shape[1])
        keep, send = run(
            row_split_kernel, "row_split",
            [(idx, "s")] + [(array, "v") for array in terms],
            [(part, BF, "v")] * 2, [pltpu.VMEM((2,) + part, BF)],
        )
        return True, keep, exchange(send, by_level=1)

    def level_second(first, *earlier):
        halved, kept, arriving = first
        if earlier:
            kept = after(kept, *earlier)
        return halved, add([kept, arriving], kept.shape)

    def level_last(halved, total, step):
        while step < levels:
            total = add([total, exchange(total, by_level=step)], total.shape)
            step *= 2
        near = [total, exchange(total, by_level=1)] if halved else [total]
        return near + far_of(near)

    waiting = []
    for layer in reversed(range(layers)):
        entry = saved[layer]
        pair, offset = pieces[layer], 2 * width
        if layer + 1 < layers:
            keys = [("qkv", layer + 1), ("mlp", layer + 1)]
            summed = core_sum(keys, grad_stream)
            waiting.append((keys, summed, shard_send(summed)))
            grad_stream = after(grad_stream, summed[0])
            d_middle, vecs["mlp", layer], *raw["mlp", layer] = run(
                functools.partial(mlp_backward, layer, rows, offset, n_shard), "mlp_backward",
                [(idx, "s"), (entry["middle"], "v"), (mod_all, "v"), (grad_stream, "v"),
                 (entry["act_low"], "v"), (entry["slopes"], "v"), (entry["mlp_out"], "v"),
                 (w_fc1, "a"), (w_fc2, "a")] + piece_args(pair),
                [row(), ((1, vec_wide["mlp"]), F32, "v")] + grads_out("mlp"),
                [w_mlp_all, w_mlp_all, mlp_sems, out_sems], flops=32 * big * width,
            )
            core_mlp = core_sum([("mlp", layer)], d_middle)
            sent_mlp = shard_send(core_mlp)
            d_middle = after(d_middle, core_mlp[0])
        pair, offset = pieces[layer], 0
        grad_stream, vecs["qkv", layer], *raw["qkv", layer] = run(
            functools.partial(attention_backward, layer, rows, offset, n_shard),
            "attention_backward",
            [(idx, "s"), (entry["stream"], "v"), (mod_all, "v"), (d_middle, "v"),
             (entry["qkv"], "v"), (entry["probs"], "v"), (entry["attended"], "v"),
             (entry["branch"], "v"), (w_qkv, "a"), (w_proj, "a")] + piece_args(pair),
            [row(), ((1, vec_wide["qkv"]), F32, "v")] + grads_out("qkv"),
            [w_qkv_all, pltpu.VMEM((seq, 3 * width), BF), w_qkv_all, qkv_sems, out_sems],
            flops=28 * big * width,
        )
    cond_in = condition.astype(F32)
    vector = [jax.nn.silu(cond_in).astype(BF)]
    for layer in range(layers):
        vector += [vecs[kind, layer][:, : 3 * width].astype(BF) for kind in ("qkv", "mlp")]
    for layer in range(layers):
        vector += [vecs[kind, layer][:, 3 * width :].astype(BF) for kind in ("qkv", "mlp")]
    vector = jnp.concatenate(vector, axis=1)
    length = vector.shape[1]
    masks = [first_turn, second_turn] if relay else []
    while not relay and 2 ** len(masks) < n_shard:
        masks.append((2 ** len(masks),) * 2)

    cols = width + layers * wide
    extra = -(-(length - cols) // cols)

    def stack(first, second, extra=0):
        shape = (2 * first.shape[0] - extra, first.shape[1])
        return run(
            functools.partial(stack_kernel, extra), "stack", [(first, "v"), (second, "v")],
            [(shape, BF, "v")], [pltpu.VMEM(shape, F32)],
        )[0]

    (keys_first, core_first, sent_first), = waiting
    plan = [keys_first, [("mlp", 0)], [("qkv", 0)]]
    a = shard_second(core_first, sent_first, grad_stream)
    core_qkv = core_sum(plan[2], a[0])
    sent_qkv = shard_send(core_qkv)
    b = shard_second(core_mlp, sent_mlp, core_qkv[0])
    a = level_first(a, True, b[0])
    c = shard_second(core_qkv, sent_qkv, a[1])
    vector = after(vector, b[0])
    for mask in masks[:-2]:
        vector = stack(vector, exchange(vector, turn=mask))
    arriving = exchange(vector, turn=masks[-2])
    vector = stack(after(vector, c[0]), arriving)
    arriving = exchange(vector, turn=masks[-1])
    b = level_first(b, True, vector)
    a = level_second(a, b[1])
    a_moving = exchange(a[1], by_level=2)
    c = level_first(c, False, a[1])
    grad_cond, passed, stacked = run(
        group_kernel, "group",
        [(idx, "s"), (w_ada, "a"), (after(vector, c[1]), "v"), (arriving, "v")],
        [((n_shard // 2, width), F32, "v")] * 2 + [((n_shard + extra, cols), BF, "v")],
        [pltpu.VMEM((n_shard, length), F32), pltpu.VMEM((n_shard + extra, cols), F32)]
        + pad_scratch, flops=10**7,
    )
    arriving = exchange(stacked, by_level=1)
    b = level_second(b, stacked)
    b_moving = exchange(b[1], by_level=2)
    c = level_second(c, b[1])
    c_moving = exchange(c[1], by_level=2)
    stacked = stack(after(stacked, c[1]), arriving, extra)
    step = 2
    while 2 * step < levels:
        stacked = stack(stacked, exchange(stacked, by_level=step), extra)
        step *= 2
    arriving = exchange(stacked, by_level=step)
    a = (a[0], add([after(a[1], stacked), a_moving], a[1].shape))
    a_parts = level_last(*a, 4)
    b = (b[0], add([after(b[1], a[1]), b_moving], b[1].shape))
    b_parts = level_last(*b, 4)
    grad_cond = grad_cond + exchange(passed, turn=masks[-1])
    for mask in masks[-2::-1]:
        half = grad_cond.shape[0] // 2
        grad_cond = grad_cond[:half] + exchange(grad_cond[half:], turn=mask)
    cond_grad = jax.vjp(jax.nn.silu, cond_in)[1](grad_cond)[0]
    stacks = [after(stacked, b[1]), arriving]
    stacks = stacks + far_of(stacks)
    grad_ada, sums = run(
        functools.partial(ada_grad_kernel, rows, wide, extra, factor), "ada_grad",
        [(idx, "s")] + [(array, "v") for array in stacks],
        [((layers, rows, wide), F32, "v"), ((1, length - width), F32, "v")],
        [pltpu.VMEM((width, total_latents), F32), pltpu.VMEM((total_latents, cols), F32)],
        flops=10**8,
    )

    c = (c[0], add([after(c[1], sums), c_moving], c[1].shape))
    finals = [a_parts, b_parts, level_last(*c, 4)]

    def own_part(parts):
        whole = jnp.concatenate(parts, axis=0)
        length = whole.shape[1] // n_shard
        return lax.dynamic_slice_in_dim(whole, shard_id * length, length, axis=1)

    base = layers * wide
    at = [base + layer * (4 * width + hidden) for layer in range(layers)]
    grad_ada_bias = own_part([sums[:, layer * wide : (layer + 1) * wide] for layer in range(layers)])
    grad_qv_bias = own_part([sums[:, a : a + 2 * width] for a in at])
    grad_proj_bias = own_part([sums[:, a + 2 * width : a + 3 * width] for a in at])
    grad_fc1_bias = own_part([sums[:, a + 3 * width : a + 3 * width + hidden] for a in at])
    grad_fc2_bias = own_part([sums[:, a + 3 * width + hidden : a + 4 * width + hidden] for a in at])

    finish_plan, finish_inputs, finish_scratch = [], [(idx, "s")], []
    for keys, parts in zip(plan, finals):
        members, skip = [], 0
        for kind, layer in keys:
            members.append((kind, layer, skip))
            skip += half_wide[kind]
        finish_plan.append((members, len(parts) // 2))
        finish_inputs += [(array, "v") for array in parts]
        finish_scratch.append(pltpu.VMEM((2, rows, skip), BF))
    grad_qkv, grad_proj, grad_fc1, grad_fc2 = run(
        functools.partial(finish_kernel, rows, finish_plan, factor), "finish",
        finish_inputs,
        [(array.shape, F32, "v") for array in (w_qkv, w_proj, w_fc1, w_fc2)],
        finish_scratch,
    )
    return (
        x_out[None], grad_stream[None], cond_grad, grad_qkv, grad_qv_bias, grad_proj,
        grad_proj_bias, grad_fc1, grad_fc1_bias, grad_fc2, grad_fc2_bias, grad_ada, grad_ada_bias,
    )


def solution(mesh):
    rows3, rows2 = P(("shard", "rep"), None, None), P(("shard", "rep"), None)
    weight, bias = P(None, "shard", None), P(None, "shard")
    return jax.shard_map(
        shards,
        mesh=mesh,
        in_specs=(rows3, rows2, rows3) + (weight, bias) * 5,
        out_specs=(rows3, rows3, rows2) + (weight, bias) * 5,
        check_vma=False,
    )
```

```python
import functools

import jax
import jax.numpy as jnp
from jax import lax
from jax.experimental import pallas as pl
from jax.experimental.pallas import tpu as pltpu
from jax.sharding import PartitionSpec as P

HEADS = 6
BF = jnp.bfloat16
F32 = jnp.float32
CORES = 2
VMEM_LIMIT = 40 * 1024 * 1024


def dot(left, right):
    return jnp.dot(left, right, preferred_element_type=F32)


def dot_nt(left, right):
    return lax.dot_general(left, right, (((1,), (1,)), ((), ())), preferred_element_type=F32)


def dot_tn(left, right):
    return lax.dot_general(left, right, (((0,), (0,)), ((), ())), preferred_element_type=F32)


def layer_norm(rows):
    center = rows - jnp.mean(rows, axis=-1, keepdims=True)
    inverse = lax.rsqrt(jnp.mean(center * center, axis=-1, keepdims=True) + 1e-06)
    return center * inverse, inverse


def norm_back(grad_norm, normed, inverse):
    centered = grad_norm - jnp.mean(grad_norm, axis=-1, keepdims=True)
    return inverse * (centered - normed * jnp.mean(grad_norm * normed, axis=-1, keepdims=True))


def col_sum(rows):
    return jnp.sum(rows, axis=0, keepdims=True)


def block_at(start, size):
    return pl.ds(pl.multiple_of(start, size), size)


def start_all(copies):
    for copy in copies:
        copy.start()


def wait_all(copies):
    for copy in copies:
        copy.wait()


def make_copies(pairs, sems):
    return [
        pltpu.make_async_copy(source, target, sems.at[slot])
        for slot, (source, target) in enumerate(pairs)
    ]


def run(body, name, inputs, outputs, scratch=(), flops=0):
    places = {"v": pltpu.VMEM, "k": pltpu.VMEM, "a": pl.ANY, "h": pl.ANY, "s": pltpu.SMEM}
    arrays = [
        pltpu.with_memory_space_constraint(arr, pltpu.HBM) if kind in "hk" else arr
        for arr, kind in inputs
    ]
    return pl.pallas_call(
        body,
        out_shape=[
            pltpu.HBM(shape, dtype) if kind in "hk" else jax.ShapeDtypeStruct(shape, dtype)
            for shape, dtype, kind in outputs
        ],
        in_specs=[pl.BlockSpec(memory_space=places[kind]) for _, kind in inputs],
        out_specs=[pl.BlockSpec(memory_space=places[kind]) for _, _, kind in outputs],
        scratch_shapes=list(scratch),
        compiler_params=pltpu.CompilerParams(vmem_limit_bytes=VMEM_LIMIT),
        cost_estimate=pl.CostEstimate(flops=1, bytes_accessed=1, transcendentals=0),
        name=name,
    )(*arrays)


def pack_kernel(plan, *refs):
    w_qkv, w_proj, w_fc1, w_fc2 = refs[:4]
    outs, sems = refs[4:-1], refs[-1]
    rows, width = w_proj.shape[1:]
    hidden = w_fc1.shape[-1]
    pairs = []
    for (layer, kinds), out in zip(plan, outs):
        at = 0
        pieces = {"qkv": [w_qkv.at[layer, :, : 2 * width]], "mlp": [w_fc1.at[layer]]}
        second = {
            "qkv": [w_qkv.at[layer, :, 2 * width :], w_proj.at[layer]],
            "mlp": [
                w_fc2.at[layer, part * rows : (part + 1) * rows]
                for part in range(hidden // width)
            ],
        }
        for half in (pieces, second):
            for kind in kinds:
                for piece in half[kind]:
                    pairs.append((piece, out.at[:, at : at + piece.shape[-1]]))
                    at += piece.shape[-1]
    copies = make_copies(pairs, sems)
    start_all(copies)
    wait_all(copies)


def half_kernel(idx, whole, out, sems):
    half = out.shape[1]
    copies = make_copies([(whole.at[:, block_at(idx[2] * half, half)], out)], sems)
    start_all(copies)
    wait_all(copies)


def piece_count(shards):
    return 2 if shards == 4 else shards - 1


def peer_order(shards, core):
    if shards != 4:
        return list(range(shards))
    return [0, 2 - core, 1 + core, 3]


def qkv_pairs(idx, layer, rows, offset, w_qkv, w_proj, near, far, w_all):
    width = w_proj.shape[-1]
    own = block_at(idx[0] * rows, rows)
    pairs = [
        (w_qkv.at[layer, :, : 2 * width], w_all.at[0, own, :]),
        (w_qkv.at[layer, :, 2 * width :], w_all.at[1, own, :width]),
        (w_proj.at[layer], w_all.at[1, own, width:]),
    ]
    return pairs + piece_pairs(idx, rows, offset, 2 * width, near, far, w_all)


def mlp_pairs(idx, layer, rows, offset, w_fc1, w_fc2, near, far, w_all):
    width = w_fc2.shape[-1]
    hidden = w_fc1.shape[-1]
    own = block_at(idx[0] * rows, rows)
    pairs = [(w_fc1.at[layer], w_all.at[0, own, :])]
    for part in range(hidden // width):
        pairs.append(
            (
                w_fc2.at[layer, part * rows : (part + 1) * rows, :],
                w_all.at[1, own, part * width : (part + 1) * width],
            )
        )
    return pairs + piece_pairs(idx, rows, offset, hidden, near, far, w_all)


def piece_pairs(idx, rows, offset, wide, near, far, w_all):
    pairs = []
    shards = w_all.shape[1] // rows
    for pieces, core in ((near, idx[2]), (far, 1 - idx[2])):
        for slot, piece in enumerate(pieces):
            if shards != 4:
                mask, halves = slot + 1, [(core, 0)]
            elif slot == 0:
                mask, halves = 1 + core, [(0, 0), (1, piece.shape[1] // 2)]
            else:
                mask, halves = 3, [(core, 0)]
            place = block_at(jnp.bitwise_xor(idx[0], mask) * rows, rows)
            for half, first in halves:
                at = first + offset
                pairs.append((piece.at[:, at : at + wide], w_all.at[half, place, :]))
    return pairs


def grad_pairs(idx, rows, shards, grad_all, keep, send):
    pairs = []
    for slot in range(shards):
        for target, core in ((keep, idx[2]), (send, 1 - idx[2])):
            mask = peer_order(shards, core)[slot]
            place = block_at(jnp.bitwise_xor(idx[0], mask) * rows, rows)
            pairs.append((grad_all.at[core, place, :], target.at[slot]))
    return pairs


def fc2_chunk(w_all, rows, chunk):
    width = w_all.shape[1]
    parts = w_all.shape[2] // width
    blocks = []
    for number in range(chunk * width // rows, (chunk + 1) * width // rows):
        at, part = number // parts, number % parts
        blocks.append(w_all[1, at * rows : (at + 1) * rows, part * width : (part + 1) * width])
    return jnp.concatenate(blocks, axis=0)


def attention_forward(layer, rows, offset, shards, *refs):
    peers = piece_count(shards)
    idx, stream, mod_all, w_qkv, w_proj = refs[:5]
    near, far = refs[5 : 5 + peers], refs[5 + peers : 5 + 2 * peers]
    qkv_out, probs_out, attended_out, branch_out, middle_out, w_all, sems = refs[5 + 2 * peers :]
    mod = mod_all.at[layer : layer + 1]
    copies = make_copies(
        qkv_pairs(idx, layer, rows, offset, w_qkv, w_proj, near, far, w_all), sems
    )
    start_all(copies)
    width = stream.shape[-1]
    head = width // HEADS
    b_qv, b_proj = mod[:, 6 * width : 8 * width], mod[:, 8 * width : 9 * width]
    values = stream[...].astype(F32)
    shift, scale, gate = (mod[:, part * width : (part + 1) * width] for part in range(3))
    normed, _ = layer_norm(values)
    h_one = (normed * (1.0 + scale) + shift).astype(BF)
    wait_all(copies)
    mixed = dot(h_one, w_all[0])
    qkv_out[:, :width] = (mixed[:, :width] + b_qv[:, :width]).astype(BF)
    qkv_out[:, width : 2 * width] = mixed[:, width:].astype(BF)
    qkv_out[:, 2 * width :] = (dot(h_one, w_all[1, :, :width]) + b_qv[:, width:]).astype(BF)
    lane = lax.broadcasted_iota(jnp.int32, (1, 2 * head), 1)
    masks = [(lane < head).astype(BF), (lane >= head).astype(BF)]
    for pair in range(HEADS // 2):
        at = pair * 2 * head
        queries = qkv_out[:, at : at + 2 * head]
        keys = qkv_out[:, width + at : width + at + 2 * head]
        vals = qkv_out[:, 2 * width + at : 2 * width + at + 2 * head]
        attended = 0.0
        for side in range(2):
            scores = dot_nt(queries, keys * masks[side]) * head ** (-0.5)
            raised = jnp.exp(scores - jnp.max(scores, axis=-1, keepdims=True))
            probs = raised * (1.0 / jnp.sum(raised, axis=-1, keepdims=True))
            probs_out[2 * pair + side] = probs
            attended = attended + dot(probs.astype(BF), vals * masks[side])
        attended_out[:, at : at + 2 * head] = attended.astype(BF)
    branch = dot(attended_out[...], w_all[1, :, width:]) + b_proj
    branch_out[...] = branch
    middle_out[...] = values + gate * branch


def attention_backward(layer, rows, offset, shards, *refs):
    peers = piece_count(shards)
    idx, stream, mod_all, d_middle_in, qkv, probs_in, attended, branch, w_qkv, w_proj = refs[:10]
    near, far = refs[10 : 10 + peers], refs[10 + peers : 10 + 2 * peers]
    d_stream, vec, keep, send, w_all, d_qkv, grad_all, sems, out_sems = refs[10 + 2 * peers :]
    mod = mod_all.at[layer : layer + 1]
    copies = make_copies(
        qkv_pairs(idx, layer, rows, offset, w_qkv, w_proj, near, far, w_all), sems
    )
    start_all(copies)
    width = stream.shape[-1]
    head = width // HEADS
    root = head ** (-0.5)
    shift, scale, gate = (mod[:, part * width : (part + 1) * width] for part in range(3))
    normed, inverse = layer_norm(stream[...].astype(F32))
    h_one = (normed * (1.0 + scale) + shift).astype(BF)
    d_middle = d_middle_in[...]
    vec[:, 2 * width : 3 * width] = col_sum(d_middle * branch[...])
    d_branch = (d_middle * gate).astype(BF)
    grad_all[1, :, width:] = dot_tn(attended[...], d_branch).astype(BF)
    vec[:, 5 * width :] = col_sum(d_branch.astype(F32))
    wait_all(copies)
    d_attended = dot_nt(d_branch, w_all[1, :, width:]).astype(BF)
    lane = lax.broadcasted_iota(jnp.int32, (1, 2 * head), 1)
    masks = [(lane < head).astype(BF), (lane >= head).astype(BF)]
    for pair in range(HEADS // 2):
        at = pair * 2 * head
        queries = qkv[:, at : at + 2 * head]
        keys = qkv[:, width + at : width + at + 2 * head]
        vals = qkv[:, 2 * width + at : 2 * width + at + 2 * head]
        d_att = d_attended[:, at : at + 2 * head]
        d_queries, d_keys, d_values = 0.0, 0.0, 0.0
        for side in range(2):
            probs = probs_in[2 * pair + side]
            d_values = d_values + dot_tn(probs.astype(BF), d_att * masks[side])
            d_probs = dot_nt(d_att, vals * masks[side])
            inner = jnp.sum(probs * d_probs, axis=-1, keepdims=True)
            d_scores = (probs * (d_probs - inner)).astype(BF)
            d_queries = d_queries + dot(d_scores, keys * masks[side])
            d_keys = d_keys + dot_tn(d_scores, queries * masks[side])
        d_qkv[:, at : at + 2 * head] = (d_queries * root).astype(BF)
        d_qkv[:, width + at : width + at + 2 * head] = (d_keys * root).astype(BF)
        d_qkv[:, 2 * width + at : 2 * width + at + 2 * head] = d_values.astype(BF)
    d_qk, d_val = d_qkv[:, : 2 * width], d_qkv[:, 2 * width :]
    grad_all[0] = dot_tn(h_one, d_qk).astype(BF)
    grad_all[1, :, :width] = dot_tn(h_one, d_val).astype(BF)
    out_copies = make_copies(grad_pairs(idx, rows, shards, grad_all, keep, send), out_sems)
    start_all(out_copies)
    vec[:, 3 * width : 4 * width] = col_sum(d_qk[:, :width].astype(F32))
    vec[:, 4 * width : 5 * width] = col_sum(d_val.astype(F32))
    d_h_one = dot_nt(d_qk, w_all[0]) + dot_nt(d_val, w_all[1, :, :width])
    vec[:, :width] = col_sum(d_h_one)
    vec[:, width : 2 * width] = col_sum(d_h_one * normed)
    d_stream[...] = d_middle + norm_back(d_h_one * (1.0 + scale), normed, inverse)
    wait_all(out_copies)


def gelu_parts(pre_act):
    root = 0.7978845608028654
    square = pre_act * pre_act
    bent = jnp.tanh(root * pre_act * (1.0 + 0.044715 * square))
    half = 0.5 * (1.0 + bent)
    slope = half + 0.5 * pre_act * (1.0 - bent * bent) * (root * (1.0 + 3 * 0.044715 * square))
    return pre_act * half, slope


def mlp_vectors(mod_all, layer, width):
    mod = mod_all.at[layer : layer + 1]
    last = mod_all.shape[-1] - width
    return mod, mod[:, 9 * width : last], mod[:, last:]


def mlp_forward_part(rows, h_two, b_fc1, b_fc2, w_all, act_low, slopes):
    width = w_all.shape[1]
    mlp_out = b_fc2
    for chunk in range(w_all.shape[2] // width):
        cols = slice(chunk * width, (chunk + 1) * width)
        act, slope = gelu_parts(dot(h_two, w_all[0, :, cols]) + b_fc1[:, cols])
        act_low[:, cols] = act.astype(BF)
        slopes[:, cols] = slope
        mlp_out = mlp_out + dot(act_low[:, cols], fc2_chunk(w_all, rows, chunk))
    return mlp_out


def mlp_backward_part(
    idx, rows, shards, grad_out, mlp_out, middle, normed, inverse, h_two, scale, gate,
    w_all, act_low, slopes, vec, d_middle_out, grad_all, keep, send, out_sems,
):
    width = w_all.shape[1]
    parts = w_all.shape[2] // width
    vec[:, 2 * width : 3 * width] = col_sum(grad_out * mlp_out)
    d_mlp = (grad_out * gate).astype(BF)
    vec[:, (3 + parts) * width :] = col_sum(d_mlp.astype(F32))
    d_h_two = 0.0
    for chunk in range(parts):
        cols = slice(chunk * width, (chunk + 1) * width)
        d_act = dot_nt(d_mlp, fc2_chunk(w_all, rows, chunk))
        d_pre = (d_act * slopes[:, cols]).astype(BF)
        vec[:, (3 + chunk) * width : (4 + chunk) * width] = col_sum(d_pre.astype(F32))
        grad_all[0, :, cols] = dot_tn(h_two, d_pre).astype(BF)
        grad_fc2 = dot_tn(act_low[:, cols], d_mlp).astype(BF)
        first = chunk * width // rows
        for number in range(first, (chunk + 1) * width // rows):
            at, part = number // parts, number % parts
            grad_all[1, at * rows : (at + 1) * rows, part * width : (part + 1) * width] = grad_fc2[
                (number - first) * rows : (number - first + 1) * rows
            ]
        d_h_two = d_h_two + dot_nt(d_pre, w_all[0, :, cols])
    out_copies = make_copies(grad_pairs(idx, rows, shards, grad_all, keep, send), out_sems)
    start_all(out_copies)
    vec[:, :width] = col_sum(d_h_two)
    vec[:, width : 2 * width] = col_sum(d_h_two * normed)
    d_middle_out[...] = grad_out + norm_back(d_h_two * (1.0 + scale), normed, inverse)
    wait_all(out_copies)


def mlp_forward(layer, rows, offset, shards, *refs):
    peers = piece_count(shards)
    idx, middle, mod_all, w_fc1, w_fc2 = refs[:5]
    near, far = refs[5 : 5 + peers], refs[5 + peers : 5 + 2 * peers]
    act_low, slopes, mlp_out, stream_out, w_all, sems = refs[5 + 2 * peers :]
    mod, b_fc1, b_fc2 = mlp_vectors(mod_all, layer, middle.shape[-1])
    copies = make_copies(mlp_pairs(idx, layer, rows, offset, w_fc1, w_fc2, near, far, w_all), sems)
    start_all(copies)
    width = middle.shape[-1]
    shift, scale, gate = (mod[:, part * width : (part + 1) * width] for part in range(3, 6))
    normed, _ = layer_norm(middle[...])
    h_two = (normed * (1.0 + scale) + shift).astype(BF)
    wait_all(copies)
    mlp_out[...] = mlp_forward_part(rows, h_two, b_fc1, b_fc2, w_all, act_low, slopes)
    stream_out[...] = middle[...] + gate * mlp_out[...]


def mlp_backward(layer, rows, offset, shards, *refs):
    peers = piece_count(shards)
    idx, middle, mod_all, grad_out, act_low, slopes, mlp_out, w_fc1, w_fc2 = refs[:9]
    near, far = refs[9 : 9 + peers], refs[9 + peers : 9 + 2 * peers]
    d_middle, vec, keep, send, w_all, grad_all, sems, out_sems = refs[9 + 2 * peers :]
    mod = mod_all.at[layer : layer + 1]
    copies = make_copies(mlp_pairs(idx, layer, rows, offset, w_fc1, w_fc2, near, far, w_all), sems)
    start_all(copies)
    width = middle.shape[-1]
    shift, scale, gate = (mod[:, part * width : (part + 1) * width] for part in range(3, 6))
    normed, inverse = layer_norm(middle[...])
    h_two = (normed * (1.0 + scale) + shift).astype(BF)
    wait_all(copies)
    mlp_backward_part(
        idx, rows, shards, grad_out[...], mlp_out[...], middle, normed, inverse, h_two, scale,
        gate, w_all, act_low, slopes, vec, d_middle, grad_all, keep, send, out_sems,
    )


def mlp_both(layer, rows, offset, shards, *refs):
    peers = piece_count(shards)
    idx, middle, mod_all, cotangent, w_fc1, w_fc2 = refs[:6]
    near, far = refs[6 : 6 + peers], refs[6 + peers : 6 + 2 * peers]
    x_out, d_middle, vec, keep, send = refs[6 + 2 * peers : 11 + 2 * peers]
    w_all, grad_all, act_low, slopes, sems, out_sems = refs[11 + 2 * peers :]
    mod, b_fc1, b_fc2 = mlp_vectors(mod_all, layer, middle.shape[-1])
    copies = make_copies(mlp_pairs(idx, layer, rows, offset, w_fc1, w_fc2, near, far, w_all), sems)
    start_all(copies)
    width = middle.shape[-1]
    shift, scale, gate = (mod[:, part * width : (part + 1) * width] for part in range(3, 6))
    normed, inverse = layer_norm(middle[...])
    h_two = (normed * (1.0 + scale) + shift).astype(BF)
    wait_all(copies)
    mlp_out = mlp_forward_part(rows, h_two, b_fc1, b_fc2, w_all, act_low, slopes)
    x_out[...] = (middle[...] + gate * mlp_out).astype(BF)
    mlp_backward_part(
        idx, rows, shards, cotangent[...].astype(F32), mlp_out, middle, normed, inverse, h_two,
        scale, gate, w_all, act_low, slopes, vec, d_middle, grad_all, keep, send, out_sems,
    )


def padded_rows(idx, w_ada, w_pad, sems):
    layers, rows, wide = w_ada.shape
    w_pad[...] = jnp.zeros(w_pad.shape, BF)
    own = block_at(idx[0] * rows, rows)
    return make_copies(
        [
            (w_ada.at[layer], w_pad.at[own, layer * wide : (layer + 1) * wide])
            for layer in range(layers)
        ],
        sems,
    )


def modulate_kernel(shards, *refs):
    idx, w_ada, b_ada = refs[:3]
    biases, conditions = refs[3:7], refs[7 : 7 + shards]
    outs = refs[7 + shards : 7 + 2 * shards]
    w_pad, sems = refs[7 + 2 * shards :]
    copies = padded_rows(idx, w_ada, w_pad, sems)
    start_all(copies)
    layers = w_ada.shape[0]
    wide = w_ada.shape[2]
    acts = []
    for ref in conditions:
        cond = ref[...].astype(F32)
        acts.append(cond / (1.0 + jnp.exp(-cond)))
    acts = jnp.concatenate(acts, axis=0).astype(BF)

    def spread(bias):
        length = bias.shape[1]
        row = lax.broadcasted_iota(jnp.int32, (length, shards * length), 0)
        col = lax.broadcasted_iota(jnp.int32, (length, shards * length), 1)
        place = jnp.where(col - row == idx[0] * length, 1.0, 0.0).astype(BF)
        return dot(bias[...], place)

    first = spread(b_ada)
    at = wide
    for bias in biases:
        full = spread(bias)
        for out in outs:
            out[:, at : at + full.shape[1]] = full
        at += full.shape[1]
    wait_all(copies)
    for layer in range(layers):
        result = dot(acts, w_pad[:, layer * wide : (layer + 1) * wide]) + first[layer : layer + 1]
        for step in range(shards):
            outs[step][layer : layer + 1, :wide] = result[step : step + 1]


def stack_kernel(extra, first, second, out, rows_f32):
    size = first.shape[0] - extra
    rows_f32[:size] = first[:size].astype(F32)
    rows_f32[size : 2 * size] = second[:size].astype(F32)
    if extra:
        rows_f32[2 * size :] = first[size:].astype(F32) + second[size:].astype(F32)
    out[...] = rows_f32[...].astype(BF)


def group_kernel(idx, w_ada, first, second, keep, send, stacked, rows_f32, out_f32, w_pad, sems):
    copies = padded_rows(idx, w_ada, w_pad, sems)
    start_all(copies)
    width = w_pad.shape[0]
    size = first.shape[0]
    rows_f32[:size] = first[...].astype(F32)
    rows_f32[size:] = second[...].astype(F32)
    cols = stacked.shape[1]
    biases = col_sum(rows_f32[:, cols:])
    out_f32[...] = jnp.zeros(out_f32.shape, F32)
    out_f32[: 2 * size] = rows_f32[:, :cols]
    for row, at in enumerate(range(0, biases.shape[1], cols)):
        part = biases[:, at : at + cols]
        out_f32[2 * size + row : 2 * size + row + 1, : part.shape[1]] = part
    stacked[...] = out_f32[...].astype(BF)
    wait_all(copies)
    result = dot_nt(rows_f32[:, width:cols].astype(BF), w_pad[...])
    half = keep.shape[0]
    keep[...] = result[:half]
    send[...] = result[half:]


def ada_grad_kernel(rows, wide, extra, inverse_count, *refs):
    idx, stacks = refs[0], refs[1:-4]
    grad_ada, sums, turned, gathered_f32 = refs[-4:]
    layers = grad_ada.shape[0]
    width = turned.shape[0]
    size = stacks[0].shape[0] - extra
    cols = stacks[0].shape[1]
    biases = 0.0
    for number, stack in enumerate(stacks):
        gathered_f32[number * size : (number + 1) * size] = stack[:size].astype(F32)
        biases = biases + stack[size:].astype(F32)
    gathered = gathered_f32[...].astype(BF)
    turned[...] = gathered_f32[:, :width].T
    own = turned[block_at(idx[0] * rows, rows), :].astype(BF)
    for layer in range(layers):
        at = width + layer * wide
        grad_ada[layer] = dot(own, gathered[:, at : at + wide]) * inverse_count
    sums[:, : cols - width] = col_sum(gathered_f32[:, width:]) * inverse_count
    for row in range(extra):
        at = cols - width + row * cols
        part = min(cols, sums.shape[1] - at)
        sums[:, at : at + part] = biases[row : row + 1, :part] * inverse_count


def core_sum_kernel(slots, count, *refs):
    keeps, recvs, outs = refs[:count], refs[count : 2 * count], refs[2 * count :]
    for (first, number), out in zip(slots, outs):
        for slot in range(number):
            at = 0
            for keep, recv in zip(keeps, recvs):
                wide = keep.shape[-1]
                total = keep[first + slot].astype(F32) + recv[first + slot].astype(F32)
                out[slot, :, at : at + wide] = total.astype(BF)
                at += wide


def split_sum_kernel(mine, other, keep, send):
    keep[...] = (mine[0].astype(F32) + other[0].astype(F32)).astype(BF)
    send[...] = (mine[1].astype(F32) + other[1].astype(F32)).astype(BF)


def row_split_kernel(*refs):
    idx, terms, keep, send, halves = refs[0], refs[1:-3], refs[-3], refs[-2], refs[-1]
    total = terms[0][...].astype(F32)
    for term in terms[1:]:
        total = total + term[...].astype(F32)
    half = halves.shape[1]
    for side in range(2):
        halves[side] = total[side * half : (side + 1) * half].astype(BF)
    mine = idx[1] % 2
    keep[...] = halves[mine]
    send[...] = halves[1 - mine]


def sum_kernel(*refs):
    total = refs[0][...].astype(F32)
    for term in refs[1:-1]:
        total = total + term[...].astype(F32)
    refs[-1][...] = total.astype(BF).reshape(refs[-1].shape)


def finish_kernel(rows, plan, factor, *refs):
    idx = refs[0]
    terms = list(refs[1 : 1 + sum(2 * parts for _, parts in plan)])
    at = 1 + len(terms)
    g_qkv, g_proj, g_fc1, g_fc2 = refs[at : at + 4]
    scratch = refs[at + 4 :]
    width = g_proj.shape[-1]
    hidden = g_fc1.shape[-1]
    for (members, parts), halves in zip(plan, scratch):
        for core in (idx[2], 1 - idx[2]):
            if parts == 1:
                halves[core] = terms.pop(0)[...]
            else:
                size = terms[0].shape[0]
                for side in (idx[1] % 2, 1 - idx[1] % 2):
                    halves[core, block_at(side * size, size), :] = terms.pop(0)[...]
        for kind, layer, skip in members:
            if kind == "qkv":
                first = halves[0, :, skip : skip + 2 * width]
                g_qkv[layer, :, : 2 * width] = first.astype(F32) * factor
                second = halves[1, :, skip : skip + 2 * width].astype(F32) * factor
                g_qkv[layer, :, 2 * width :] = second[:, :width]
                g_proj[layer] = second[:, width:]
            else:
                g_fc1[layer] = halves[0, :, skip : skip + hidden].astype(F32) * factor
                for part in range(hidden // width):
                    at = skip + part * width
                    g_fc2[layer, part * rows : (part + 1) * rows] = (
                        halves[1, :, at : at + width].astype(F32) * factor
                    )


def shards(
    latents, condition, cotangent, w_qkv, b_qv, w_proj, b_proj, w_fc1, b_fc1, w_fc2, b_fc2, w_ada,
    b_ada,
):
    layers, rows, _ = w_qkv.shape
    width = w_proj.shape[-1]
    hidden = w_fc1.shape[-1]
    wide = w_ada.shape[-1]
    seq = latents.shape[1]
    n_shard = lax.axis_size("shard")
    n_rep = lax.axis_size("rep")
    levels = n_rep // CORES
    shard_id = lax.axis_index("shard")
    rep_id = lax.axis_index("rep")
    core = rep_id % CORES
    idx = jnp.stack([shard_id, rep_id // CORES, core]).astype(jnp.int32)
    total_latents = latents.shape[0] * n_shard * n_rep
    factor = 1.0 / total_latents

    def exchange(array, by_shard=0, by_level=0, by_core=0, turn=None):
        moves = []
        for own_shard in range(n_shard):
            for own_rep in range(n_rep):
                mask = turn[own_rep % CORES] if turn else by_shard
                peer = (own_shard ^ mask) * n_rep + (own_rep ^ (by_level * CORES + by_core))
                moves.append((own_shard * n_rep + own_rep, peer))
        return lax.ppermute(array, ("shard", "rep"), moves)

    def after(array, *earlier):
        return lax.optimization_barrier((array,) + earlier)[0]

    relay = n_shard == 4
    first_turn, second_turn = (1, 2), (2, 1)

    half_wide = {"qkv": 2 * width, "mlp": hidden}
    copy_total = {"qkv": 3, "mlp": 1 + hidden // width}

    def pack(*plan):
        whole = run(
            functools.partial(pack_kernel, plan), "pack",
            [(array, "h") for array in (w_qkv, w_proj, w_fc1, w_fc2)],
            [((rows, 2 * sum(half_wide[kind] for kind in kinds)), BF, "v") for _, kinds in plan],
            [pltpu.SemaphoreType.DMA((sum(copy_total[kind] for _, ks in plan for kind in ks),))],
        )
        if relay:
            return whole
        return [
            lax.dynamic_slice_in_dim(array, core * (array.shape[1] // 2), array.shape[1] // 2, 1)
            for array in whole
        ]

    def near_first(packed):
        if relay:
            return [exchange(packed, turn=first_turn)]
        return [exchange(packed, by_shard=step) for step in range(1, n_shard)]

    def near_half(near, *earlier):
        source = after(near[0], *earlier) if earlier else near[0]
        if not relay:
            return source
        half = source.shape[1] // 2
        return run(
            half_kernel, "half", [(idx, "s"), (source, "a")],
            [((source.shape[0], half), BF, "a")], [pltpu.SemaphoreType.DMA((1,))],
        )[0]

    def near_second(near, part):
        return near + [exchange(part, turn=second_turn)] if relay else near

    def far_of(near, *earlier):
        return [exchange(after(piece, *earlier) if earlier else piece, by_core=1) for piece in near]

    conditions = [condition] + [exchange(condition, by_shard=step) for step in range(1, n_shard)]
    packed = [pack((layer, ("qkv", "mlp")))[0] for layer in range(layers)]
    near = [near_first(packed[0])]
    near += [near_first(after(own, *conditions[1:])) for own in packed[1:]]
    pad_scratch = [pltpu.VMEM((width, layers * wide), BF), pltpu.SemaphoreType.DMA((layers,))]
    span = wide + 4 * width + hidden
    partial = run(
        functools.partial(modulate_kernel, n_shard), "modulate",
        [(idx, "s"), (w_ada, "a"), (b_ada, "k"), (b_qv, "k"), (b_proj, "k"), (b_fc1, "k"),
         (b_fc2, "k"), (conditions[0], "k")] + [(array, "v") for array in conditions[1:]],
        [((layers, span), F32, "v")] * n_shard, pad_scratch, flops=10**7,
    )
    parts = [near_half(near[0], partial[0])]
    mod_all = partial[0]
    for step in range(1, n_shard):
        mod_all = mod_all + exchange(after(partial[step], parts[0]), by_shard=step)
    for own in near[1:]:
        parts.append(near_half(own, mod_all))
    near = [near_second(own, part) for own, part in zip(near, parts)]
    pieces = {0: (near[0], far_of(near[0]))}

    big = seq * width
    row = lambda kind="v": ((seq, width), F32, kind)
    vec_wide = {"qkv": 6 * width, "mlp": 4 * width + hidden}

    def piece_args(pair):
        return [(array, "a") for array in pair[0] + pair[1]]

    copy_count = 6 if relay else 2 * (n_shard - 1)
    qkv_sems = pltpu.SemaphoreType.DMA((3 + copy_count,))
    mlp_sems = pltpu.SemaphoreType.DMA((1 + hidden // width + copy_count,))
    out_sems = pltpu.SemaphoreType.DMA((2 * n_shard,))
    w_qkv_all = pltpu.VMEM((2, width, 2 * width), BF)
    w_mlp_all = pltpu.VMEM((2, width, hidden), BF)

    def grads_out(kind):
        return [((n_shard, rows, half_wide[kind]), BF, "a")] * 2

    stream = latents[0]
    saved = []
    vecs, raw = {}, {}
    for layer in range(layers):
        pair, offset = pieces[layer], 0
        keep_in = "v" if layer + 1 == layers else "k"
        qkv, probs, attended, branch, middle = run(
            functools.partial(attention_forward, layer, rows, offset, n_shard), "attention_forward",
            [(idx, "s"), (stream, "v"), (mod_all, "v"), (w_qkv, "a"), (w_proj, "a")]
            + piece_args(pair),
            [((seq, 3 * width), BF, keep_in), ((HEADS, seq, seq), F32, keep_in),
             ((seq, width), BF, keep_in), row(keep_in), row()],
            [w_qkv_all, qkv_sems], flops=10 * big * width,
        )
        pair, offset = pieces[layer], 2 * width
        if layer == 0:
            middle = after(middle, *parts[1:])
        entry = dict(stream=stream, qkv=qkv, probs=probs, attended=attended, branch=branch,
                     middle=middle)
        if layer + 1 < layers:
            act_low, slopes, mlp_out, stream = run(
                functools.partial(mlp_forward, layer, rows, offset, n_shard), "mlp_forward",
                [(idx, "s"), (middle, "v"), (mod_all, "v"), (w_fc1, "a"), (w_fc2, "a")]
                + piece_args(pair),
                [((seq, hidden), BF, keep_in), ((seq, hidden), F32, keep_in), row(keep_in), row()],
                [w_mlp_all, mlp_sems], flops=16 * big * width,
            )
            entry.update(act_low=act_low, slopes=slopes, mlp_out=mlp_out)
            pieces[layer + 1] = (near[layer + 1], far_of(near[layer + 1], middle))
        else:
            x_out, d_middle, vecs["mlp", layer], *raw["mlp", layer] = run(
                functools.partial(mlp_both, layer, rows, offset, n_shard), "mlp_both",
                [(idx, "s"), (middle, "v"), (mod_all, "v"), (cotangent[0], "v"), (w_fc1, "a"),
                 (w_fc2, "a")] + piece_args(pair),
                [((seq, width), BF, "v"), row(), ((1, vec_wide["mlp"]), F32, "v")]
                + grads_out("mlp"),
                [w_mlp_all, w_mlp_all, pltpu.VMEM((seq, hidden), BF),
                 pltpu.VMEM((seq, hidden), F32), mlp_sems, out_sems], flops=48 * big * width,
            )
        saved.append(entry)

    def core_sum(keys, *earlier):
        keeps = [raw[key][0] for key in keys]
        received = [exchange(raw[key][1], by_core=1) for key in keys]
        if earlier:
            keeps[0] = after(keeps[0], *earlier)
        total_wide = sum(keep.shape[-1] for keep in keeps)
        slots = [(0, 2), (2, 2)] if relay else [(slot, 1) for slot in range(n_shard)]
        return run(
            functools.partial(core_sum_kernel, slots, len(keys)), "core_sum",
            [(array, "v") for array in keeps + received],
            [((number, rows, total_wide), BF, "v") for _, number in slots],
        )

    def shard_send(summed):
        if relay:
            return [exchange(summed[1], turn=first_turn)]
        return [exchange(summed[step], by_shard=step) for step in range(1, n_shard)]

    def add(terms, shape):
        return run(sum_kernel, "add", [(array, "v") for array in terms], [(shape, BF, "v")])[0]

    def shard_second(summed, arrived, *earlier):
        shape = summed[0].shape[1:]
        mine = after(summed[0], *earlier) if earlier else summed[0]
        if not relay:
            return [mine.reshape(shape)] + [array.reshape(shape) for array in arrived]
        keep, send = run(
            split_sum_kernel, "split_sum", [(mine, "v"), (arrived[0], "v")], [(shape, BF, "v")] * 2
        )
        return [keep, exchange(send, turn=second_turn)]

    def level_first(terms, halve, *earlier):
        shape = terms[0].shape
        if earlier:
            terms = [after(terms[0], *earlier)] + terms[1:]
        if not halve or shape[0] % 32:
            total = add(terms, shape)
            return False, total, exchange(total, by_level=1)
        part = (shape[0] // 2, shape[1])
        keep, send = run(
            row_split_kernel, "row_split",
            [(idx, "s")] + [(array, "v") for array in terms],
            [(part, BF, "v")] * 2, [pltpu.VMEM((2,) + part, BF)],
        )
        return True, keep, exchange(send, by_level=1)

    def level_second(first, *earlier):
        halved, kept, arriving = first
        if earlier:
            kept = after(kept, *earlier)
        return halved, add([kept, arriving], kept.shape)

    def level_last(halved, total, step):
        while step < levels:
            total = add([total, exchange(total, by_level=step)], total.shape)
            step *= 2
        near = [total, exchange(total, by_level=1)] if halved else [total]
        return near + far_of(near)

    waiting = []
    for layer in reversed(range(layers)):
        entry = saved[layer]
        pair, offset = pieces[layer], 2 * width
        if layer + 1 < layers:
            keys = [("qkv", layer + 1), ("mlp", layer + 1)]
            summed = core_sum(keys, grad_stream)
            waiting.append((keys, summed, shard_send(summed)))
            grad_stream = after(grad_stream, summed[0])
            d_middle, vecs["mlp", layer], *raw["mlp", layer] = run(
                functools.partial(mlp_backward, layer, rows, offset, n_shard), "mlp_backward",
                [(idx, "s"), (entry["middle"], "v"), (mod_all, "v"), (grad_stream, "v"),
                 (entry["act_low"], "v"), (entry["slopes"], "v"), (entry["mlp_out"], "v"),
                 (w_fc1, "a"), (w_fc2, "a")] + piece_args(pair),
                [row(), ((1, vec_wide["mlp"]), F32, "v")] + grads_out("mlp"),
                [w_mlp_all, w_mlp_all, mlp_sems, out_sems], flops=32 * big * width,
            )
            core_mlp = core_sum([("mlp", layer)], d_middle)
            sent_mlp = shard_send(core_mlp)
            d_middle = after(d_middle, core_mlp[0])
        pair, offset = pieces[layer], 0
        grad_stream, vecs["qkv", layer], *raw["qkv", layer] = run(
            functools.partial(attention_backward, layer, rows, offset, n_shard),
            "attention_backward",
            [(idx, "s"), (entry["stream"], "v"), (mod_all, "v"), (d_middle, "v"),
             (entry["qkv"], "v"), (entry["probs"], "v"), (entry["attended"], "v"),
             (entry["branch"], "v"), (w_qkv, "a"), (w_proj, "a")] + piece_args(pair),
            [row(), ((1, vec_wide["qkv"]), F32, "v")] + grads_out("qkv"),
            [w_qkv_all, pltpu.VMEM((seq, 3 * width), BF), w_qkv_all, qkv_sems, out_sems],
            flops=28 * big * width,
        )
    cond_in = condition.astype(F32)
    vector = [jax.nn.silu(cond_in).astype(BF)]
    for layer in range(layers):
        vector += [vecs[kind, layer][:, : 3 * width].astype(BF) for kind in ("qkv", "mlp")]
    for layer in range(layers):
        vector += [vecs[kind, layer][:, 3 * width :].astype(BF) for kind in ("qkv", "mlp")]
    vector = jnp.concatenate(vector, axis=1)
    length = vector.shape[1]
    masks = [first_turn, second_turn] if relay else []
    while not relay and 2 ** len(masks) < n_shard:
        masks.append((2 ** len(masks),) * 2)

    cols = width + layers * wide
    extra = -(-(length - cols) // cols)

    def stack(first, second, extra=0):
        shape = (2 * first.shape[0] - extra, first.shape[1])
        return run(
            functools.partial(stack_kernel, extra), "stack", [(first, "v"), (second, "v")],
            [(shape, BF, "v")], [pltpu.VMEM(shape, F32)],
        )[0]

    (keys_first, core_first, sent_first), = waiting
    plan = [keys_first, [("mlp", 0)], [("qkv", 0)]]
    a = shard_second(core_first, sent_first, grad_stream)
    core_qkv = core_sum(plan[2], a[0])
    sent_qkv = shard_send(core_qkv)
    b = shard_second(core_mlp, sent_mlp, core_qkv[0])
    a = level_first(a, True, b[0])
    c = shard_second(core_qkv, sent_qkv, a[1])
    vector = after(vector, b[0])
    for mask in masks[:-2]:
        vector = stack(vector, exchange(vector, turn=mask))
    arriving = exchange(vector, turn=masks[-2])
    vector = stack(after(vector, c[0]), arriving)
    arriving = exchange(vector, turn=masks[-1])
    b = level_first(b, True, vector)
    a = level_second(a, b[1])
    a_moving = exchange(a[1], by_level=2)
    c = level_first(c, False, a[1])
    grad_cond, passed, stacked = run(
        group_kernel, "group",
        [(idx, "s"), (w_ada, "a"), (after(vector, c[1]), "v"), (arriving, "v")],
        [((n_shard // 2, width), F32, "v")] * 2 + [((n_shard + extra, cols), BF, "v")],
        [pltpu.VMEM((n_shard, length), F32), pltpu.VMEM((n_shard + extra, cols), F32)]
        + pad_scratch, flops=10**7,
    )
    arriving = exchange(stacked, by_level=1)
    b = level_second(b, stacked)
    b_moving = exchange(b[1], by_level=2)
    c = level_second(c, b[1])
    c_moving = exchange(c[1], by_level=2)
    stacked = stack(after(stacked, c[1]), arriving, extra)
    step = 2
    while 2 * step < levels:
        stacked = stack(stacked, exchange(stacked, by_level=step), extra)
        step *= 2
    arriving = exchange(stacked, by_level=step)
    a = (a[0], add([after(a[1], stacked), a_moving], a[1].shape))
    a_parts = level_last(*a, 4)
    b = (b[0], add([after(b[1], a[1]), b_moving], b[1].shape))
    b_parts = level_last(*b, 4)
    grad_cond = grad_cond + exchange(passed, turn=masks[-1])
    for mask in masks[-2::-1]:
        half = grad_cond.shape[0] // 2
        grad_cond = grad_cond[:half] + exchange(grad_cond[half:], turn=mask)
    cond_grad = jax.vjp(jax.nn.silu, cond_in)[1](grad_cond)[0]
    stacks = [after(stacked, b[1]), arriving]
    stacks = stacks + far_of(stacks)
    grad_ada, sums = run(
        functools.partial(ada_grad_kernel, rows, wide, extra, factor), "ada_grad",
        [(idx, "s")] + [(array, "v") for array in stacks],
        [((layers, rows, wide), F32, "v"), ((1, length - width), F32, "v")],
        [pltpu.VMEM((width, total_latents), F32), pltpu.VMEM((total_latents, cols), F32)],
        flops=10**8,
    )

    c = (c[0], add([after(c[1], sums), c_moving], c[1].shape))
    finals = [a_parts, b_parts, level_last(*c, 4)]

    def own_part(parts):
        whole = jnp.concatenate(parts, axis=0)
        length = whole.shape[1] // n_shard
        return lax.dynamic_slice_in_dim(whole, shard_id * length, length, axis=1)

    base = layers * wide
    at = [base + layer * (4 * width + hidden) for layer in range(layers)]
    grad_ada_bias = own_part([sums[:, layer * wide : (layer + 1) * wide] for layer in range(layers)])
    grad_qv_bias = own_part([sums[:, a : a + 2 * width] for a in at])
    grad_proj_bias = own_part([sums[:, a + 2 * width : a + 3 * width] for a in at])
    grad_fc1_bias = own_part([sums[:, a + 3 * width : a + 3 * width + hidden] for a in at])
    grad_fc2_bias = own_part([sums[:, a + 3 * width + hidden : a + 4 * width + hidden] for a in at])

    finish_plan, finish_inputs, finish_scratch = [], [(idx, "s")], []
    for keys, parts in zip(plan, finals):
        members, skip = [], 0
        for kind, layer in keys:
            members.append((kind, layer, skip))
            skip += half_wide[kind]
        finish_plan.append((members, len(parts) // 2))
        finish_inputs += [(array, "v") for array in parts]
        finish_scratch.append(pltpu.VMEM((2, rows, skip), BF))
    grad_qkv, grad_proj, grad_fc1, grad_fc2 = run(
        functools.partial(finish_kernel, rows, finish_plan, factor), "finish",
        finish_inputs,
        [(array.shape, F32, "v") for array in (w_qkv, w_proj, w_fc1, w_fc2)],
        finish_scratch,
    )
    return (
        x_out[None], grad_stream[None], cond_grad, grad_qkv, grad_qv_bias, grad_proj,
        grad_proj_bias, grad_fc1, grad_fc1_bias, grad_fc2, grad_fc2_bias, grad_ada, grad_ada_bias,
    )


def solution(mesh):
    rows3, rows2 = P(("shard", "rep"), None, None), P(("shard", "rep"), None)
    weight, bias = P(None, "shard", None), P(None, "shard")
    return jax.shard_map(
        shards,
        mesh=mesh,
        in_specs=(rows3, rows2, rows3) + (weight, bias) * 5,
        out_specs=(rows3, rows3, rows2) + (weight, bias) * 5,
        check_vma=False,
    )
```
